256 devices in a mesh: strip: 32 (over y, z_hi, core), seg: 8 (over x, z_lo).
Axes of the slice: x: 4, y: 4, z: 8 (z_hi: 4, z_lo: 2; z = z_hi * 2 + z_lo), core: 2. Of those that a mesh axis runs over, the one named last changes fastest.
Arguments:
- gradient: float32 [9, 32, 4096], P(None, 'strip', 'seg'), may hold values from -72 to 72
- live_blocks: int32 [32, 8], P('strip', 'seg'), may hold values from 8 to 16, as said below
- loc_cam_jac: bfloat16 [18, 6, 32, 16384], P(None, None, 'strip', 'seg'), may hold values from -0.59765625 to 0.59765625
- loc_point_jac: bfloat16 [6, 6, 32, 16384], P(None, None, 'strip', 'seg'), may hold values from -6 to 6
- loc_cams: int32 [6, 32, 16384], P(None, 'strip', 'seg'), may hold values from 0 to 511
- fwd_cam_jac: bfloat16 [2, 18, 2, 32, 32768], P(None, None, None, 'strip', 'seg'), may hold values from -0.59765625 to 0.59765625
- fwd_point_jac: bfloat16 [2, 6, 2, 32, 32768], P(None, None, None, 'strip', 'seg'), may hold values from -6 to 6
- fwd_cams: int32 [2, 2, 32, 32768], P(None, None, 'strip', 'seg'), may hold values from 0 to 511
- side_cam_jac: bfloat16 [2, 18, 2, 32, 24576], P(None, None, None, 'strip', 'seg'), may hold values from -0.59765625 to 0.59765625
- side_point_jac: bfloat16 [2, 6, 2, 32, 24576], P(None, None, None, 'strip', 'seg'), may hold values from -6 to 6
- side_cams: int32 [2, 2, 32, 24576], P(None, None, 'strip', 'seg'), may hold values from 0 to 511
Outputs:
- solution_step: float32 [9, 32, 4096], P(None, 'strip', 'seg')
- residual: float32 [9, 32, 4096], P(None, 'strip', 'seg')
The draws below stay inside these ranges and needn't reach their ends.
Inputs may be any that keep to these rules, and one draw needn't show every extreme that they name: `live_blocks`: the largest count, 16, is reached by some segment in every draw.
All inputs are finite; a program needn't handle non-finite values.
Results may differ from the reference program's by a relative error of at most 0.0054.
Values may be sent and summed in bfloat16 or wider, within the bound.
No kernel may reach another device: no remote copies, remote signals or barrier semaphores. Data moves between devices by JAX's collectives and lax.ppermute only.
A program may use at most 128 MiB of HBM per device.

```python
import jax
import jax.numpy as jnp
from jax import lax

CAMS = 512
BLOCK = 128
LOC_BLOCKS = 16
OBS_LOC = 6
ITERS = 2
SEGMENTS = 8
STRIPS = 32
IMAGES = 4096
LOC_DEV = 2048
LOC_ALL = 16384
FWD_ALL = 32768
SIDE_ALL = 24576


def draw_gradient(key, part):
    first = jax.random.fold_in(jax.random.fold_in(key, 11), 0)
    shape = (9, STRIPS, IMAGES)
    ramp = 1.0 + lax.broadcasted_iota(jnp.float32, shape, 1) / max(STRIPS - 1, 1)
    ramp = ramp * (1.0 + lax.broadcasted_iota(jnp.float32, shape, 2) / max(IMAGES - 1, 1))
    base = jax.random.normal(first, shape, jnp.float32)
    return (3.0 * jnp.clip(base, -6.0, 6.0) * ramp).astype(jnp.float32)


def draw_live_blocks(key, part):
    first, second = jax.random.split(jax.random.fold_in(key, 23))
    counts = jax.random.randint(first, (STRIPS * SEGMENTS,), (LOC_BLOCKS + 1) // 2, LOC_BLOCKS + 1)
    chosen = jax.random.randint(second, (), 0, STRIPS * SEGMENTS)
    counts = jnp.where(jnp.arange(STRIPS * SEGMENTS) == chosen, LOC_BLOCKS, counts)
    return counts.reshape(STRIPS, SEGMENTS).astype(jnp.int32)


def plant(entries, own_key, least, largest):
    extent = entries.shape
    place = [jax.random.randint(jax.random.fold_in(own_key, axis), (), 0, extent[axis]) for axis in range(len(extent))]
    entries = entries.at[tuple(place)].set(least)
    longest = extent.index(max(extent))
    place[longest] = (place[longest] + 1) % extent[longest]
    return entries.at[tuple(place)].set(largest)


def levels(rng, dims, shards, smallest, high):
    gain = 1.0
    for axis_at, shards_of in shards:
        heights = jax.random.uniform(jax.random.fold_in(jax.random.fold_in(rng, 6), axis_at), (shards_of,), jnp.float32, smallest / len(shards), high / len(shards))
        gain = gain * jnp.repeat(jnp.exp(heights), dims[axis_at] // shards_of).reshape((-1,) + (1,) * (len(dims) - 1 - axis_at))
    return gain


def bell_draw(own_key, extent, scale, reach, cuts=(), kind=jnp.bfloat16):
    factor_of = levels(own_key, extent, cuts, -0.22, 0.18) if cuts else 1.0
    entries = jax.random.normal(own_key, extent, jnp.float32) * scale * factor_of
    return jnp.minimum(jnp.maximum(entries, -reach), reach).astype(kind)


def setup_inputs(seed: int = 0) -> dict:
    arg_keys = jax.random.split(jax.random.key(seed), 12)
    return {
        "gradient": draw_gradient(jax.random.fold_in(arg_keys[11], 71), 0),
        "live_blocks": draw_live_blocks(jax.random.fold_in(arg_keys[11], 71), 0),
        "loc_cam_jac": bell_draw(arg_keys[2], (18, OBS_LOC, STRIPS, LOC_ALL), 0.1, 0.59765625, ((2, 32), (3, 8))),
        "loc_point_jac": bell_draw(arg_keys[3], (6, OBS_LOC, STRIPS, LOC_ALL), 1.0, 6.0, ((2, 32), (3, 8))),
        "loc_cams": plant(jax.random.randint(arg_keys[4], (OBS_LOC, STRIPS, LOC_ALL), 0, CAMS), jax.random.fold_in(arg_keys[4], 1), 0, CAMS - 1).astype(jnp.int32),
        "fwd_cam_jac": bell_draw(arg_keys[5], (2, 18, 2, STRIPS, FWD_ALL), 0.1, 0.59765625, ((3, 32), (4, 8))),
        "fwd_point_jac": bell_draw(arg_keys[6], (2, 6, 2, STRIPS, FWD_ALL), 1.0, 6.0, ((3, 32), (4, 8))),
        "fwd_cams": plant(jax.random.randint(arg_keys[7], (2, 2, STRIPS, FWD_ALL), 0, CAMS), jax.random.fold_in(arg_keys[7], 1), 0, CAMS - 1).astype(jnp.int32),
        "side_cam_jac": bell_draw(arg_keys[8], (2, 18, 2, STRIPS, SIDE_ALL), 0.1, 0.59765625, ((3, 32), (4, 8))),
        "side_point_jac": bell_draw(arg_keys[9], (2, 6, 2, STRIPS, SIDE_ALL), 1.0, 6.0, ((3, 32), (4, 8))),
        "side_cams": plant(jax.random.randint(arg_keys[10], (2, 2, STRIPS, SIDE_ALL), 0, CAMS), jax.random.fold_in(arg_keys[10], 1), 0, CAMS - 1).astype(jnp.int32),
    }


camera_damping = 1.0
point_damping = 1.0


def observe(cam_jac, point_jac, cam_index, vector):
    across = cam_jac.astype(jnp.float32).reshape((2, 9) + cam_index.shape)
    along = point_jac.astype(jnp.float32).reshape((2, 3) + cam_index.shape)
    cameras = vector[:, cam_index]
    predicted = jnp.sum(across * cameras[None], axis=1)
    gathered = jnp.sum(along * predicted[:, None], axis=(0, 2))
    return predicted, gathered


def hessian(point_jac):
    along = point_jac.astype(jnp.float32).reshape((2, 3) + point_jac.shape[1:])
    entry_pairs = [(0, 0), (0, 1), (0, 2), (1, 1), (1, 2), (2, 2)]
    return jnp.stack([jnp.sum(along[:, i] * along[:, j], axis=(0, 1)) for i, j in entry_pairs])


def invert_blocks(blocks):
    a = blocks[0] + point_damping
    b = blocks[1]
    c = blocks[2]
    d = blocks[3] + point_damping
    e = blocks[4]
    f = blocks[5] + point_damping
    first = d * f - e * e
    second = c * e - b * f
    third = b * e - c * d
    determinant = a * first + b * second + c * third
    return jnp.stack([first, second, third, a * f - c * c, b * c - a * e, a * d - b * b]) / determinant


def solve_blocks(inverse, summed):
    return jnp.stack([
        inverse[0] * summed[0] + inverse[1] * summed[1] + inverse[2] * summed[2],
        inverse[1] * summed[0] + inverse[3] * summed[1] + inverse[4] * summed[2],
        inverse[2] * summed[0] + inverse[4] * summed[1] + inverse[5] * summed[2]])


def return_terms(cam_jac, point_jac, cam_index, predicted, solved, weight):
    across = cam_jac.astype(jnp.float32).reshape((2, 9) + cam_index.shape)
    along = point_jac.astype(jnp.float32).reshape((2, 3) + cam_index.shape)
    fitted = jnp.sum(along * solved[None, :, None], axis=1)
    residue = (predicted - fitted) * weight
    terms = jnp.sum(across * residue[:, None], axis=0)
    return jnp.zeros((9, CAMS), jnp.float32).at[:, cam_index].add(terms)


def per_device(function):
    def mapped(*arrays):
        return lax.map(lambda group: jax.vmap(function)(*group), arrays)
    return mapped


def to_blocks(array):
    leading = array.ndim - 2
    shaped = array.reshape(array.shape[:-1] + (SEGMENTS, array.shape[-1] // SEGMENTS))
    return jnp.moveaxis(shaped, (leading, leading + 1), (0, 1))


def from_blocks(array):
    moved = jnp.moveaxis(array, (0, 1), (1, 2))
    return moved.reshape((moved.shape[0], moved.shape[1], moved.shape[2] * moved.shape[3]))


def from_next(array):
    return jnp.concatenate([array[:, 1:], jnp.zeros_like(array[:, :1])], axis=1)


def to_next(array):
    return jnp.concatenate([jnp.zeros_like(array[:, :1]), array[:, :-1]], axis=1)


def from_partner(array):
    mirrored = array[:, ::-1]
    return jnp.concatenate([mirrored[1:], jnp.zeros_like(mirrored[:1])], axis=0)


def to_partner(array):
    mirrored = array[:, ::-1]
    return jnp.concatenate([jnp.zeros_like(mirrored[:1]), mirrored[:-1]], axis=0)


def reference(gradient, live_blocks, loc_cam_jac, loc_point_jac, loc_cams, fwd_cam_jac, fwd_point_jac, fwd_cams, side_cam_jac, side_point_jac, side_cams):
    observe_all = per_device(observe)
    terms_all = per_device(return_terms)
    hessian_all = per_device(hessian)
    invert_all = per_device(invert_blocks)
    solve_all = per_device(solve_blocks)

    loc_cj = to_blocks(loc_cam_jac)
    loc_pj = to_blocks(loc_point_jac)
    loc_ix = to_blocks(loc_cams)
    fwd_cj = to_blocks(fwd_cam_jac)
    fwd_pj = to_blocks(fwd_point_jac)
    fwd_ix = to_blocks(fwd_cams)
    side_cj = to_blocks(side_cam_jac)
    side_pj = to_blocks(side_point_jac)
    side_ix = to_blocks(side_cams)

    positions = jnp.arange(LOC_DEV, dtype=jnp.int32) // BLOCK
    live_weight = (positions[None, None, :] < live_blocks[:, :, None]).astype(jnp.float32)
    seg_ok = jnp.broadcast_to((jnp.arange(SEGMENTS, dtype=jnp.int32) > 0)[None, :], (STRIPS, SEGMENTS)).astype(jnp.float32)
    strip_ok = jnp.broadcast_to((jnp.arange(STRIPS, dtype=jnp.int32) > 0)[:, None], (STRIPS, SEGMENTS)).astype(jnp.float32)
    unit_weight = jnp.ones((STRIPS, SEGMENTS), jnp.float32)

    inverse_loc = invert_all(hessian_all(loc_pj))
    inverse_fwd = invert_all(hessian_all(fwd_pj[:, :, 0]) + from_next(hessian_all(fwd_pj[:, :, 1])))
    inverse_side = invert_all(hessian_all(side_pj[:, :, 0]) + from_partner(hessian_all(side_pj[:, :, 1])))

    def schur(vector):
        result = camera_damping * vector
        predicted, gathered = observe_all(loc_cj, loc_pj, loc_ix, vector)
        solved = solve_all(inverse_loc, gathered)
        result = result + terms_all(loc_cj, loc_pj, loc_ix, predicted, solved, live_weight)
        own_pred, own_sum = observe_all(fwd_cj[:, :, 0], fwd_pj[:, :, 0], fwd_ix[:, :, 0], vector)
        guest_pred, guest_sum = observe_all(fwd_cj[:, :, 1], fwd_pj[:, :, 1], fwd_ix[:, :, 1], vector)
        solved = solve_all(inverse_fwd, own_sum + from_next(guest_sum))
        result = result + terms_all(fwd_cj[:, :, 0], fwd_pj[:, :, 0], fwd_ix[:, :, 0], own_pred, solved, unit_weight)
        result = result + terms_all(fwd_cj[:, :, 1], fwd_pj[:, :, 1], fwd_ix[:, :, 1], guest_pred, to_next(solved), seg_ok)
        own_pred, own_sum = observe_all(side_cj[:, :, 0], side_pj[:, :, 0], side_ix[:, :, 0], vector)
        guest_pred, guest_sum = observe_all(side_cj[:, :, 1], side_pj[:, :, 1], side_ix[:, :, 1], vector)
        solved = solve_all(inverse_side, own_sum + from_partner(guest_sum))
        result = result + terms_all(side_cj[:, :, 0], side_pj[:, :, 0], side_ix[:, :, 0], own_pred, solved, unit_weight)
        result = result + terms_all(side_cj[:, :, 1], side_pj[:, :, 1], side_ix[:, :, 1], guest_pred, to_partner(solved), strip_ok)
        return result

    residual = -to_blocks(gradient)
    solution_step = jnp.zeros_like(residual)
    direction = residual
    norm_now = jnp.sum(residual * residual)
    for iteration in range(ITERS):
        image = schur(direction)
        alpha = norm_now / jnp.sum(direction * image)
        solution_step = solution_step + alpha * direction
        residual = residual - alpha * image
        norm_next = jnp.sum(residual * residual)
        direction = residual + (norm_next / norm_now) * direction
        norm_now = norm_next
    return from_blocks(solution_step), from_blocks(residual)
```

```python
import jax
import jax.numpy as jnp
from jax import lax
from jax.experimental import pallas as pl
from jax.experimental.pallas import tpu as pltpu
from jax.sharding import PartitionSpec as P

AXES = ("strip", "seg")
LANES = 128
JAC = 9
PAGES = 4
ROWS = JAC * PAGES
LIFT = 40
STACK = 2 * LIFT
STEP = 16
SYM = ((0, 0), (0, 1), (0, 2), (1, 1), (1, 2), (2, 2))
DAMP = 1.0
VMEM = pl.BlockSpec(memory_space=pltpu.VMEM)
SMEM = pl.BlockSpec(memory_space=pltpu.SMEM)
F32 = jnp.float32


def fetch(table, index):
    lane = index & (LANES - 1)
    odd = (index & LANES) != 0
    upper = index >= 2 * LANES
    found = []
    for j in range(JAC):
        page = [
            jnp.take_along_axis(
                jnp.broadcast_to(table[pl.ds(PAGES * j + k, 1), :], index.shape), lane, axis=1
            )
            for k in range(PAGES)
        ]
        low = jnp.where(odd, page[1], page[0])
        high = jnp.where(odd, page[3], page[2])
        found.append(jnp.where(upper, high, low))
    return found


def predict(across, values):
    return [sum(across[JAC * r + j] * values[j] for j in range(JAC)) for r in range(2)]


def project(along, seen):
    return [along[k] * seen[0] + along[3 + k] * seen[1] for k in range(3)]


def normal(along):
    return [along[i] * along[j] + along[3 + i] * along[3 + j] for i, j in SYM]


def invert(h):
    a, b, c, d, e, f = h[0] + DAMP, h[1], h[2], h[3] + DAMP, h[4], h[5] + DAMP
    first = d * f - e * e
    second = c * e - b * f
    third = b * e - c * d
    scale = 1.0 / (a * first + b * second + c * third)
    return [
        m * scale for m in (first, second, third, a * f - c * c, b * c - a * e, a * d - b * b)
    ]


def solve(m, b):
    return [
        m[0] * b[0] + m[1] * b[1] + m[2] * b[2],
        m[1] * b[0] + m[3] * b[1] + m[4] * b[2],
        m[2] * b[0] + m[4] * b[1] + m[5] * b[2],
    ]


def residue(along, seen, z):
    return [seen[r] - sum(along[3 * r + k] * z[k] for k in range(3)) for r in range(2)]


def spread(terms, index, stage, total):
    count = index.shape[0]
    page = index >> 7
    hit = [page == h for h in range(PAGES)]
    for j in range(JAC):
        coarse = terms[j].astype(jnp.bfloat16).astype(F32)
        fine = terms[j] - coarse
        for h in range(PAGES):
            row = PAGES * j + h
            stage[pl.ds(row, count, stride=STACK), :] = jnp.where(hit[h], coarse, 0.0)
            stage[pl.ds(LIFT + row, count, stride=STACK), :] = jnp.where(hit[h], fine, 0.0)
    lane = (index & (LANES - 1)).astype(F32)
    place = lax.broadcasted_iota(jnp.int32, (LANES, LANES), 0).astype(F32).astype(jnp.bfloat16)
    one, none = jnp.ones((), jnp.bfloat16), jnp.zeros((), jnp.bfloat16)
    group = 4 if count % 4 == 0 else 3
    for start in range(0, count, group):
        left, right = [], []
        for row in range(start, start + group):
            left.append(stage[pl.ds(row * STACK, STACK), :].astype(jnp.bfloat16))
            wide = jnp.broadcast_to(lane[row : row + 1], (16, LANES)).astype(jnp.bfloat16)
            wide = jnp.concatenate([wide] * (LANES // 16), axis=0)
            right.append(jnp.where(wide == place, one, none))
        total[...] += lax.dot_general(
            jnp.concatenate(left, axis=1),
            jnp.concatenate(right, axis=1),
            (((1,), (1,)), ((), ())),
            preferred_element_type=F32,
        )


def folded(total):
    return total[0:ROWS, :] + total[LIFT : LIFT + ROWS, :]


def weave(cams, index):
    half = cams.shape[2]
    for s in range(2):
        for o in range(2):
            index[s, pl.ds(o, half, stride=2), :] = cams[s, o]


def pair_look(cam, point, index, table, seen_out, loose, sums, with_h, squares, weights):
    rows = cam.shape[2]
    half = rows // 2
    for s in range(2):

        def body(i, carry, s=s):
            at = pl.ds(pl.multiple_of(i * STEP, STEP), STEP)
            across = [cam[s, j, at, :].astype(F32) for j in range(2 * JAC)]
            along = [point[s, j, at, :].astype(F32) for j in range(6)]
            seen = predict(across, fetch(table, index[s, at, :]))
            for r in range(2):
                seen_out[s, r, at, :] = seen[r]
            parts = project(along, seen)
            if with_h:
                parts = parts + normal(along)
            for n, part in enumerate(parts):
                loose[n, at, :] = part
            if squares is not None:
                squares[...] += weights[s] * (seen[0] * seen[0] + seen[1] * seen[1])
            return carry

        lax.fori_loop(0, rows // STEP, body, 0)
        for n in range(9 if with_h else 3):
            sums[s, n] = (
                loose[n, pl.ds(0, half, stride=2), :] + loose[n, pl.ds(1, half, stride=2), :]
            )


def pair_return(cam, point, index, seen_in, z, weights, stage, total):
    rows = cam.shape[2]
    for s in range(2):

        def body(i, carry, s=s):
            at = pl.ds(pl.multiple_of(i * STEP, STEP), STEP)
            across = [cam[s, j, at, :].astype(F32) for j in range(2 * JAC)]
            along = [point[s, j, at, :].astype(F32) for j in range(6)]
            left = residue(
                along, [seen_in[s, r, at, :] for r in range(2)], [z[s, k, at, :] for k in range(3)]
            )
            left = [weights[s] * e for e in left]
            terms = [across[j] * left[0] + across[JAC + j] * left[1] for j in range(JAC)]
            spread(terms, index[s, at, :], stage, total)
            return carry

        lax.fori_loop(0, rows // STEP, body, 0)


def pair_solve(mine, other, inverse_out, inverse_in, z, products, weights):
    half = mine.shape[2]
    for s in range(2):
        for i in range(half // 8):
            at = pl.ds(8 * i, 8)
            b = [mine[s, k, at, :] + other[s][k, at, :] for k in range(3)]
            if inverse_in is None:
                inverse = invert(
                    [mine[s, 3 + k, at, :] + other[s][3 + k, at, :] for k in range(6)]
                )
                for k in range(6):
                    inverse_out[s, k, at, :] = inverse[k]
            else:
                inverse = [inverse_in[s, k, at, :] for k in range(6)]
            solved = solve(inverse, b)
            if products is not None:
                products[...] += weights[s] * sum(
                    mine[s, k, at, :] * solved[k] for k in range(3)
                )
            for k in range(3):
                for o in range(2):
                    z[s, k, pl.ds(16 * i + o, 8, stride=2), :] = solved[k]


def look_kernel(
    table, fcam, fpoint, fcams, scam, spoint, scams,
    fseen, fsums, sseen, ssums,
    findex, sindex, floose, sloose,
):
    weave(fcams, findex)
    weave(scams, sindex)
    pair_look(fcam, fpoint, findex, table, fseen, floose, fsums, True, None, None)
    pair_look(scam, spoint, sindex, table, sseen, sloose, ssums, True, None, None)


def local_kernel(live, table, cam, point, cams, out, product, stage, total):
    total[...] = jnp.zeros_like(total)
    stage[...] = jnp.zeros_like(stage)
    product[...] = jnp.zeros_like(product)
    watched = cams.shape[0] // 16

    def body(i, carry):
        at = pl.ds(pl.multiple_of(i * LANES, LANES), LANES)
        index = cams[pl.ds(i, watched, stride=16), :]
        across = [cam[j, :, at].astype(F32) for j in range(2 * JAC)]
        along = [point[j, :, at].astype(F32) for j in range(6)]
        seen = predict(across, fetch(table, index))
        summed = [jnp.sum(x, axis=0, keepdims=True) for x in project(along, seen) + normal(along)]
        z = solve(invert(summed[3:]), summed[:3])
        left = residue(along, seen, z)
        terms = [across[j] * left[0] + across[JAC + j] * left[1] for j in range(JAC)]
        product[0:1, :] += jnp.sum(seen[0] * left[0] + seen[1] * left[1], axis=0, keepdims=True)
        spread(terms, index, stage, total)
        return carry

    lax.fori_loop(0, live[0], body, 0)
    out[...] = folded(total)


def middle_kernel(
    weights, table, extra, fcam, fpoint, fcams, scam, spoint, scams,
    fseen, fsums, fown, fguest, sseen, ssums, sown, sguest,
    result, finverse, sinverse, fseen2, fsums2, sseen2, ssums2, dots,
    findex, sindex, floose, sloose, fz, sz, stage, total, squares,
):
    weave(fcams, findex)
    weave(scams, sindex)
    total[...] = jnp.zeros_like(total)
    stage[...] = jnp.zeros_like(stage)
    fweights = (1.0, weights[0])
    sweights = (1.0, weights[1])
    pair_solve(fsums, (fown, fguest), finverse, None, fz, None, None)
    pair_return(fcam, fpoint, findex, fseen, fz, fweights, stage, total)
    pair_solve(ssums, (sown, sguest), sinverse, None, sz, None, None)
    pair_return(scam, spoint, sindex, sseen, sz, sweights, stage, total)
    step = folded(total) + extra[...]
    result[...] = step
    squares[...] = jnp.zeros_like(squares)
    pair_look(fcam, fpoint, findex, result, fseen2, floose, fsums2, False, squares, fweights)
    pair_look(scam, spoint, sindex, result, sseen2, sloose, ssums2, False, squares, sweights)
    base = table[...]
    dots[...] = jnp.zeros_like(dots)
    for row, value in enumerate((base * base, base * step, step * step, squares[...])):
        dots[row : row + 1, :] = jnp.sum(value, axis=0, keepdims=True)


def dots_kernel(
    weights, dots, product, fsums, fown, fguest, finverse, ssums, sown, sguest, sinverse,
    fz, sz, out, products,
):
    products[...] = jnp.zeros_like(products)
    pair_solve(fsums, (fown, fguest), None, finverse, fz, products, (1.0, weights[0]))
    pair_solve(ssums, (sown, sguest), None, sinverse, sz, products, (1.0, weights[1]))
    curve = dots[3:4, :] + product[0:1, :] - jnp.sum(products[...], axis=0, keepdims=True)
    rows = jnp.concatenate([dots[0:3, :], curve], axis=0)
    sums = jnp.sum(rows, axis=1, keepdims=True)
    place = lax.broadcasted_iota(jnp.int32, (1, LANES), 1)
    line = jnp.zeros((1, LANES), F32)
    for n in range(4):
        line = line + jnp.where(place == n, sums[n : n + 1, :], 0.0)
    out[...] = jnp.broadcast_to(line, out.shape)


def last_kernel(
    weights, extra, fcam, fpoint, fcams, scam, spoint, scams, fseen, fz, sseen, sz,
    result, findex, sindex, stage, total,
):
    weave(fcams, findex)
    weave(scams, sindex)
    total[...] = jnp.zeros_like(total)
    stage[...] = jnp.zeros_like(stage)
    pair_return(fcam, fpoint, findex, fseen, fz, (1.0, weights[0]), stage, total)
    pair_return(scam, spoint, sindex, sseen, sz, (1.0, weights[1]), stage, total)
    result[...] = folded(total) + extra[...]


def close_kernel(sums, base, first, second, step_out, residual_out):
    line = jnp.sum(sums[...], axis=0, keepdims=True)
    place = lax.broadcasted_iota(jnp.int32, line.shape, 1)
    rr, bp, pp, curve = [
        jnp.sum(jnp.where(place == n, line, 0.0), axis=1, keepdims=True) for n in range(4)
    ]
    whole = rr + bp
    alpha = rr / whole
    rest = bp / whole
    new = alpha * (alpha * pp - rest * bp)
    gamma = rest + new / rr
    bend = gamma * gamma * rr - 2.0 * gamma * alpha * bp + alpha * alpha * pp
    bend = bend + gamma * gamma * bp - 2.0 * gamma * alpha * pp + alpha * alpha * curve
    again = new / bend
    d0, p, t = base[...], first[...], second[...]
    direction = gamma * d0 - alpha * p
    image = gamma * d0 + (gamma - alpha) * p - alpha * t
    step_out[...] = -(alpha * d0 + again * direction)
    residual_out[...] = -(rest * d0 - alpha * p - again * image)


def call(kernel, ins, outs, scratch, flops, name):
    outs = [jax.ShapeDtypeStruct(shape, F32) for shape in outs]
    specs = [SMEM if i == 0 and x.ndim == 1 else VMEM for i, x in enumerate(ins)]
    return pl.pallas_call(
        kernel,
        out_shape=outs,
        in_specs=specs,
        out_specs=[VMEM] * len(outs),
        scratch_shapes=scratch,
        compiler_params=pltpu.CompilerParams(vmem_limit_bytes=40 << 20),
        cost_estimate=pl.CostEstimate(flops=flops, bytes_accessed=2 << 20, transcendentals=0),
        name=name,
    )(*ins)


def rows_of(array):
    kinds, parts, two, _, points = array.shape
    array = array.reshape(kinds, parts, two, points // LANES, LANES)
    return array.transpose(0, 1, 3, 2, 4).reshape(kinds, parts, two * points // LANES, LANES)


def per_device(
    gradient, live_blocks, loc_cam_jac, loc_point_jac, loc_cams,
    fwd_cam_jac, fwd_point_jac, fwd_cams, side_cam_jac, side_point_jac, side_cams,
):
    strips, segs = lax.axis_size("strip"), lax.axis_size("seg")
    cells = [(s, g) for s in range(strips) for g in range(segs)]

    def pairs(move):
        found = []
        for s, g in cells:
            t, h = move(s, g)
            if 0 <= t < strips and 0 <= h < segs:
                found.append((s * segs + g, t * segs + h))
        return found

    fwd_down = pairs(lambda s, g: (s, g - 1))
    fwd_up = pairs(lambda s, g: (s, g + 1))
    side_down = pairs(lambda s, g: (s - 1, segs - 1 - g))
    side_up = pairs(lambda s, g: (s + 1, segs - 1 - g))

    weights = jnp.stack(
        [(lax.axis_index("seg") > 0).astype(F32), (lax.axis_index("strip") > 0).astype(F32)]
    )
    base = gradient.reshape(ROWS, LANES)
    live = live_blocks.reshape(1)
    lcam, lpoint = loc_cam_jac[:, :, 0], loc_point_jac[:, :, 0]
    lcams = loc_cams.reshape(-1, LANES)
    fcam, fpoint = rows_of(fwd_cam_jac), rows_of(fwd_point_jac)
    scam, spoint = rows_of(side_cam_jac), rows_of(side_point_jac)
    fcams = fwd_cams.reshape(2, 2, -1, LANES)
    scams = side_cams.reshape(2, 2, -1, LANES)
    fr, sr = fcam.shape[2], scam.shape[2]
    watched = lcam.shape[1]

    def both(values, up, down):
        return lax.ppermute(values[1], AXES, down), lax.ppermute(values[0], AXES, up)

    index_scratch = [pltpu.VMEM((2, fr, LANES), jnp.int32), pltpu.VMEM((2, sr, LANES), jnp.int32)]
    z_scratch = [pltpu.VMEM((2, 3, fr, LANES), F32), pltpu.VMEM((2, 3, sr, LANES), F32)]
    total_scratch = [pltpu.VMEM((STEP * STACK, LANES), F32), pltpu.VMEM((STACK, LANES), F32)]

    fseen, fsums, sseen, ssums = call(
        look_kernel,
        [base, fcam, fpoint, fcams, scam, spoint, scams],
        [(2, 2, fr, LANES), (2, 9, fr // 2, LANES), (2, 2, sr, LANES), (2, 9, sr // 2, LANES)],
        index_scratch + [pltpu.VMEM((9, fr, LANES), F32), pltpu.VMEM((9, sr, LANES), F32)],
        10**9,
        "look",
    )
    fown, fguest = both(fsums, fwd_up, fwd_down)
    sown, sguest = both(ssums, side_up, side_down)

    def local(table):
        return call(
            local_kernel,
            [live, table, lcam, lpoint, lcams],
            [(ROWS, LANES), (8, LANES)],
            [pltpu.VMEM((watched * STACK, LANES), F32), pltpu.VMEM((STACK, LANES), F32)],
            5 * 10**9,
            "local",
        )

    extra, _ = local(base)
    p, finverse, sinverse, fseen, fsums, sseen, ssums, dots = call(
        middle_kernel,
        [weights, base, extra, fcam, fpoint, fcams, scam, spoint, scams,
         fseen, fsums, fown, fguest, sseen, ssums, sown, sguest],
        [(ROWS, LANES), (2, 6, fr // 2, LANES), (2, 6, sr // 2, LANES),
         (2, 2, fr, LANES), (2, 3, fr // 2, LANES), (2, 2, sr, LANES), (2, 3, sr // 2, LANES),
         (8, LANES)],
        index_scratch + [pltpu.VMEM((3, fr, LANES), F32), pltpu.VMEM((3, sr, LANES), F32)]
        + z_scratch + total_scratch + [pltpu.VMEM((STEP, LANES), F32)],
        10**10,
        "middle",
    )
    fown, fguest = both(fsums, fwd_up, fwd_down)
    sown, sguest = both(ssums, side_up, side_down)
    extra, product = local(p)
    fz, sz, line = call(
        dots_kernel,
        [weights, dots, product, fsums, fown, fguest, finverse, ssums, sown, sguest, sinverse],
        [(2, 3, fr, LANES), (2, 3, sr, LANES), (segs, LANES)],
        [pltpu.VMEM((8, LANES), F32)],
        10**8,
        "dots",
    )
    line = lax.all_to_all(line, "seg", 0, 0, tiled=True)
    line = jnp.broadcast_to(jnp.sum(line, axis=0, keepdims=True), (strips, LANES))
    line = lax.all_to_all(line, "strip", 0, 0, tiled=True)
    (t,) = call(
        last_kernel,
        [weights, extra, fcam, fpoint, fcams, scam, spoint, scams, fseen, fz, sseen, sz],
        [(ROWS, LANES)],
        index_scratch + total_scratch,
        5 * 10**9,
        "last",
    )
    step, residual = call(
        close_kernel, [line, base, p, t], [(ROWS, LANES)] * 2, [], 10**6, "close"
    )
    return step.reshape(gradient.shape), residual.reshape(gradient.shape)


def solution(mesh):
    placed = (
        P(None, "strip", "seg"),
        P("strip", "seg"),
        P(None, None, "strip", "seg"),
        P(None, None, "strip", "seg"),
        P(None, "strip", "seg"),
        P(None, None, None, "strip", "seg"),
        P(None, None, None, "strip", "seg"),
        P(None, None, "strip", "seg"),
        P(None, None, None, "strip", "seg"),
        P(None, None, None, "strip", "seg"),
        P(None, None, "strip", "seg"),
    )
    return jax.shard_map(
        per_device,
        mesh=mesh,
        in_specs=placed,
        out_specs=(P(None, "strip", "seg"), P(None, "strip", "seg")),
        check_vma=False,
    )
```

```python
import jax
import jax.numpy as jnp
from jax import lax
from jax.experimental import pallas as pl
from jax.experimental.pallas import tpu as pltpu
from jax.sharding import PartitionSpec as P

AXES = ("strip", "seg")
LANES = 128
JAC = 9
PAGES = 4
ROWS = JAC * PAGES
LIFT = 40
STACK = 2 * LIFT
STEP = 16
SYM = ((0, 0), (0, 1), (0, 2), (1, 1), (1, 2), (2, 2))
DAMP = 1.0
VMEM = pl.BlockSpec(memory_space=pltpu.VMEM)
SMEM = pl.BlockSpec(memory_space=pltpu.SMEM)
FAR = pl.BlockSpec(memory_space=pltpu.HBM)
F32 = jnp.float32


def fetch(table, index):
    lane = index & (LANES - 1)
    odd = (index & LANES) != 0
    upper = index >= 2 * LANES
    found = []
    for j in range(JAC):
        page = [
            jnp.take_along_axis(
                jnp.broadcast_to(table[pl.ds(PAGES * j + k, 1), :], index.shape), lane, axis=1
            )
            for k in range(PAGES)
        ]
        low = jnp.where(odd, page[1], page[0])
        high = jnp.where(odd, page[3], page[2])
        found.append(jnp.where(upper, high, low))
    return found


def predict(across, values):
    return [sum(across[JAC * r + j] * values[j] for j in range(JAC)) for r in range(2)]


def project(along, seen):
    return [along[k] * seen[0] + along[3 + k] * seen[1] for k in range(3)]


def normal(along):
    return [along[i] * along[j] + along[3 + i] * along[3 + j] for i, j in SYM]


def invert(h):
    a, b, c, d, e, f = h[0] + DAMP, h[1], h[2], h[3] + DAMP, h[4], h[5] + DAMP
    first = d * f - e * e
    second = c * e - b * f
    third = b * e - c * d
    scale = 1.0 / (a * first + b * second + c * third)
    return [
        m * scale for m in (first, second, third, a * f - c * c, b * c - a * e, a * d - b * b)
    ]


def solve(m, b):
    return [
        m[0] * b[0] + m[1] * b[1] + m[2] * b[2],
        m[1] * b[0] + m[3] * b[1] + m[4] * b[2],
        m[2] * b[0] + m[4] * b[1] + m[5] * b[2],
    ]


def residue(along, seen, z):
    return [seen[r] - sum(along[3 * r + k] * z[k] for k in range(3)) for r in range(2)]


def spread(terms, index, stage, total):
    count = index.shape[0]
    page = index >> 7
    hit = [page == h for h in range(PAGES)]
    for j in range(JAC):
        coarse = terms[j].astype(jnp.bfloat16).astype(F32)
        fine = terms[j] - coarse
        for h in range(PAGES):
            row = PAGES * j + h
            stage[pl.ds(row, count, stride=STACK), :] = jnp.where(hit[h], coarse, 0.0)
            stage[pl.ds(LIFT + row, count, stride=STACK), :] = jnp.where(hit[h], fine, 0.0)
    lane = (index & (LANES - 1)).astype(F32)
    place = lax.broadcasted_iota(jnp.int32, (LANES, LANES), 0).astype(F32).astype(jnp.bfloat16)
    one, none = jnp.ones((), jnp.bfloat16), jnp.zeros((), jnp.bfloat16)
    group = 4 if count % 4 == 0 else 3
    for start in range(0, count, group):
        left, right = [], []
        for row in range(start, start + group):
            left.append(stage[pl.ds(row * STACK, STACK), :].astype(jnp.bfloat16))
            wide = jnp.broadcast_to(lane[row : row + 1], (16, LANES)).astype(jnp.bfloat16)
            wide = jnp.concatenate([wide] * (LANES // 16), axis=0)
            right.append(jnp.where(wide == place, one, none))
        total[...] += lax.dot_general(
            jnp.concatenate(left, axis=1),
            jnp.concatenate(right, axis=1),
            (((1,), (1,)), ((), ())),
            preferred_element_type=F32,
        )


def folded(total):
    return total[0:ROWS, :] + total[LIFT : LIFT + ROWS, :]


def weave(cams, index):
    half = cams.shape[2]
    for s in range(2):
        for o in range(2):
            index[s, pl.ds(o, half, stride=2), :] = cams[s, o]


def pair_look(cam, point, index, table, seen_out, loose, sums, sends, odd, with_h, squares, weights):
    rows = cam.shape[2]
    half = rows // 2
    for s in range(2):

        def body(i, carry, s=s):
            at = pl.ds(pl.multiple_of(i * STEP, STEP), STEP)
            across = [cam[s, j, at, :].astype(F32) for j in range(2 * JAC)]
            along = [point[s, j, at, :].astype(F32) for j in range(6)]
            seen = predict(across, fetch(table, index[s, at, :]))
            for r in range(2):
                seen_out[s, r, at, :] = seen[r]
            parts = project(along, seen)
            if with_h:
                parts = parts + normal(along)
            for n, part in enumerate(parts):
                loose[n, at, :] = part
            if squares is not None:
                squares[...] += weights[s] * (seen[0] * seen[0] + seen[1] * seen[1])
            return carry

        lax.fori_loop(0, rows // STEP, body, 0)
        for n in range(9 if with_h else 3):
            sums[s, n] = (
                loose[n, pl.ds(0, half, stride=2), :] + loose[n, pl.ds(1, half, stride=2), :]
            )

    for flag in range(2):

        @pl.when((odd > 0.5) == (flag == 1))
        def _(flag=flag):
            for s in range(2):
                sends[s ^ flag][...] = sums[s]


def pair_return(cam, point, index, seen_in, z, weights, stage, total):
    rows = cam.shape[2]
    for s in range(2):

        def body(i, carry, s=s):
            at = pl.ds(pl.multiple_of(i * STEP, STEP), STEP)
            across = [cam[s, j, at, :].astype(F32) for j in range(2 * JAC)]
            along = [point[s, j, at, :].astype(F32) for j in range(6)]
            left = residue(
                along, [seen_in[s, r, at, :] for r in range(2)], [z[s, k, at, :] for k in range(3)]
            )
            left = [weights[s] * e for e in left]
            terms = [across[j] * left[0] + across[JAC + j] * left[1] for j in range(JAC)]
            spread(terms, index[s, at, :], stage, total)
            return carry

        lax.fori_loop(0, rows // STEP, body, 0)


def pair_solve(mine, met, odd, inverse_out, inverse_in, z, products, weights):
    half = mine.shape[2]
    for s in range(2):
        first = (odd > 0.5) == (s == 1)
        for i in range(half // 8):
            at = pl.ds(8 * i, 8)

            def joined(k, at=at, first=first):
                return mine[s, k, at, :] + jnp.where(first, met[0][k, at, :], met[1][k, at, :])

            b = [joined(k) for k in range(3)]
            if inverse_in is None:
                inverse = invert([joined(3 + k) for k in range(6)])
                for k in range(6):
                    inverse_out[s, k, at, :] = inverse[k]
            else:
                inverse = [inverse_in[s, k, at, :] for k in range(6)]
            solved = solve(inverse, b)
            if products is not None:
                products[...] += weights[s] * sum(
                    mine[s, k, at, :] * solved[k] for k in range(3)
                )
            for k in range(3):
                for o in range(2):
                    z[s, k, pl.ds(16 * i + o, 8, stride=2), :] = solved[k]


def look_kernel(
    weights, gradient, fcam_at, fpoint_at, fcams_at, scam_at, spoint_at, scams_at,
    table, fseen, fsums, fsend0, fsend1, sseen, ssums, ssend0, ssend1,
    lines, fcam, fpoint, fcams, scam, spoint, scams, findex, sindex, floose, sloose, arrived,
):
    moves = [
        pltpu.make_async_copy(source, target, arrived.at[n])
        for n, (source, target) in enumerate(
            (
                (gradient, lines), (fcams_at, fcams), (scams_at, scams), (fcam_at, fcam),
                (fpoint_at, fpoint), (scam_at, scam), (spoint_at, spoint),
            )
        )
    ]
    for move in moves:
        move.start()
    for move in moves[:3]:
        move.wait()
    for j in range(JAC):
        for k in range(PAGES):
            table[pl.ds(PAGES * j + k, 1), :] = lines[j, :, pl.ds(LANES * k, LANES)]
    weave(fcams, findex)
    weave(scams, sindex)
    for move in moves[3:5]:
        move.wait()
    sends = (fsend0, fsend1)
    pair_look(fcam, fpoint, findex, table, fseen, floose, fsums, sends, weights[2], True, None, None)
    for move in moves[5:]:
        move.wait()
    sends = (ssend0, ssend1)
    pair_look(scam, spoint, sindex, table, sseen, sloose, ssums, sends, weights[3], True, None, None)


def local_kernel(live, table, cam, point, cams, out, product, stage, total):
    total[...] = jnp.zeros_like(total)
    stage[...] = jnp.zeros_like(stage)
    product[...] = jnp.zeros_like(product)
    watched = cams.shape[0] // 16

    def body(i, carry):
        at = pl.ds(pl.multiple_of(i * LANES, LANES), LANES)
        index = cams[pl.ds(i, watched, stride=16), :]
        across = [cam[j, :, at].astype(F32) for j in range(2 * JAC)]
        along = [point[j, :, at].astype(F32) for j in range(6)]
        seen = predict(across, fetch(table, index))
        summed = [jnp.sum(x, axis=0, keepdims=True) for x in project(along, seen) + normal(along)]
        z = solve(invert(summed[3:]), summed[:3])
        left = residue(along, seen, z)
        terms = [across[j] * left[0] + across[JAC + j] * left[1] for j in range(JAC)]
        product[0:1, :] += jnp.sum(seen[0] * left[0] + seen[1] * left[1], axis=0, keepdims=True)
        spread(terms, index, stage, total)
        return carry

    lax.fori_loop(0, live[0], body, 0)
    out[...] = folded(total)


def middle_kernel(
    weights, table, extra, fcam, fpoint, fcams, scam, spoint, scams,
    fseen, fsums, fmet0, fmet1, sseen, ssums, smet0, smet1,
    result, finverse, sinverse, fseen2, fsums2, fsend0, fsend1,
    sseen2, ssums2, ssend0, ssend1, dots,
    findex, sindex, floose, sloose, fz, sz, stage, total, squares,
):
    weave(fcams, findex)
    weave(scams, sindex)
    total[...] = jnp.zeros_like(total)
    stage[...] = jnp.zeros_like(stage)
    fweights = (1.0, weights[0])
    sweights = (1.0, weights[1])
    pair_solve(fsums, (fmet0, fmet1), weights[2], finverse, None, fz, None, None)
    pair_return(fcam, fpoint, findex, fseen, fz, fweights, stage, total)
    pair_solve(ssums, (smet0, smet1), weights[3], sinverse, None, sz, None, None)
    pair_return(scam, spoint, sindex, sseen, sz, sweights, stage, total)
    step = folded(total) + extra[...]
    result[...] = step
    squares[...] = jnp.zeros_like(squares)
    sends = (fsend0, fsend1)
    pair_look(
        fcam, fpoint, findex, result, fseen2, floose, fsums2, sends, weights[2], False,
        squares, fweights,
    )
    sends = (ssend0, ssend1)
    pair_look(
        scam, spoint, sindex, result, sseen2, sloose, ssums2, sends, weights[3], False,
        squares, sweights,
    )
    base = table[...]
    dots[...] = jnp.zeros_like(dots)
    for row, value in enumerate((base * base, base * step, step * step, squares[...])):
        dots[row : row + 1, :] = jnp.sum(value, axis=0, keepdims=True)


def dots_kernel(
    weights, dots, product, fsums, fmet0, fmet1, finverse, ssums, smet0, smet1, sinverse,
    fz, sz, out, products,
):
    products[...] = jnp.zeros_like(products)
    pair_solve(
        fsums, (fmet0, fmet1), weights[2], None, finverse, fz, products, (1.0, weights[0])
    )
    pair_solve(
        ssums, (smet0, smet1), weights[3], None, sinverse, sz, products, (1.0, weights[1])
    )
    curve = dots[3:4, :] + product[0:1, :] - jnp.sum(products[...], axis=0, keepdims=True)
    rows = jnp.concatenate([dots[0:3, :], curve], axis=0)
    sums = jnp.sum(rows, axis=1, keepdims=True)
    place = lax.broadcasted_iota(jnp.int32, (1, LANES), 1)
    line = jnp.zeros((1, LANES), F32)
    for n in range(4):
        line = line + jnp.where(place == n, sums[n : n + 1, :], 0.0)
    out[...] = jnp.broadcast_to(line, out.shape)


def last_kernel(
    weights, extra, fcam, fpoint, fcams, scam, spoint, scams, fseen, fz, sseen, sz,
    result, findex, sindex, stage, total,
):
    weave(fcams, findex)
    weave(scams, sindex)
    total[...] = jnp.zeros_like(total)
    stage[...] = jnp.zeros_like(stage)
    pair_return(fcam, fpoint, findex, fseen, fz, (1.0, weights[0]), stage, total)
    pair_return(scam, spoint, sindex, sseen, sz, (1.0, weights[1]), stage, total)
    result[...] = folded(total) + extra[...]


def close_kernel(sums, base, first, second, step_out, residual_out):
    line = jnp.sum(sums[...], axis=0, keepdims=True)
    place = lax.broadcasted_iota(jnp.int32, line.shape, 1)
    rr, bp, pp, curve = [
        jnp.sum(jnp.where(place == n, line, 0.0), axis=1, keepdims=True) for n in range(4)
    ]
    whole = rr + bp
    alpha = rr / whole
    rest = bp / whole
    new = alpha * (alpha * pp - rest * bp)
    gamma = rest + new / rr
    bend = gamma * gamma * rr - 2.0 * gamma * alpha * bp + alpha * alpha * pp
    bend = bend + gamma * gamma * bp - 2.0 * gamma * alpha * pp + alpha * alpha * curve
    again = new / bend
    d0, p, t = base[...], first[...], second[...]
    direction = gamma * d0 - alpha * p
    image = gamma * d0 + (gamma - alpha) * p - alpha * t
    step = -(alpha * d0 + again * direction)
    residual = -(rest * d0 - alpha * p - again * image)
    for j in range(JAC):
        for k in range(PAGES):
            row = PAGES * j + k
            step_out[j, :, pl.ds(LANES * k, LANES)] = step[row : row + 1, :]
            residual_out[j, :, pl.ds(LANES * k, LANES)] = residual[row : row + 1, :]


def call(kernel, ins, outs, scratch, flops, name, place=VMEM, room=12):
    outs = [jax.ShapeDtypeStruct(shape, F32) for shape in outs]
    specs = [SMEM if i == 0 and x.ndim == 1 else place for i, x in enumerate(ins)]
    return pl.pallas_call(
        kernel,
        out_shape=outs,
        in_specs=specs,
        out_specs=[VMEM] * len(outs),
        scratch_shapes=scratch,
        compiler_params=pltpu.CompilerParams(vmem_limit_bytes=room << 20),
        cost_estimate=pl.CostEstimate(flops=flops, bytes_accessed=2 << 20, transcendentals=0),
        name=name,
    )(*ins)


def rows_of(array):
    kinds, parts, two, _, points = array.shape
    array = array.reshape(kinds, parts, two, points // LANES, LANES)
    return array.transpose(0, 1, 3, 2, 4).reshape(kinds, parts, two * points // LANES, LANES)


def per_device(
    gradient, live_blocks, loc_cam_jac, loc_point_jac, loc_cams,
    fwd_cam_jac, fwd_point_jac, fwd_cams, side_cam_jac, side_point_jac, side_cams,
):
    strips, segs = lax.axis_size("strip"), lax.axis_size("seg")
    cells = [(s, g) for s in range(strips) for g in range(segs)]

    def pairs(move):
        found = []
        for s, g in cells:
            t, h = move(s, g)
            if 0 <= t < strips and 0 <= h < segs:
                found.append((s * segs + g, t * segs + h))
        return found

    fwd_rounds = pairs(lambda s, g: (s, g ^ 1)), pairs(lambda s, g: (s, (g + 1 ^ 1) - 1))
    side_rounds = (
        pairs(lambda s, g: (s ^ 1, segs - 1 - g)),
        pairs(lambda s, g: ((s + 1 ^ 1) - 1, segs - 1 - g)),
    )
    seg, strip = lax.axis_index("seg"), lax.axis_index("strip")
    weights = jnp.stack([seg > 0, strip > 0, (seg & 1) > 0, (strip & 1) > 0]).astype(F32)
    live = live_blocks.reshape(1)
    lcam, lpoint = loc_cam_jac[:, :, 0], loc_point_jac[:, :, 0]
    lcams = loc_cams.reshape(-1, LANES)
    fcam, fpoint = rows_of(fwd_cam_jac), rows_of(fwd_point_jac)
    scam, spoint = rows_of(side_cam_jac), rows_of(side_point_jac)
    fcams = fwd_cams.reshape(2, 2, -1, LANES)
    scams = side_cams.reshape(2, 2, -1, LANES)
    fr, sr = fcam.shape[2], scam.shape[2]
    watched = lcam.shape[1]

    def meet(sends, rounds):
        return [lax.ppermute(send, AXES, pairs) for send, pairs in zip(sends, rounds)]

    index_scratch = [pltpu.VMEM((2, fr, LANES), jnp.int32), pltpu.VMEM((2, sr, LANES), jnp.int32)]
    z_scratch = [pltpu.VMEM((2, 3, fr, LANES), F32), pltpu.VMEM((2, 3, sr, LANES), F32)]
    total_scratch = [pltpu.VMEM((STEP * STACK, LANES), F32), pltpu.VMEM((STACK, LANES), F32)]

    def sends_of(parts):
        return [(parts, fr // 2, LANES)] * 2, [(parts, sr // 2, LANES)] * 2

    far = [gradient, fcam, fpoint, fcams, scam, spoint, scams]
    fshapes, sshapes = sends_of(9)
    base, fseen, fsums, *sends, sseen, ssums, ssend0, ssend1 = call(
        look_kernel,
        [weights] + far,
        [(ROWS, LANES), (2, 2, fr, LANES), (2, 9, fr // 2, LANES)] + fshapes
        + [(2, 2, sr, LANES), (2, 9, sr // 2, LANES)] + sshapes,
        [pltpu.VMEM(far[n].shape, far[n].dtype) for n in (0, 1, 2, 3, 4, 5, 6)]
        + index_scratch
        + [pltpu.VMEM((9, fr, LANES), F32), pltpu.VMEM((9, sr, LANES), F32)]
        + [pltpu.SemaphoreType.DMA((len(far),))],
        10**9,
        "look",
        FAR,
        63,
    )
    smet = meet((ssend0, ssend1), side_rounds)
    fmet = meet(sends, fwd_rounds)

    def local(table):
        return call(
            local_kernel,
            [live, table, lcam, lpoint, lcams],
            [(ROWS, LANES), (8, LANES)],
            [pltpu.VMEM((watched * STACK, LANES), F32), pltpu.VMEM((STACK, LANES), F32)],
            5 * 10**9,
            "local",
        )

    extra, _ = local(base)
    fshapes, sshapes = sends_of(3)
    p, finverse, sinverse, fseen, fsums2, fsend0, fsend1, sseen, ssums2, ssend0, ssend1, dots = call(
        middle_kernel,
        [weights, base, extra, fcam, fpoint, fcams, scam, spoint, scams,
         fseen, fsums, *fmet, sseen, ssums, *smet],
        [(ROWS, LANES), (2, 6, fr // 2, LANES), (2, 6, sr // 2, LANES),
         (2, 2, fr, LANES), (2, 3, fr // 2, LANES)] + fshapes
        + [(2, 2, sr, LANES), (2, 3, sr // 2, LANES)] + sshapes + [(8, LANES)],
        index_scratch + [pltpu.VMEM((3, fr, LANES), F32), pltpu.VMEM((3, sr, LANES), F32)]
        + z_scratch + total_scratch + [pltpu.VMEM((STEP, LANES), F32)],
        10**10,
        "middle",
    )
    smet = meet((ssend0, ssend1), side_rounds)
    fmet = meet((fsend0, fsend1), fwd_rounds)
    extra, product = local(p)
    fz, sz, line = call(
        dots_kernel,
        [weights, dots, product, fsums2, *fmet, finverse, ssums2, *smet, sinverse],
        [(2, 3, fr, LANES), (2, 3, sr, LANES), (strips * segs, LANES)],
        [pltpu.VMEM((8, LANES), F32)],
        10**8,
        "dots",
    )
    line = lax.all_to_all(line, AXES, 0, 0, tiled=True)
    (t,) = call(
        last_kernel,
        [weights, extra, fcam, fpoint, fcams, scam, spoint, scams, fseen, fz, sseen, sz],
        [(ROWS, LANES)],
        index_scratch + total_scratch,
        5 * 10**9,
        "last",
    )
    step, residual = call(
        close_kernel, [line, base, p, t], [gradient.shape] * 2, [], 10**6, "close"
    )
    return step, residual


def solution(mesh):
    placed = (
        P(None, "strip", "seg"),
        P("strip", "seg"),
        P(None, None, "strip", "seg"),
        P(None, None, "strip", "seg"),
        P(None, "strip", "seg"),
        P(None, None, None, "strip", "seg"),
        P(None, None, None, "strip", "seg"),
        P(None, None, "strip", "seg"),
        P(None, None, None, "strip", "seg"),
        P(None, None, None, "strip", "seg"),
        P(None, None, "strip", "seg"),
    )
    return jax.shard_map(
        per_device,
        mesh=mesh,
        in_specs=placed,
        out_specs=(P(None, "strip", "seg"), P(None, "strip", "seg")),
        check_vma=False,
    )
```

```python
import jax
import jax.numpy as jnp
from jax import lax
from jax.experimental import pallas as pl
from jax.experimental.pallas import tpu as pltpu
from jax.sharding import PartitionSpec as P

AXES = ("strip", "seg")
LANES = 128
JAC = 9
PAGES = 4
ROWS = JAC * PAGES
LIFT = 40
STACK = 2 * LIFT
STEP = 16
LOOK_UNROLL = 1
RETURN_UNROLL = 1
SYM = ((0, 0), (0, 1), (0, 2), (1, 1), (1, 2), (2, 2))
DAMP = 1.0
VMEM = pl.BlockSpec(memory_space=pltpu.VMEM)
SMEM = pl.BlockSpec(memory_space=pltpu.SMEM)
FAR = pl.BlockSpec(memory_space=pltpu.HBM)
F32 = jnp.float32


def fetch(table, index):
    lane = index & (LANES - 1)
    odd = (index & LANES) != 0
    upper = index >= 2 * LANES
    found = []
    for j in range(JAC):
        page = [
            jnp.take_along_axis(
                jnp.broadcast_to(table[pl.ds(PAGES * j + k, 1), :], index.shape), lane, axis=1
            )
            for k in range(PAGES)
        ]
        low = jnp.where(odd, page[1], page[0])
        high = jnp.where(odd, page[3], page[2])
        found.append(jnp.where(upper, high, low))
    return found


def predict(across, values):
    return [sum(across[JAC * r + j] * values[j] for j in range(JAC)) for r in range(2)]


def project(along, seen):
    return [along[k] * seen[0] + along[3 + k] * seen[1] for k in range(3)]


def normal(along):
    return [along[i] * along[j] + along[3 + i] * along[3 + j] for i, j in SYM]


def invert(h):
    a, b, c, d, e, f = h[0] + DAMP, h[1], h[2], h[3] + DAMP, h[4], h[5] + DAMP
    first = d * f - e * e
    second = c * e - b * f
    third = b * e - c * d
    scale = 1.0 / (a * first + b * second + c * third)
    return [
        m * scale for m in (first, second, third, a * f - c * c, b * c - a * e, a * d - b * b)
    ]


def solve(m, b):
    return [
        m[0] * b[0] + m[1] * b[1] + m[2] * b[2],
        m[1] * b[0] + m[3] * b[1] + m[4] * b[2],
        m[2] * b[0] + m[4] * b[1] + m[5] * b[2],
    ]


def residue(along, seen, z):
    return [seen[r] - sum(along[3 * r + k] * z[k] for k in range(3)) for r in range(2)]


def spread(terms, index, stage, total):
    count = index.shape[0]
    page = index >> 7
    hit = [page == h for h in range(PAGES)]
    for j in range(JAC):
        coarse = terms[j].astype(jnp.bfloat16).astype(F32)
        fine = terms[j] - coarse
        for h in range(PAGES):
            row = PAGES * j + h
            stage[pl.ds(row, count, stride=STACK), :] = jnp.where(hit[h], coarse, 0.0)
            stage[pl.ds(LIFT + row, count, stride=STACK), :] = jnp.where(hit[h], fine, 0.0)
    lane = (index & (LANES - 1)).astype(F32)
    place = lax.broadcasted_iota(jnp.int32, (LANES, LANES), 0).astype(F32).astype(jnp.bfloat16)
    one, none = jnp.ones((), jnp.bfloat16), jnp.zeros((), jnp.bfloat16)
    group = 4 if count % 4 == 0 else 3
    for start in range(0, count, group):
        left, right = [], []
        for row in range(start, start + group):
            left.append(stage[pl.ds(row * STACK, STACK), :].astype(jnp.bfloat16))
            wide = jnp.broadcast_to(lane[row : row + 1], (16, LANES)).astype(jnp.bfloat16)
            wide = jnp.concatenate([wide] * (LANES // 16), axis=0)
            right.append(jnp.where(wide == place, one, none))
        total[...] += lax.dot_general(
            jnp.concatenate(left, axis=1),
            jnp.concatenate(right, axis=1),
            (((1,), (1,)), ((), ())),
            preferred_element_type=F32,
        )


def folded(total):
    return total[0:ROWS, :] + total[LIFT : LIFT + ROWS, :]


def weave(cams, index):
    half = cams.shape[2]
    for s in range(2):
        for o in range(2):
            index[s, pl.ds(o, half, stride=2), :] = cams[s, o]


def pair_look(cam, point, index, table, seen_out, loose, sends, odd, with_h, squares, held, done):
    rows = cam.shape[2]
    half = rows // 2
    for turn in range(2):
        s = turn ^ odd
        share = part_of(s, held)

        def body(i, carry, s=s, turn=turn, share=share):
            at = pl.ds(pl.multiple_of(i * STEP, STEP), STEP)
            across = [cam[s, j, at, :].astype(F32) for j in range(2 * JAC)]
            along = [point[s, j, at, :].astype(F32) for j in range(6)]
            seen = predict(across, fetch(table, index[s, at, :]))
            for r in range(2):
                seen_out[turn, r, at, :] = seen[r]
            parts = project(along, seen)
            if with_h:
                parts = parts + normal(along)
            for n, part in enumerate(parts):
                loose[n, at, :] = part
            if squares is not None:
                squares[...] += share * (seen[0] * seen[0] + seen[1] * seen[1])
            return carry

        lax.fori_loop(0, rows // STEP, body, 0, unroll=LOOK_UNROLL)
        for n in range(9 if with_h else 3):
            sends[turn][n] = (
                loose[n, pl.ds(0, half, stride=2), :] + loose[n, pl.ds(1, half, stride=2), :]
            )
        if done is not None:
            done(turn)


def part_of(side, held):
    return jnp.where(side == 0, 1, held).astype(F32)


def pair_return(cam, point, index, seen_in, z, odd, held, stage, total):
    rows = cam.shape[2]
    for turn in range(2):
        s = turn ^ odd
        share = part_of(s, held)

        def body(i, carry, s=s, turn=turn, share=share):
            at = pl.ds(pl.multiple_of(i * STEP, STEP), STEP)
            across = [cam[s, j, at, :].astype(F32) for j in range(2 * JAC)]
            along = [point[s, j, at, :].astype(F32) for j in range(6)]
            left = residue(
                along,
                [seen_in[turn, r, at, :] for r in range(2)],
                [z[turn, k, at, :] for k in range(3)],
            )
            left = [share * e for e in left]
            terms = [across[j] * left[0] + across[JAC + j] * left[1] for j in range(JAC)]
            spread(terms, index[s, at, :], stage, total)
            return carry

        lax.fori_loop(0, rows // STEP, body, 0, unroll=RETURN_UNROLL)


def pair_solve(sent, met, inverse_out, inverse_in, z, products, odd, held):
    half = sent[0].shape[1]
    for turn in range(2):
        share = part_of(turn ^ odd, held)
        for i in range(half // 8):
            at = pl.ds(8 * i, 8)
            mine = [sent[turn][k, at, :] for k in range(3)]
            b = [mine[k] + met[turn][k, at, :] for k in range(3)]
            if inverse_in is None:
                inverse = invert(
                    [sent[turn][3 + k, at, :] + met[turn][3 + k, at, :] for k in range(6)]
                )
                for k in range(6):
                    inverse_out[turn, k, at, :] = inverse[k]
            else:
                inverse = [inverse_in[turn, k, at, :] for k in range(6)]
            solved = solve(inverse, b)
            if products is not None:
                products[...] += share * sum(mine[k] * solved[k] for k in range(3))
            for k in range(3):
                for o in range(2):
                    z[turn, k, pl.ds(16 * i + o, 8, stride=2), :] = solved[k]


def place_of():
    seg, strip = lax.axis_index("seg"), lax.axis_index("strip")
    return (seg & 1, jnp.minimum(seg, 1)), (strip & 1, jnp.minimum(strip, 1))


def in_rows(lines, table):
    for j in range(JAC):
        for k in range(PAGES):
            table[pl.ds(PAGES * j + k, 1), :] = lines[j, :, pl.ds(LANES * k, LANES)]


def look_kernel(
    gradient, fcam_at, fpoint_at, fcams_at, scam_at, spoint_at, scams_at,
    fseen_at, fsend0_at, fsend1_at, sseen_at, ssend0_at, ssend1_at,
    lines, fcam, fpoint, fcams, scam, spoint, scams,
    fseen, fsend0, fsend1, sseen, ssend0, ssend1,
    table, findex, sindex, floose, sloose, arrived, left,
):
    (fodd, _), (sodd, _) = place_of()
    moves = [
        pltpu.make_async_copy(source, target, arrived.at[n])
        for n, (source, target) in enumerate(
            (
                (gradient, lines), (scams_at, scams), (scam_at, scam), (spoint_at, spoint),
                (fcams_at, fcams), (fcam_at, fcam), (fpoint_at, fpoint),
            )
        )
    ]
    back = [
        pltpu.make_async_copy(source, target, left.at[n])
        for n, (source, target) in enumerate(
            (
                (ssend0, ssend0_at), (ssend1, ssend1_at), (sseen, sseen_at),
                (fsend0, fsend0_at), (fsend1, fsend1_at), (fseen, fseen_at),
            )
        )
    ]
    for move in moves:
        move.start()
    for move in moves[:2]:
        move.wait()
    in_rows(lines, table)
    weave(scams, sindex)
    for move in moves[2:4]:
        move.wait()

    def sent(first):
        def done(turn):
            back[first + turn].start()
            if turn == 1:
                back[first + 2].start()

        return done

    pair_look(
        scam, spoint, sindex, table, sseen, sloose, (ssend0, ssend1), sodd, True, None, 0, sent(0)
    )
    moves[4].wait()
    weave(fcams, findex)
    for move in moves[5:]:
        move.wait()
    pair_look(
        fcam, fpoint, findex, table, fseen, floose, (fsend0, fsend1), fodd, True, None, 0, sent(3)
    )
    for move in back:
        move.wait()


def local_kernel(live, values, cam, point, cams, out, product, stage, total, table):
    total[...] = jnp.zeros_like(total)
    stage[...] = jnp.zeros_like(stage)
    product[...] = jnp.zeros_like(product)
    if values.shape[0] == JAC:
        in_rows(values, table)
    else:
        table = values
    watched = cams.shape[0] // 16

    def body(i, carry):
        at = pl.ds(pl.multiple_of(i * LANES, LANES), LANES)
        index = cams[pl.ds(i, watched, stride=16), :]
        across = [cam[j, :, at].astype(F32) for j in range(2 * JAC)]
        along = [point[j, :, at].astype(F32) for j in range(6)]
        seen = predict(across, fetch(table, index))
        summed = [jnp.sum(x, axis=0, keepdims=True) for x in project(along, seen) + normal(along)]
        z = solve(invert(summed[3:]), summed[:3])
        left = residue(along, seen, z)
        terms = [across[j] * left[0] + across[JAC + j] * left[1] for j in range(JAC)]
        product[0:1, :] += jnp.sum(seen[0] * left[0] + seen[1] * left[1], axis=0, keepdims=True)
        spread(terms, index, stage, total)
        return carry

    lax.fori_loop(0, live[0], body, 0)
    out[...] = folded(total)


def middle_kernel(
    lines, extra, fcam, fpoint, fcams, scam, spoint, scams,
    fseen, fsent0, fsent1, fmet0, fmet1, sseen, ssent0, ssent1, smet0, smet1,
    result, finverse, sinverse, fseen2, fsend0, fsend1, sseen2, ssend0, ssend1, dots,
    table, findex, sindex, floose, sloose, fz, sz, stage, total, squares,
):
    (fodd, fheld), (sodd, sheld) = place_of()
    in_rows(lines, table)
    weave(fcams, findex)
    weave(scams, sindex)
    total[...] = jnp.zeros_like(total)
    stage[...] = jnp.zeros_like(stage)
    pair_solve((fsent0, fsent1), (fmet0, fmet1), finverse, None, fz, None, fodd, fheld)
    pair_return(fcam, fpoint, findex, fseen, fz, fodd, fheld, stage, total)
    pair_solve((ssent0, ssent1), (smet0, smet1), sinverse, None, sz, None, sodd, sheld)
    pair_return(scam, spoint, sindex, sseen, sz, sodd, sheld, stage, total)
    step = folded(total) + extra[...]
    result[...] = step
    squares[...] = jnp.zeros_like(squares)
    sends = (fsend0, fsend1)
    pair_look(
        fcam, fpoint, findex, result, fseen2, floose, sends, fodd, False, squares, fheld, None
    )
    sends = (ssend0, ssend1)
    pair_look(
        scam, spoint, sindex, result, sseen2, sloose, sends, sodd, False, squares, sheld, None
    )
    base = table[...]
    dots[...] = jnp.zeros_like(dots)
    for row, value in enumerate((base * base, base * step, step * step, squares[...])):
        dots[row : row + 1, :] = jnp.sum(value, axis=0, keepdims=True)


def dots_kernel(
    dots, product, fsent0, fsent1, fmet0, fmet1, finverse,
    ssent0, ssent1, smet0, smet1, sinverse, fz, sz, out, products,
):
    (fodd, fheld), (sodd, sheld) = place_of()
    products[...] = jnp.zeros_like(products)
    pair_solve((fsent0, fsent1), (fmet0, fmet1), None, finverse, fz, products, fodd, fheld)
    pair_solve((ssent0, ssent1), (smet0, smet1), None, sinverse, sz, products, sodd, sheld)
    curve = dots[3:4, :] + product[0:1, :] - jnp.sum(products[...], axis=0, keepdims=True)
    rows = jnp.concatenate([dots[0:3, :], curve], axis=0)
    sums = jnp.sum(rows, axis=1, keepdims=True)
    place = lax.broadcasted_iota(jnp.int32, (1, LANES), 1)
    line = jnp.zeros((1, LANES), F32)
    for n in range(4):
        line = line + jnp.where(place == n, sums[n : n + 1, :], 0.0)
    out[...] = jnp.broadcast_to(line, out.shape)


def last_kernel(
    extra, fcam, fpoint, fcams, scam, spoint, scams, fseen, fz, sseen, sz,
    result, findex, sindex, stage, total,
):
    (fodd, fheld), (sodd, sheld) = place_of()
    weave(fcams, findex)
    weave(scams, sindex)
    total[...] = jnp.zeros_like(total)
    stage[...] = jnp.zeros_like(stage)
    pair_return(fcam, fpoint, findex, fseen, fz, fodd, fheld, stage, total)
    pair_return(scam, spoint, sindex, sseen, sz, sodd, sheld, stage, total)
    result[...] = folded(total) + extra[...]


def close_kernel(sums, lines, first, second, step_out, residual_out, base):
    in_rows(lines, base)
    line = jnp.sum(sums[...], axis=0, keepdims=True)
    place = lax.broadcasted_iota(jnp.int32, line.shape, 1)
    rr, bp, pp, curve = [
        jnp.sum(jnp.where(place == n, line, 0.0), axis=1, keepdims=True) for n in range(4)
    ]
    whole = rr + bp
    alpha = rr / whole
    rest = bp / whole
    new = alpha * (alpha * pp - rest * bp)
    gamma = rest + new / rr
    bend = gamma * gamma * rr - 2.0 * gamma * alpha * bp + alpha * alpha * pp
    bend = bend + gamma * gamma * bp - 2.0 * gamma * alpha * pp + alpha * alpha * curve
    again = new / bend
    d0, p, t = base[...], first[...], second[...]
    direction = gamma * d0 - alpha * p
    image = gamma * d0 + (gamma - alpha) * p - alpha * t
    step = -(alpha * d0 + again * direction)
    residual = -(rest * d0 - alpha * p - again * image)
    for j in range(JAC):
        for k in range(PAGES):
            row = PAGES * j + k
            step_out[j, :, pl.ds(LANES * k, LANES)] = step[row : row + 1, :]
            residual_out[j, :, pl.ds(LANES * k, LANES)] = residual[row : row + 1, :]


def call(kernel, ins, outs, scratch, flops, name, place=VMEM, to=VMEM, room=12):
    outs = [jax.ShapeDtypeStruct(shape, F32) for shape in outs]
    specs = [SMEM if i == 0 and x.ndim == 1 else place for i, x in enumerate(ins)]
    return pl.pallas_call(
        kernel,
        out_shape=outs,
        in_specs=specs,
        out_specs=[to] * len(outs),
        scratch_shapes=scratch,
        compiler_params=pltpu.CompilerParams(vmem_limit_bytes=room << 20),
        cost_estimate=pl.CostEstimate(flops=flops, bytes_accessed=2 << 20, transcendentals=0),
        name=name,
    )(*ins)


def rows_of(array):
    kinds, parts, two, _, points = array.shape
    array = array.reshape(kinds, parts, two, points // LANES, LANES)
    return array.transpose(0, 1, 3, 2, 4).reshape(kinds, parts, two * points // LANES, LANES)


def per_device(
    gradient, live_blocks, loc_cam_jac, loc_point_jac, loc_cams,
    fwd_cam_jac, fwd_point_jac, fwd_cams, side_cam_jac, side_point_jac, side_cams,
):
    strips, segs = lax.axis_size("strip"), lax.axis_size("seg")
    cells = [(s, g) for s in range(strips) for g in range(segs)]

    def pairs(move):
        found = []
        for s, g in cells:
            t, h = move(s, g)
            if 0 <= t < strips and 0 <= h < segs:
                found.append((s * segs + g, t * segs + h))
        return found

    fwd_rounds = pairs(lambda s, g: (s, g ^ 1)), pairs(lambda s, g: (s, (g + 1 ^ 1) - 1))
    side_rounds = (
        pairs(lambda s, g: (s ^ 1, segs - 1 - g)),
        pairs(lambda s, g: ((s + 1 ^ 1) - 1, segs - 1 - g)),
    )
    live = live_blocks.reshape(1)
    lcam, lpoint = loc_cam_jac[:, :, 0], loc_point_jac[:, :, 0]
    lcams = loc_cams.reshape(-1, LANES)
    fcam, fpoint = rows_of(fwd_cam_jac), rows_of(fwd_point_jac)
    scam, spoint = rows_of(side_cam_jac), rows_of(side_point_jac)
    fcams = fwd_cams.reshape(2, 2, -1, LANES)
    scams = side_cams.reshape(2, 2, -1, LANES)
    fr, sr = fcam.shape[2], scam.shape[2]
    watched = lcam.shape[1]

    def meet(sends, rounds):
        return [lax.ppermute(send, AXES, pairs) for send, pairs in zip(sends, rounds)]

    index_scratch = [pltpu.VMEM((2, fr, LANES), jnp.int32), pltpu.VMEM((2, sr, LANES), jnp.int32)]
    z_scratch = [pltpu.VMEM((2, 3, fr, LANES), F32), pltpu.VMEM((2, 3, sr, LANES), F32)]
    total_scratch = [pltpu.VMEM((STEP * STACK, LANES), F32), pltpu.VMEM((STACK, LANES), F32)]

    def sends_of(parts):
        return [(parts, fr // 2, LANES)] * 2, [(parts, sr // 2, LANES)] * 2

    far = [gradient, fcam, fpoint, fcams, scam, spoint, scams]
    table = [pltpu.VMEM((ROWS, LANES), F32)]
    fshapes, sshapes = sends_of(9)
    shapes = [(2, 2, fr, LANES)] + fshapes + [(2, 2, sr, LANES)] + sshapes
    fseen, *fsent, sseen, ssent0, ssent1 = call(
        look_kernel,
        far,
        shapes,
        [pltpu.VMEM(x.shape, x.dtype) for x in far]
        + [pltpu.VMEM(shape, F32) for shape in shapes]
        + table
        + index_scratch
        + [pltpu.VMEM((9, fr, LANES), F32), pltpu.VMEM((9, sr, LANES), F32)]
        + [pltpu.SemaphoreType.DMA((len(far),)), pltpu.SemaphoreType.DMA((len(shapes),))],
        10**9,
        "look",
        FAR,
        FAR,
        63,
    )
    ssent = [ssent0, ssent1]
    smet = meet(ssent, side_rounds)
    fmet = meet(fsent, fwd_rounds)

    def local(values):
        return call(
            local_kernel,
            [live, values, lcam, lpoint, lcams],
            [(ROWS, LANES), (8, LANES)],
            [pltpu.VMEM((watched * STACK, LANES), F32), pltpu.VMEM((STACK, LANES), F32)] + table,
            5 * 10**9,
            "local",
        )

    extra, _ = local(gradient)
    fshapes, sshapes = sends_of(3)
    p, finverse, sinverse, fseen, fsend0, fsend1, sseen, ssend0, ssend1, dots = call(
        middle_kernel,
        [gradient, extra, fcam, fpoint, fcams, scam, spoint, scams,
         fseen, *fsent, *fmet, sseen, *ssent, *smet],
        [(ROWS, LANES), (2, 6, fr // 2, LANES), (2, 6, sr // 2, LANES), (2, 2, fr, LANES)]
        + fshapes + [(2, 2, sr, LANES)] + sshapes + [(8, LANES)],
        table + index_scratch
        + [pltpu.VMEM((3, fr, LANES), F32), pltpu.VMEM((3, sr, LANES), F32)]
        + z_scratch + total_scratch + [pltpu.VMEM((STEP, LANES), F32)],
        10**10,
        "middle",
    )
    fsent, ssent = [fsend0, fsend1], [ssend0, ssend1]
    smet = meet(ssent, side_rounds)
    fmet = meet(fsent, fwd_rounds)
    extra, product = local(p)
    fz, sz, line = call(
        dots_kernel,
        [dots, product, *fsent, *fmet, finverse, *ssent, *smet, sinverse],
        [(2, 3, fr, LANES), (2, 3, sr, LANES), (strips * segs, LANES)],
        [pltpu.VMEM((8, LANES), F32)],
        10**8,
        "dots",
    )
    line = lax.all_to_all(line, AXES, 0, 0, tiled=True)
    (t,) = call(
        last_kernel,
        [extra, fcam, fpoint, fcams, scam, spoint, scams, fseen, fz, sseen, sz],
        [(ROWS, LANES)],
        index_scratch + total_scratch,
        5 * 10**9,
        "last",
    )
    step, residual = call(
        close_kernel, [line, gradient, p, t], [gradient.shape] * 2, table, 10**6, "close"
    )
    return step, residual


def solution(mesh):
    placed = (
        P(None, "strip", "seg"),
        P("strip", "seg"),
        P(None, None, "strip", "seg"),
        P(None, None, "strip", "seg"),
        P(None, "strip", "seg"),
        P(None, None, None, "strip", "seg"),
        P(None, None, None, "strip", "seg"),
        P(None, None, "strip", "seg"),
        P(None, None, None, "strip", "seg"),
        P(None, None, None, "strip", "seg"),
        P(None, None, "strip", "seg"),
    )
    return jax.shard_map(
        per_device,
        mesh=mesh,
        in_specs=placed,
        out_specs=(P(None, "strip", "seg"), P(None, "strip", "seg")),
        check_vma=False,
    )
```

```python
import jax
import jax.numpy as jnp
from jax import lax
from jax.experimental import pallas as pl
from jax.experimental.pallas import tpu as pltpu
from jax.sharding import PartitionSpec as P

AXES = ("strip", "seg")
LANES = 128
JAC = 9
PAGES = 4
ROWS = JAC * PAGES
STACK = 80
STEP = 16
LOCAL_GROUP = 8
SYM = ((0, 0), (0, 1), (0, 2), (1, 1), (1, 2), (2, 2))
DAMP = 1.0
VMEM = pl.BlockSpec(memory_space=pltpu.VMEM)
SMEM = pl.BlockSpec(memory_space=pltpu.SMEM)
FAR = pl.BlockSpec(memory_space=pltpu.HBM)
F32 = jnp.float32


def fetch(table, index):
    lane = index & (LANES - 1)
    odd = (index & LANES) != 0
    upper = index >= 2 * LANES
    found = []
    for j in range(JAC):
        page = [
            jnp.take_along_axis(
                jnp.broadcast_to(table[pl.ds(PAGES * j + k, 1), :], index.shape), lane, axis=1
            )
            for k in range(PAGES)
        ]
        low = jnp.where(odd, page[1], page[0])
        high = jnp.where(odd, page[3], page[2])
        found.append(jnp.where(upper, high, low))
    return found


def predict(across, values):
    return [sum(across[JAC * r + j] * values[j] for j in range(JAC)) for r in range(2)]


def project(along, seen):
    return [along[k] * seen[0] + along[3 + k] * seen[1] for k in range(3)]


def normal(along):
    return [along[i] * along[j] + along[3 + i] * along[3 + j] for i, j in SYM]


def invert(h):
    a, b, c, d, e, f = h[0] + DAMP, h[1], h[2], h[3] + DAMP, h[4], h[5] + DAMP
    first = d * f - e * e
    second = c * e - b * f
    third = b * e - c * d
    scale = 1.0 / (a * first + b * second + c * third)
    return [
        m * scale for m in (first, second, third, a * f - c * c, b * c - a * e, a * d - b * b)
    ]


def solve(m, b):
    return [
        m[0] * b[0] + m[1] * b[1] + m[2] * b[2],
        m[1] * b[0] + m[3] * b[1] + m[4] * b[2],
        m[2] * b[0] + m[4] * b[1] + m[5] * b[2],
    ]


def residue(along, seen, z):
    return [seen[r] - sum(along[3 * r + k] * z[k] for k in range(3)) for r in range(2)]


def spread(terms, index, stage, total):
    add_in([stacked(terms, index, stage)], total)


def add_in(parts, total):
    total[...] += lax.dot_general(
        jnp.concatenate([x for left, _ in parts for x in left], axis=1),
        jnp.concatenate([x for _, right in parts for x in right], axis=1),
        (((1,), (1,)), ((), ())),
        preferred_element_type=F32,
    )


def stacked(terms, index, stage):
    count = index.shape[0]
    page = index >> 7
    coarse = terms[JAC - 1].astype(jnp.bfloat16).astype(F32)
    fine = terms[JAC - 1] - coarse
    for j in range(JAC - 1):
        stage[pl.ds(j, count, stride=16), :] = terms[j]
    for h in range(PAGES):
        stage[pl.ds(8 + h, count, stride=16), :] = jnp.where(page == h, coarse, 0.0)
        stage[pl.ds(12 + h, count, stride=16), :] = jnp.where(page == h, fine, 0.0)
    page = page.astype(F32)
    lane = (index & (LANES - 1)).astype(F32)
    place = lax.broadcasted_iota(jnp.int32, (LANES, LANES), 0).astype(F32).astype(jnp.bfloat16)
    one, none = jnp.ones((), jnp.bfloat16), jnp.zeros((), jnp.bfloat16)
    left, right = [], []
    for row in range(count):
        raw = stage[pl.ds(16 * row, 8), :]
        rest = stage[pl.ds(16 * row + 8, 8), :]
        coarse = raw.astype(jnp.bfloat16).astype(F32)
        both = jnp.concatenate([coarse, raw - coarse], axis=0).astype(jnp.bfloat16)
        wide = jnp.broadcast_to(page[row : row + 1], (16, LANES)).astype(jnp.bfloat16)
        tiles = [jnp.where(wide == h, both, none) for h in range(PAGES)]
        tiles.append(jnp.concatenate([rest, jnp.zeros_like(rest)], axis=0).astype(jnp.bfloat16))
        left.append(jnp.concatenate(tiles, axis=0))
        wide = jnp.broadcast_to(lane[row : row + 1], (16, LANES)).astype(jnp.bfloat16)
        wide = jnp.concatenate([wide] * (LANES // 16), axis=0)
        right.append(jnp.where(wide == place, one, none))
    return left, right


def scatter_scratch(count):
    return [pltpu.VMEM((16 * count, LANES), F32), pltpu.VMEM((STACK, LANES), F32)]


def fold(total, out):
    for h in range(PAGES):
        out[pl.ds(h, JAC - 1, stride=PAGES), :] = (
            total[pl.ds(16 * h, 8), :] + total[pl.ds(16 * h + 8, 8), :]
        )
    out[pl.ds(ROWS - PAGES, PAGES), :] = total[64:68, :] + total[68:72, :]


def weave(cams, index):
    half = cams.shape[2]
    for s in range(2):
        for o in range(2):
            index[s, pl.ds(o, half, stride=2), :] = cams[s, o]


def pair_look(cam, point, index, table, seen_out, loose, sends, odd, with_h, squares, held, done):
    rows = cam.shape[2]
    half = rows // 2
    for turn in range(2):
        s = turn ^ odd
        share = part_of(s, held)

        def body(i, carry, s=s, turn=turn, share=share):
            at = pl.ds(pl.multiple_of(i * STEP, STEP), STEP)
            across = [cam[s, j, at, :].astype(F32) for j in range(2 * JAC)]
            along = [point[s, j, at, :].astype(F32) for j in range(6)]
            seen = predict(across, fetch(table, index[s, at, :]))
            for r in range(2):
                seen_out[turn, r, at, :] = seen[r]
            parts = project(along, seen)
            if with_h:
                parts = parts + normal(along)
            for n, part in enumerate(parts):
                loose[n, at, :] = part
            if squares is not None:
                squares[...] += share * (seen[0] * seen[0] + seen[1] * seen[1])
            return carry

        lax.fori_loop(0, rows // STEP, body, 0, unroll=True)
        for n in range(9 if with_h else 3):
            sends[turn][n] = (
                loose[n, pl.ds(0, half, stride=2), :] + loose[n, pl.ds(1, half, stride=2), :]
            )
        if done is not None:
            done(turn)


def part_of(side, held):
    return jnp.where(side == 0, 1, held).astype(F32)


def pair_return(cam, point, index, seen_in, z, odd, held, stage, total):
    rows = cam.shape[2]
    for turn in range(2):
        s = turn ^ odd
        share = part_of(s, held)

        def body(i, carry, s=s, turn=turn, share=share):
            at = pl.ds(pl.multiple_of(i * STEP, STEP), STEP)
            across = [cam[s, j, at, :].astype(F32) for j in range(2 * JAC)]
            along = [point[s, j, at, :].astype(F32) for j in range(6)]
            left = residue(
                along,
                [seen_in[turn, r, at, :] for r in range(2)],
                [z[turn, k, at, :] for k in range(3)],
            )
            left = [share * e for e in left]
            terms = [across[j] * left[0] + across[JAC + j] * left[1] for j in range(JAC)]
            spread(terms, index[s, at, :], stage, total)
            return carry

        lax.fori_loop(0, rows // STEP, body, 0, unroll=True)


def pair_solve(sent, met, inverse_out, inverse_in, z, products, odd, held):
    half = sent[0].shape[1]
    for turn in range(2):
        share = part_of(turn ^ odd, held)
        for i in range(half // 8):
            at = pl.ds(8 * i, 8)
            mine = [sent[turn][k, at, :] for k in range(3)]
            b = [mine[k] + met[turn][k, at, :] for k in range(3)]
            if inverse_in is None:
                inverse = invert(
                    [sent[turn][3 + k, at, :] + met[turn][3 + k, at, :] for k in range(6)]
                )
                for k in range(6):
                    inverse_out[turn, k, at, :] = inverse[k]
            else:
                inverse = [inverse_in[turn, k, at, :] for k in range(6)]
            solved = solve(inverse, b)
            if products is not None:
                products[...] += share * sum(mine[k] * solved[k] for k in range(3))
            for k in range(3):
                for o in range(2):
                    z[turn, k, pl.ds(16 * i + o, 8, stride=2), :] = solved[k]


def place_of():
    seg, strip = lax.axis_index("seg"), lax.axis_index("strip")
    return (seg & 1, jnp.minimum(seg, 1)), (strip & 1, jnp.minimum(strip, 1))


def in_rows(lines, table):
    for j in range(JAC):
        for k in range(PAGES):
            table[pl.ds(PAGES * j + k, 1), :] = lines[j, :, pl.ds(LANES * k, LANES)]


def look_kernel(
    gradient, fcam_at, fpoint_at, fcams_at, scam_at, spoint_at, scams_at,
    fseen_at, fsend0_at, fsend1_at, sseen_at, ssend0_at, ssend1_at,
    lines, fcam, fpoint, fcams, scam, spoint, scams,
    fseen, fsend0, fsend1, sseen, ssend0, ssend1,
    table, findex, sindex, floose, sloose, arrived, left,
):
    (fodd, _), (sodd, _) = place_of()
    moves = [
        pltpu.make_async_copy(source, target, arrived.at[n])
        for n, (source, target) in enumerate(
            (
                (gradient, lines), (scams_at, scams), (scam_at, scam), (spoint_at, spoint),
                (fcams_at, fcams), (fcam_at, fcam), (fpoint_at, fpoint),
            )
        )
    ]
    back = [
        pltpu.make_async_copy(source, target, left.at[n])
        for n, (source, target) in enumerate(
            (
                (ssend0, ssend0_at), (ssend1, ssend1_at), (sseen, sseen_at),
                (fsend0, fsend0_at), (fsend1, fsend1_at), (fseen, fseen_at),
            )
        )
    ]
    for move in moves:
        move.start()
    for move in moves[:2]:
        move.wait()
    in_rows(lines, table)
    weave(scams, sindex)
    for move in moves[2:4]:
        move.wait()

    def sent(first):
        def done(turn):
            back[first + turn].start()
            if turn == 1:
                back[first + 2].start()

        return done

    pair_look(
        scam, spoint, sindex, table, sseen, sloose, (ssend0, ssend1), sodd, True, None, 0, sent(0)
    )
    moves[4].wait()
    weave(fcams, findex)
    for move in moves[5:]:
        move.wait()
    pair_look(
        fcam, fpoint, findex, table, fseen, floose, (fsend0, fsend1), fodd, True, None, 0, sent(3)
    )
    for move in back:
        move.wait()


def local_kernel(live, values, cam, point, cams, out, product, stage, total, table):
    total[...] = jnp.zeros_like(total)
    product[...] = jnp.zeros_like(product)
    if values.shape[0] == JAC:
        in_rows(values, table)
    else:
        table = values
    watched = cams.shape[0] // 16

    def block(i, stage):
        at = pl.ds(pl.multiple_of(i * LANES, LANES), LANES)
        index = cams[pl.ds(i, watched, stride=16), :]
        across = [cam[j, :, at].astype(F32) for j in range(2 * JAC)]
        along = [point[j, :, at].astype(F32) for j in range(6)]
        seen = predict(across, fetch(table, index))
        summed = [jnp.sum(x, axis=0, keepdims=True) for x in project(along, seen) + normal(along)]
        z = solve(invert(summed[3:]), summed[:3])
        share = (i < live[0]).astype(F32)
        left = [share * e for e in residue(along, seen, z)]
        terms = [across[j] * left[0] + across[JAC + j] * left[1] for j in range(JAC)]
        seen = jnp.sum(seen[0] * left[0] + seen[1] * left[1], axis=0, keepdims=True)
        return seen, stacked(terms, index, stage)

    def body(i, carry):
        done = [
            block(LOCAL_GROUP * i + n, stage.at[pl.ds(16 * watched * n, 16 * watched)])
            for n in range(LOCAL_GROUP)
        ]
        product[0:1, :] += sum(seen for seen, _ in done)
        add_in([parts for _, parts in done], total)
        return carry

    lax.fori_loop(0, (live[0] + LOCAL_GROUP - 1) // LOCAL_GROUP, body, 0)
    fold(total, out)


def middle_kernel(
    lines, extra, fcam, fpoint, fcams, scam, spoint, scams,
    fseen, fsent0, fsent1, fmet0, fmet1, sseen, ssent0, ssent1, smet0, smet1,
    result, finverse, sinverse, fseen2, fsend0, fsend1, sseen2, ssend0, ssend1, dots,
    table, findex, sindex, floose, sloose, fz, sz, stage, total, squares,
):
    (fodd, fheld), (sodd, sheld) = place_of()
    in_rows(lines, table)
    weave(fcams, findex)
    weave(scams, sindex)
    total[...] = jnp.zeros_like(total)
    pair_solve((fsent0, fsent1), (fmet0, fmet1), finverse, None, fz, None, fodd, fheld)
    pair_return(fcam, fpoint, findex, fseen, fz, fodd, fheld, stage, total)
    pair_solve((ssent0, ssent1), (smet0, smet1), sinverse, None, sz, None, sodd, sheld)
    pair_return(scam, spoint, sindex, sseen, sz, sodd, sheld, stage, total)
    fold(total, result)
    step = result[...] + extra[...]
    result[...] = step
    squares[...] = jnp.zeros_like(squares)
    sends = (fsend0, fsend1)
    pair_look(
        fcam, fpoint, findex, result, fseen2, floose, sends, fodd, False, squares, fheld, None
    )
    sends = (ssend0, ssend1)
    pair_look(
        scam, spoint, sindex, result, sseen2, sloose, sends, sodd, False, squares, sheld, None
    )
    base = table[...]
    dots[...] = jnp.zeros_like(dots)
    for row, value in enumerate((base * base, base * step, step * step, squares[...])):
        dots[row : row + 1, :] = jnp.sum(value, axis=0, keepdims=True)


def dots_kernel(
    dots, product, fsent0, fsent1, fmet0, fmet1, finverse,
    ssent0, ssent1, smet0, smet1, sinverse, fz, sz, out, products,
):
    (fodd, fheld), (sodd, sheld) = place_of()
    products[...] = jnp.zeros_like(products)
    pair_solve((fsent0, fsent1), (fmet0, fmet1), None, finverse, fz, products, fodd, fheld)
    pair_solve((ssent0, ssent1), (smet0, smet1), None, sinverse, sz, products, sodd, sheld)
    curve = dots[3:4, :] + product[0:1, :] - jnp.sum(products[...], axis=0, keepdims=True)
    rows = jnp.concatenate([dots[0:3, :], curve], axis=0)
    sums = jnp.sum(rows, axis=1, keepdims=True)
    place = lax.broadcasted_iota(jnp.int32, (1, LANES), 1)
    line = jnp.zeros((1, LANES), F32)
    for n in range(4):
        line = line + jnp.where(place == n, sums[n : n + 1, :], 0.0)
    out[...] = jnp.broadcast_to(line, out.shape)


def last_kernel(
    extra, fcam, fpoint, fcams, scam, spoint, scams, fseen, fz, sseen, sz,
    result, findex, sindex, stage, total,
):
    (fodd, fheld), (sodd, sheld) = place_of()
    weave(fcams, findex)
    weave(scams, sindex)
    total[...] = jnp.zeros_like(total)
    pair_return(fcam, fpoint, findex, fseen, fz, fodd, fheld, stage, total)
    pair_return(scam, spoint, sindex, sseen, sz, sodd, sheld, stage, total)
    fold(total, result)
    result[...] += extra[...]


def close_kernel(sums, lines, first, second, step_out, residual_out, base):
    in_rows(lines, base)
    line = jnp.sum(sums[...], axis=0, keepdims=True)
    place = lax.broadcasted_iota(jnp.int32, line.shape, 1)
    rr, bp, pp, curve = [
        jnp.sum(jnp.where(place == n, line, 0.0), axis=1, keepdims=True) for n in range(4)
    ]
    whole = rr + bp
    alpha = rr / whole
    rest = bp / whole
    new = alpha * (alpha * pp - rest * bp)
    gamma = rest + new / rr
    bend = gamma * gamma * rr - 2.0 * gamma * alpha * bp + alpha * alpha * pp
    bend = bend + gamma * gamma * bp - 2.0 * gamma * alpha * pp + alpha * alpha * curve
    again = new / bend
    d0, p, t = base[...], first[...], second[...]
    direction = gamma * d0 - alpha * p
    image = gamma * d0 + (gamma - alpha) * p - alpha * t
    step = -(alpha * d0 + again * direction)
    residual = -(rest * d0 - alpha * p - again * image)
    for j in range(JAC):
        for k in range(PAGES):
            row = PAGES * j + k
            step_out[j, :, pl.ds(LANES * k, LANES)] = step[row : row + 1, :]
            residual_out[j, :, pl.ds(LANES * k, LANES)] = residual[row : row + 1, :]


def call(kernel, ins, outs, scratch, flops, name, place=VMEM, to=VMEM, room=12):
    outs = [jax.ShapeDtypeStruct(shape, F32) for shape in outs]
    specs = [SMEM if i == 0 and x.ndim == 1 else place for i, x in enumerate(ins)]
    return pl.pallas_call(
        kernel,
        out_shape=outs,
        in_specs=specs,
        out_specs=[to] * len(outs),
        scratch_shapes=scratch,
        compiler_params=pltpu.CompilerParams(vmem_limit_bytes=room << 20),
        cost_estimate=pl.CostEstimate(flops=flops, bytes_accessed=2 << 20, transcendentals=0),
        name=name,
    )(*ins)


def rows_of(array):
    kinds, parts, two, _, points = array.shape
    array = array.reshape(kinds, parts, two, points // LANES, LANES)
    return array.transpose(0, 1, 3, 2, 4).reshape(kinds, parts, two * points // LANES, LANES)


def per_device(
    gradient, live_blocks, loc_cam_jac, loc_point_jac, loc_cams,
    fwd_cam_jac, fwd_point_jac, fwd_cams, side_cam_jac, side_point_jac, side_cams,
):
    strips, segs = lax.axis_size("strip"), lax.axis_size("seg")
    cells = [(s, g) for s in range(strips) for g in range(segs)]

    def pairs(move):
        found = []
        for s, g in cells:
            t, h = move(s, g)
            if 0 <= t < strips and 0 <= h < segs:
                found.append((s * segs + g, t * segs + h))
        return found

    fwd_rounds = pairs(lambda s, g: (s, g ^ 1)), pairs(lambda s, g: (s, (g + 1 ^ 1) - 1))
    side_rounds = (
        pairs(lambda s, g: (s ^ 1, segs - 1 - g)),
        pairs(lambda s, g: ((s + 1 ^ 1) - 1, segs - 1 - g)),
    )
    live = live_blocks.reshape(1)
    lcam, lpoint = loc_cam_jac[:, :, 0], loc_point_jac[:, :, 0]
    lcams = loc_cams.reshape(-1, LANES)
    fcam, fpoint = rows_of(fwd_cam_jac), rows_of(fwd_point_jac)
    scam, spoint = rows_of(side_cam_jac), rows_of(side_point_jac)
    fcams = fwd_cams.reshape(2, 2, -1, LANES)
    scams = side_cams.reshape(2, 2, -1, LANES)
    fr, sr = fcam.shape[2], scam.shape[2]
    watched = lcam.shape[1]

    def meet(sends, rounds):
        return [lax.ppermute(send, AXES, pairs) for send, pairs in zip(sends, rounds)]

    index_scratch = [pltpu.VMEM((2, fr, LANES), jnp.int32), pltpu.VMEM((2, sr, LANES), jnp.int32)]
    z_scratch = [pltpu.VMEM((2, 3, fr, LANES), F32), pltpu.VMEM((2, 3, sr, LANES), F32)]
    total_scratch = scatter_scratch(STEP)

    def sends_of(parts):
        return [(parts, fr // 2, LANES)] * 2, [(parts, sr // 2, LANES)] * 2

    far = [gradient, fcam, fpoint, fcams, scam, spoint, scams]
    table = [pltpu.VMEM((ROWS, LANES), F32)]
    fshapes, sshapes = sends_of(9)
    shapes = [(2, 2, fr, LANES)] + fshapes + [(2, 2, sr, LANES)] + sshapes
    fseen, *fsent, sseen, ssent0, ssent1 = call(
        look_kernel,
        far,
        shapes,
        [pltpu.VMEM(x.shape, x.dtype) for x in far]
        + [pltpu.VMEM(shape, F32) for shape in shapes]
        + table
        + index_scratch
        + [pltpu.VMEM((9, fr, LANES), F32), pltpu.VMEM((9, sr, LANES), F32)]
        + [pltpu.SemaphoreType.DMA((len(far),)), pltpu.SemaphoreType.DMA((len(shapes),))],
        10**9,
        "look",
        FAR,
        FAR,
        63,
    )
    ssent = [ssent0, ssent1]
    smet = meet(ssent, side_rounds)
    fmet = meet(fsent, fwd_rounds)

    def local(values):
        return call(
            local_kernel,
            [live, values, lcam, lpoint, lcams],
            [(ROWS, LANES), (8, LANES)],
            scatter_scratch(watched * LOCAL_GROUP) + table,
            5 * 10**9,
            "local",
        )

    extra, _ = local(gradient)
    fshapes, sshapes = sends_of(3)
    p, finverse, sinverse, fseen, fsend0, fsend1, sseen, ssend0, ssend1, dots = call(
        middle_kernel,
        [gradient, extra, fcam, fpoint, fcams, scam, spoint, scams,
         fseen, *fsent, *fmet, sseen, *ssent, *smet],
        [(ROWS, LANES), (2, 6, fr // 2, LANES), (2, 6, sr // 2, LANES), (2, 2, fr, LANES)]
        + fshapes + [(2, 2, sr, LANES)] + sshapes + [(8, LANES)],
        table + index_scratch
        + [pltpu.VMEM((3, fr, LANES), F32), pltpu.VMEM((3, sr, LANES), F32)]
        + z_scratch + total_scratch + [pltpu.VMEM((STEP, LANES), F32)],
        10**10,
        "middle",
    )
    fsent, ssent = [fsend0, fsend1], [ssend0, ssend1]
    smet = meet(ssent, side_rounds)
    fmet = meet(fsent, fwd_rounds)
    extra, product = local(p)
    fz, sz, line = call(
        dots_kernel,
        [dots, product, *fsent, *fmet, finverse, *ssent, *smet, sinverse],
        [(2, 3, fr, LANES), (2, 3, sr, LANES), (strips * segs, LANES)],
        [pltpu.VMEM((8, LANES), F32)],
        10**8,
        "dots",
    )
    line = lax.all_to_all(line, AXES, 0, 0, tiled=True)
    (t,) = call(
        last_kernel,
        [extra, fcam, fpoint, fcams, scam, spoint, scams, fseen, fz, sseen, sz],
        [(ROWS, LANES)],
        index_scratch + total_scratch,
        5 * 10**9,
        "last",
    )
    step, residual = call(
        close_kernel, [line, gradient, p, t], [gradient.shape] * 2, table, 10**6, "close"
    )
    return step, residual


def solution(mesh):
    placed = (
        P(None, "strip", "seg"),
        P("strip", "seg"),
        P(None, None, "strip", "seg"),
        P(None, None, "strip", "seg"),
        P(None, "strip", "seg"),
        P(None, None, None, "strip", "seg"),
        P(None, None, None, "strip", "seg"),
        P(None, None, "strip", "seg"),
        P(None, None, None, "strip", "seg"),
        P(None, None, None, "strip", "seg"),
        P(None, None, "strip", "seg"),
    )
    return jax.shard_map(
        per_device,
        mesh=mesh,
        in_specs=placed,
        out_specs=(P(None, "strip", "seg"), P(None, "strip", "seg")),
        check_vma=False,
    )
```

```python
import functools

import jax
import jax.numpy as jnp
from jax import lax
from jax.experimental import pallas as pl
from jax.experimental.pallas import tpu as pltpu
from jax.sharding import PartitionSpec as P

AXES = ("strip", "seg")
LANES = 128
JAC = 9
PAGES = 4
ROWS = JAC * PAGES
STACK = 80
STEP = 16
LOCAL_GROUP = 8
SYM = ((0, 0), (0, 1), (0, 2), (1, 1), (1, 2), (2, 2))
DAMP = 1.0
VMEM = pl.BlockSpec(memory_space=pltpu.VMEM)
SMEM = pl.BlockSpec(memory_space=pltpu.SMEM)
FAR = pl.BlockSpec(memory_space=pltpu.HBM)
F32 = jnp.float32


def fetch(table, index):
    lane = index & (LANES - 1)
    odd = (index & LANES) != 0
    upper = index >= 2 * LANES
    found = []
    for j in range(JAC):
        page = [
            jnp.take_along_axis(
                jnp.broadcast_to(table[pl.ds(PAGES * j + k, 1), :], index.shape), lane, axis=1
            )
            for k in range(PAGES)
        ]
        low = jnp.where(odd, page[1], page[0])
        high = jnp.where(odd, page[3], page[2])
        found.append(jnp.where(upper, high, low))
    return found


def predict(across, values):
    return [sum(across[JAC * r + j] * values[j] for j in range(JAC)) for r in range(2)]


def project(along, seen):
    return [along[k] * seen[0] + along[3 + k] * seen[1] for k in range(3)]


def normal(along):
    return [along[i] * along[j] + along[3 + i] * along[3 + j] for i, j in SYM]


def invert(h):
    a, b, c, d, e, f = h[0] + DAMP, h[1], h[2], h[3] + DAMP, h[4], h[5] + DAMP
    first = d * f - e * e
    second = c * e - b * f
    third = b * e - c * d
    scale = 1.0 / (a * first + b * second + c * third)
    return [
        m * scale for m in (first, second, third, a * f - c * c, b * c - a * e, a * d - b * b)
    ]


def solve(m, b):
    return [
        m[0] * b[0] + m[1] * b[1] + m[2] * b[2],
        m[1] * b[0] + m[3] * b[1] + m[4] * b[2],
        m[2] * b[0] + m[4] * b[1] + m[5] * b[2],
    ]


def residue(along, seen, z):
    return [seen[r] - sum(along[3 * r + k] * z[k] for k in range(3)) for r in range(2)]


def spread(terms, index, stage, total):
    add_in([stacked(terms, index, stage)], total)


def add_in(parts, total):
    total[...] += lax.dot_general(
        jnp.concatenate([x for left, _ in parts for x in left], axis=1),
        jnp.concatenate([x for _, right in parts for x in right], axis=1),
        (((1,), (1,)), ((), ())),
        preferred_element_type=F32,
    )


def stacked(terms, index, stage):
    count = index.shape[0]
    page = index >> 7
    coarse = terms[JAC - 1].astype(jnp.bfloat16).astype(F32)
    fine = terms[JAC - 1] - coarse
    for j in range(JAC - 1):
        stage[pl.ds(j, count, stride=16), :] = terms[j]
    for h in range(PAGES):
        stage[pl.ds(8 + h, count, stride=16), :] = jnp.where(page == h, coarse, 0.0)
        stage[pl.ds(12 + h, count, stride=16), :] = jnp.where(page == h, fine, 0.0)
    page = page.astype(F32)
    lane = (index & (LANES - 1)).astype(F32)
    place = lax.broadcasted_iota(jnp.int32, (LANES, LANES), 0).astype(F32).astype(jnp.bfloat16)
    one, none = jnp.ones((), jnp.bfloat16), jnp.zeros((), jnp.bfloat16)
    left, right = [], []
    for row in range(count):
        raw = stage[pl.ds(16 * row, 8), :]
        rest = stage[pl.ds(16 * row + 8, 8), :]
        coarse = raw.astype(jnp.bfloat16).astype(F32)
        both = jnp.concatenate([coarse, raw - coarse], axis=0).astype(jnp.bfloat16)
        wide = jnp.broadcast_to(page[row : row + 1], (16, LANES)).astype(jnp.bfloat16)
        tiles = [jnp.where(wide == h, both, none) for h in range(PAGES)]
        tiles.append(jnp.concatenate([rest, jnp.zeros_like(rest)], axis=0).astype(jnp.bfloat16))
        left.append(jnp.concatenate(tiles, axis=0))
        wide = jnp.broadcast_to(lane[row : row + 1], (16, LANES)).astype(jnp.bfloat16)
        wide = jnp.concatenate([wide] * (LANES // 16), axis=0)
        right.append(jnp.where(wide == place, one, none))
    return left, right


def scatter_scratch(count):
    return [pltpu.VMEM((16 * count, LANES), F32), pltpu.VMEM((STACK, LANES), F32)]


def fold(total, out):
    for h in range(PAGES):
        out[pl.ds(h, JAC - 1, stride=PAGES), :] = (
            total[pl.ds(16 * h, 8), :] + total[pl.ds(16 * h + 8, 8), :]
        )
    out[pl.ds(ROWS - PAGES, PAGES), :] = total[64:68, :] + total[68:72, :]


def weave(cams, index):
    half = cams.shape[2]
    for s in range(2):
        for o in range(2):
            index[s, pl.ds(o, half, stride=2), :] = cams[s, o]


def pair_look(cam, point, index, table, seen_out, loose, sends, odd, with_h, squares, held, done):
    rows = cam.shape[2]
    half = rows // 2
    for turn in range(2):
        s = turn ^ odd
        share = part_of(s, held)

        def body(i, carry, s=s, turn=turn, share=share):
            at = pl.ds(pl.multiple_of(i * STEP, STEP), STEP)
            across = [cam[s, j, at, :].astype(F32) for j in range(2 * JAC)]
            along = [point[s, j, at, :].astype(F32) for j in range(6)]
            seen = predict(across, fetch(table, index[s, at, :]))
            for r in range(2):
                seen_out[turn, r, at, :] = seen[r]
            parts = project(along, seen)
            if with_h:
                parts = parts + normal(along)
            for n, part in enumerate(parts):
                loose[n, at, :] = part
            if squares is not None:
                squares[...] += share * (seen[0] * seen[0] + seen[1] * seen[1])
            return carry

        lax.fori_loop(0, rows // STEP, body, 0, unroll=True)
        for n in range(9 if with_h else 3):
            sends[turn][n] = (
                loose[n, pl.ds(0, half, stride=2), :] + loose[n, pl.ds(1, half, stride=2), :]
            )
        if done is not None:
            done(turn)


def part_of(side, held):
    if isinstance(side, int):
        return 1.0 if side == 0 else held.astype(F32)
    return jnp.where(side == 0, 1, held).astype(F32)


def pair_return(cam, point, index, seen_in, z, odd, held, stage, total, turns=(0, 1)):
    rows = cam.shape[2]
    for turn in turns:
        s = turn ^ odd
        share = part_of(s, held)

        def body(i, carry, s=s, turn=turn, share=share):
            at = pl.ds(pl.multiple_of(i * STEP, STEP), STEP)
            across = [cam[s, j, at, :].astype(F32) for j in range(2 * JAC)]
            along = [point[s, j, at, :].astype(F32) for j in range(6)]
            left = residue(
                along,
                [seen_in[turn, r, at, :] for r in range(2)],
                [z[turn, k, at, :] for k in range(3)],
            )
            left = [share * e for e in left]
            terms = [across[j] * left[0] + across[JAC + j] * left[1] for j in range(JAC)]
            spread(terms, index[s, at, :], stage, total)
            return carry

        lax.fori_loop(0, rows // STEP, body, 0, unroll=True)


def pair_solve(sent, met, inverse_out, z):
    half = sent[0].shape[1]
    for turn in range(2):
        for i in range(half // 8):
            at = pl.ds(8 * i, 8)
            joined = [sent[turn][k, at, :] + met[turn][k, at, :] for k in range(9)]
            inverse = invert(joined[3:])
            for k in range(6):
                inverse_out[turn, k, at, :] = inverse[k]
            put_z(z, turn, i, solve(inverse, joined[:3]))


def put_z(z, turn, i, solved):
    for k in range(3):
        for o in range(2):
            z[turn, k, pl.ds(16 * i + o, 8, stride=2), :] = solved[k]


def own_solve(own, met, inverse, z, products, odd):
    for i in range(own.shape[1] // 8):
        at = pl.ds(8 * i, 8)
        b = [own[k, at, :] + met[k, at, :] for k in range(3)]
        solved = solve([inverse[odd, k, at, :] for k in range(6)], b)
        products[...] += sum(b[k] * solved[k] for k in range(3))
        for k in range(3):
            z[k, at, :] = solved[k]


def widened(values, z, turn):
    for i in range(values.shape[1] // 8):
        put_z(z, turn, i, [values[k, pl.ds(8 * i, 8), :] for k in range(3)])


def place_of():
    seg, strip = lax.axis_index("seg"), lax.axis_index("strip")
    return (seg & 1, jnp.minimum(seg, 1)), (strip & 1, jnp.minimum(strip, 1))


def in_rows(lines, table):
    for j in range(JAC):
        for k in range(PAGES):
            table[pl.ds(PAGES * j + k, 1), :] = lines[j, :, pl.ds(LANES * k, LANES)]


def look_kernel(
    gradient, fcam_at, fpoint_at, fcams_at, scam_at, spoint_at, scams_at,
    fseen_at, fsend0_at, fsend1_at, sseen_at, ssend0_at, ssend1_at,
    lines, fcam, fpoint, fcams, scam, spoint, scams,
    fseen, fsend0, fsend1, sseen, ssend0, ssend1,
    table, findex, sindex, floose, sloose, arrived, left,
):
    (fodd, _), (sodd, _) = place_of()
    moves = [
        pltpu.make_async_copy(source, target, arrived.at[n])
        for n, (source, target) in enumerate(
            (
                (gradient, lines), (scams_at, scams), (scam_at, scam), (spoint_at, spoint),
                (fcams_at, fcams), (fcam_at, fcam), (fpoint_at, fpoint),
            )
        )
    ]
    back = [
        pltpu.make_async_copy(source, target, left.at[n])
        for n, (source, target) in enumerate(
            (
                (ssend0, ssend0_at), (ssend1, ssend1_at), (sseen, sseen_at),
                (fsend0, fsend0_at), (fsend1, fsend1_at), (fseen, fseen_at),
            )
        )
    ]
    for move in moves:
        move.start()
    for move in moves[:2]:
        move.wait()
    in_rows(lines, table)
    weave(scams, sindex)
    for move in moves[2:4]:
        move.wait()

    def sent(first):
        def done(turn):
            back[first + turn].start()
            if turn == 1:
                back[first + 2].start()

        return done

    pair_look(
        scam, spoint, sindex, table, sseen, sloose, (ssend0, ssend1), sodd, True, None, 0, sent(0)
    )
    moves[4].wait()
    weave(fcams, findex)
    for move in moves[5:]:
        move.wait()
    pair_look(
        fcam, fpoint, findex, table, fseen, floose, (fsend0, fsend1), fodd, True, None, 0, sent(3)
    )
    for move in back:
        move.wait()


def local_kernel(live, values, cam, point, cams, out, product, stage, total, table):
    total[...] = jnp.zeros_like(total)
    product[...] = jnp.zeros_like(product)
    if values.shape[0] == JAC:
        in_rows(values, table)
    else:
        table = values
    watched = cams.shape[0] // 16

    def block(i, stage):
        at = pl.ds(pl.multiple_of(i * LANES, LANES), LANES)
        index = cams[pl.ds(i, watched, stride=16), :]
        across = [cam[j, :, at].astype(F32) for j in range(2 * JAC)]
        along = [point[j, :, at].astype(F32) for j in range(6)]
        seen = predict(across, fetch(table, index))
        summed = [jnp.sum(x, axis=0, keepdims=True) for x in project(along, seen) + normal(along)]
        z = solve(invert(summed[3:]), summed[:3])
        share = (i < live[0]).astype(F32)
        left = [share * e for e in residue(along, seen, z)]
        terms = [across[j] * left[0] + across[JAC + j] * left[1] for j in range(JAC)]
        seen = jnp.sum(seen[0] * left[0] + seen[1] * left[1], axis=0, keepdims=True)
        return seen, stacked(terms, index, stage)

    def body(i, carry):
        done = [
            block(LOCAL_GROUP * i + n, stage.at[pl.ds(16 * watched * n, 16 * watched)])
            for n in range(LOCAL_GROUP)
        ]
        product[0:1, :] += sum(seen for seen, _ in done)
        add_in([parts for _, parts in done], total)
        return carry

    lax.fori_loop(0, (live[0] + LOCAL_GROUP - 1) // LOCAL_GROUP, body, 0)
    fold(total, out)


def middle_kernel(
    lines, extra, fcam, fpoint, fcams, scam, spoint, scams,
    fseen, fsent0, fsent1, fmet0, fmet1, sseen, ssent0, ssent1, smet0, smet1,
    result, finverse, sinverse, fseen2, fown, fguest, sseen2, sown, sguest, dots,
    table, findex, sindex, floose, sloose, fz, sz, stage, total, squares,
):
    (fodd, fheld), (sodd, sheld) = place_of()
    in_rows(lines, table)
    weave(fcams, findex)
    weave(scams, sindex)
    total[...] = jnp.zeros_like(total)
    pair_solve((fsent0, fsent1), (fmet0, fmet1), finverse, fz)
    pair_return(fcam, fpoint, findex, fseen, fz, fodd, fheld, stage, total)
    pair_solve((ssent0, ssent1), (smet0, smet1), sinverse, sz)
    pair_return(scam, spoint, sindex, sseen, sz, sodd, sheld, stage, total)
    fold(total, result)
    step = result[...] + extra[...]
    result[...] = step
    squares[...] = jnp.zeros_like(squares)
    sides = (fown, fguest)
    pair_look(fcam, fpoint, findex, result, fseen2, floose, sides, 0, False, squares, fheld, None)
    sides = (sown, sguest)
    pair_look(scam, spoint, sindex, result, sseen2, sloose, sides, 0, False, squares, sheld, None)
    base = table[...]
    dots[...] = jnp.zeros_like(dots)
    for row, value in enumerate((base * base, base * step, step * step, squares[...])):
        dots[row : row + 1, :] = jnp.sum(value, axis=0, keepdims=True)


def dots_kernel(
    dots, product, fown, fmet, finverse, sown, smet, sinverse, fz, sz, out, products
):
    (fodd, _), (sodd, _) = place_of()
    products[...] = jnp.zeros_like(products)
    own_solve(fown, fmet, finverse, fz, products, fodd)
    own_solve(sown, smet, sinverse, sz, products, sodd)
    curve = dots[3:4, :] + product[0:1, :] - jnp.sum(products[...], axis=0, keepdims=True)
    rows = jnp.concatenate([dots[0:3, :], curve], axis=0)
    sums = jnp.sum(rows, axis=1, keepdims=True)
    place = lax.broadcasted_iota(jnp.int32, (1, LANES), 1)
    line = jnp.zeros((1, LANES), F32)
    for n in range(4):
        line = line + jnp.where(place == n, sums[n : n + 1, :], 0.0)
    out[...] = jnp.broadcast_to(line, out.shape)


def relay_kernel(line, fz, sz, fout, sout):
    fout[...] = fz[...]
    sout[...] = sz[...]


def last_kernel(
    turn, extra, fcam, fpoint, fcams, scam, spoint, scams, fseen, fvalues, sseen, svalues,
    result, findex, sindex, fz, sz, stage, total,
):
    (_, fheld), (_, sheld) = place_of()
    weave(fcams, findex)
    weave(scams, sindex)
    total[...] = jnp.zeros_like(total)
    widened(fvalues, fz, turn)
    widened(svalues, sz, turn)
    turns = (turn,)
    pair_return(fcam, fpoint, findex, fseen, fz, 0, fheld, stage, total, turns)
    pair_return(scam, spoint, sindex, sseen, sz, 0, sheld, stage, total, turns)
    fold(total, result)
    result[...] += extra[...]


def close_kernel(sums, lines, first, second, step_out, residual_out, base):
    in_rows(lines, base)
    line = jnp.sum(sums[...], axis=0, keepdims=True)
    place = lax.broadcasted_iota(jnp.int32, line.shape, 1)
    rr, bp, pp, curve = [
        jnp.sum(jnp.where(place == n, line, 0.0), axis=1, keepdims=True) for n in range(4)
    ]
    whole = rr + bp
    alpha = rr / whole
    rest = bp / whole
    new = alpha * (alpha * pp - rest * bp)
    gamma = rest + new / rr
    bend = gamma * gamma * rr - 2.0 * gamma * alpha * bp + alpha * alpha * pp
    bend = bend + gamma * gamma * bp - 2.0 * gamma * alpha * pp + alpha * alpha * curve
    again = new / bend
    d0, p, t = base[...], first[...], second[...]
    direction = gamma * d0 - alpha * p
    image = gamma * d0 + (gamma - alpha) * p - alpha * t
    step = -(alpha * d0 + again * direction)
    residual = -(rest * d0 - alpha * p - again * image)
    for j in range(JAC):
        for k in range(PAGES):
            row = PAGES * j + k
            step_out[j, :, pl.ds(LANES * k, LANES)] = step[row : row + 1, :]
            residual_out[j, :, pl.ds(LANES * k, LANES)] = residual[row : row + 1, :]


def call(kernel, ins, outs, scratch, flops, name, place=VMEM, to=VMEM, room=12):
    outs = [jax.ShapeDtypeStruct(shape, F32) for shape in outs]
    specs = [SMEM if i == 0 and x.ndim == 1 else place for i, x in enumerate(ins)]
    return pl.pallas_call(
        kernel,
        out_shape=outs,
        in_specs=specs,
        out_specs=[to] * len(outs),
        scratch_shapes=scratch,
        compiler_params=pltpu.CompilerParams(vmem_limit_bytes=room << 20),
        cost_estimate=pl.CostEstimate(flops=flops, bytes_accessed=2 << 20, transcendentals=0),
        name=name,
    )(*ins)


def rows_of(array):
    kinds, parts, two, _, points = array.shape
    array = array.reshape(kinds, parts, two, points // LANES, LANES)
    return array.transpose(0, 1, 3, 2, 4).reshape(kinds, parts, two * points // LANES, LANES)


def per_device(
    gradient, live_blocks, loc_cam_jac, loc_point_jac, loc_cams,
    fwd_cam_jac, fwd_point_jac, fwd_cams, side_cam_jac, side_point_jac, side_cams,
):
    strips, segs = lax.axis_size("strip"), lax.axis_size("seg")
    cells = [(s, g) for s in range(strips) for g in range(segs)]

    def pairs(move):
        found = []
        for s, g in cells:
            t, h = move(s, g)
            if 0 <= t < strips and 0 <= h < segs:
                found.append((s * segs + g, t * segs + h))
        return found

    fwd_rounds = pairs(lambda s, g: (s, g ^ 1)), pairs(lambda s, g: (s, (g + 1 ^ 1) - 1))
    fwd_down, fwd_up = pairs(lambda s, g: (s, g - 1)), pairs(lambda s, g: (s, g + 1))
    side_down = pairs(lambda s, g: (s - 1, segs - 1 - g))
    side_up = pairs(lambda s, g: (s + 1, segs - 1 - g))
    side_rounds = (
        pairs(lambda s, g: (s ^ 1, segs - 1 - g)),
        pairs(lambda s, g: ((s + 1 ^ 1) - 1, segs - 1 - g)),
    )
    live = live_blocks.reshape(1)
    lcam, lpoint = loc_cam_jac[:, :, 0], loc_point_jac[:, :, 0]
    lcams = loc_cams.reshape(-1, LANES)
    fcam, fpoint = rows_of(fwd_cam_jac), rows_of(fwd_point_jac)
    scam, spoint = rows_of(side_cam_jac), rows_of(side_point_jac)
    fcams = fwd_cams.reshape(2, 2, -1, LANES)
    scams = side_cams.reshape(2, 2, -1, LANES)
    fr, sr = fcam.shape[2], scam.shape[2]
    watched = lcam.shape[1]

    def meet(sends, rounds):
        return [lax.ppermute(send, AXES, pairs) for send, pairs in zip(sends, rounds)]

    index_scratch = [pltpu.VMEM((2, fr, LANES), jnp.int32), pltpu.VMEM((2, sr, LANES), jnp.int32)]
    z_scratch = [pltpu.VMEM((2, 3, fr, LANES), F32), pltpu.VMEM((2, 3, sr, LANES), F32)]
    total_scratch = scatter_scratch(STEP)

    def sends_of(parts):
        return [(parts, fr // 2, LANES)] * 2, [(parts, sr // 2, LANES)] * 2

    far = [gradient, fcam, fpoint, fcams, scam, spoint, scams]
    table = [pltpu.VMEM((ROWS, LANES), F32)]
    fshapes, sshapes = sends_of(9)
    shapes = [(2, 2, fr, LANES)] + fshapes + [(2, 2, sr, LANES)] + sshapes
    fseen, *fsent, sseen, ssent0, ssent1 = call(
        look_kernel,
        far,
        shapes,
        [pltpu.VMEM(x.shape, x.dtype) for x in far]
        + [pltpu.VMEM(shape, F32) for shape in shapes]
        + table
        + index_scratch
        + [pltpu.VMEM((9, fr, LANES), F32), pltpu.VMEM((9, sr, LANES), F32)]
        + [pltpu.SemaphoreType.DMA((len(far),)), pltpu.SemaphoreType.DMA((len(shapes),))],
        10**9,
        "look",
        FAR,
        FAR,
        63,
    )
    ssent = [ssent0, ssent1]
    smet = meet(ssent, side_rounds)
    fmet = meet(fsent, fwd_rounds)

    def local(values):
        return call(
            local_kernel,
            [live, values, lcam, lpoint, lcams],
            [(ROWS, LANES), (8, LANES)],
            scatter_scratch(watched * LOCAL_GROUP) + table,
            5 * 10**9,
            "local",
        )

    extra, _ = local(gradient)
    fshapes, sshapes = sends_of(3)
    p, finverse, sinverse, fseen, fown, fguest, sseen, sown, sguest, dots = call(
        middle_kernel,
        [gradient, extra, fcam, fpoint, fcams, scam, spoint, scams,
         fseen, *fsent, *fmet, sseen, *ssent, *smet],
        [(ROWS, LANES), (2, 6, fr // 2, LANES), (2, 6, sr // 2, LANES), (2, 2, fr, LANES)]
        + fshapes + [(2, 2, sr, LANES)] + sshapes + [(8, LANES)],
        table + index_scratch
        + [pltpu.VMEM((3, fr, LANES), F32), pltpu.VMEM((3, sr, LANES), F32)]
        + z_scratch + total_scratch + [pltpu.VMEM((STEP, LANES), F32)],
        10**10,
        "middle",
    )
    smet = lax.ppermute(sguest, AXES, side_down)
    fmet = lax.ppermute(fguest, AXES, fwd_down)
    extra, product = local(p)
    zshapes = [(3, fr // 2, LANES), (3, sr // 2, LANES)]
    fz, sz, line = call(
        dots_kernel,
        [dots, product, fown, fmet, finverse, sown, smet, sinverse],
        zshapes + [(strips * segs, LANES)],
        [pltpu.VMEM((8, LANES), F32)],
        10**8,
        "dots",
    )
    fsent, ssent = call(relay_kernel, [line, fz, sz], zshapes, [], 10**6, "relay")
    line = lax.all_to_all(line, AXES, 0, 0, tiled=True)
    ssent = lax.ppermute(ssent, AXES, side_up)
    fsent = lax.ppermute(fsent, AXES, fwd_up)

    def last(turn, extra, fvalues, svalues):
        return call(
            functools.partial(last_kernel, turn),
            [extra, fcam, fpoint, fcams, scam, spoint, scams, fseen, fvalues, sseen, svalues],
            [(ROWS, LANES)],
            index_scratch + z_scratch + total_scratch,
            5 * 10**9,
            "last",
        )[0]

    t = last(1, last(0, extra, fz, sz), fsent, ssent)
    step, residual = call(
        close_kernel, [line, gradient, p, t], [gradient.shape] * 2, table, 10**6, "close"
    )
    return step, residual


def solution(mesh):
    placed = (
        P(None, "strip", "seg"),
        P("strip", "seg"),
        P(None, None, "strip", "seg"),
        P(None, None, "strip", "seg"),
        P(None, "strip", "seg"),
        P(None, None, None, "strip", "seg"),
        P(None, None, None, "strip", "seg"),
        P(None, None, "strip", "seg"),
        P(None, None, None, "strip", "seg"),
        P(None, None, None, "strip", "seg"),
        P(None, None, "strip", "seg"),
    )
    return jax.shard_map(
        per_device,
        mesh=mesh,
        in_specs=placed,
        out_specs=(P(None, "strip", "seg"), P(None, "strip", "seg")),
        check_vma=False,
    )
```

```python
import jax
import jax.numpy as jnp
from jax import lax
from jax.experimental import pallas as pl
from jax.experimental.pallas import tpu as pltpu
from jax.sharding import PartitionSpec as P

AXES = ("strip", "seg")
LANES = 128
JAC = 9
PAGES = 4
ROWS = JAC * PAGES
STACK = 80
STEP = 16
LOCAL_GROUP = 8
SYM = ((0, 0), (0, 1), (0, 2), (1, 1), (1, 2), (2, 2))
DAMP = 1.0
VMEM = pl.BlockSpec(memory_space=pltpu.VMEM)
SMEM = pl.BlockSpec(memory_space=pltpu.SMEM)
FAR = pl.BlockSpec(memory_space=pltpu.HBM)
F32 = jnp.float32


def fetch(table, index):
    lane = index & (LANES - 1)
    odd = (index & LANES) != 0
    upper = index >= 2 * LANES
    found = []
    for j in range(JAC):
        page = [
            jnp.take_along_axis(
                jnp.broadcast_to(table[pl.ds(PAGES * j + k, 1), :], index.shape), lane, axis=1
            )
            for k in range(PAGES)
        ]
        low = jnp.where(odd, page[1], page[0])
        high = jnp.where(odd, page[3], page[2])
        found.append(jnp.where(upper, high, low))
    return found


def predict(across, values):
    return [sum(across[JAC * r + j] * values[j] for j in range(JAC)) for r in range(2)]


def project(along, seen):
    return [along[k] * seen[0] + along[3 + k] * seen[1] for k in range(3)]


def normal(along):
    return [along[i] * along[j] + along[3 + i] * along[3 + j] for i, j in SYM]


def invert(h):
    a, b, c, d, e, f = h[0] + DAMP, h[1], h[2], h[3] + DAMP, h[4], h[5] + DAMP
    first = d * f - e * e
    second = c * e - b * f
    third = b * e - c * d
    scale = 1.0 / (a * first + b * second + c * third)
    return [
        m * scale for m in (first, second, third, a * f - c * c, b * c - a * e, a * d - b * b)
    ]


def solve(m, b):
    return [
        m[0] * b[0] + m[1] * b[1] + m[2] * b[2],
        m[1] * b[0] + m[3] * b[1] + m[4] * b[2],
        m[2] * b[0] + m[4] * b[1] + m[5] * b[2],
    ]


def residue(along, seen, z):
    return [seen[r] - sum(along[3 * r + k] * z[k] for k in range(3)) for r in range(2)]


def spread(terms, index, stage, total):
    add_in([stacked(terms, index, stage)], total)


def add_in(parts, total):
    total[...] += lax.dot_general(
        jnp.concatenate([x for left, _ in parts for x in left], axis=1),
        jnp.concatenate([x for _, right in parts for x in right], axis=1),
        (((1,), (1,)), ((), ())),
        preferred_element_type=F32,
    )


def stacked(terms, index, stage):
    count = index.shape[0]
    page = index >> 7
    coarse = terms[JAC - 1].astype(jnp.bfloat16).astype(F32)
    fine = terms[JAC - 1] - coarse
    for j in range(JAC - 1):
        stage[pl.ds(j, count, stride=16), :] = terms[j]
    for h in range(PAGES):
        stage[pl.ds(8 + h, count, stride=16), :] = jnp.where(page == h, coarse, 0.0)
        stage[pl.ds(12 + h, count, stride=16), :] = jnp.where(page == h, fine, 0.0)
    page = page.astype(F32)
    lane = (index & (LANES - 1)).astype(F32)
    place = lax.broadcasted_iota(jnp.int32, (LANES, LANES), 0).astype(F32).astype(jnp.bfloat16)
    one, none = jnp.ones((), jnp.bfloat16), jnp.zeros((), jnp.bfloat16)
    left, right = [], []
    for row in range(count):
        raw = stage[pl.ds(16 * row, 8), :]
        rest = stage[pl.ds(16 * row + 8, 8), :]
        coarse = raw.astype(jnp.bfloat16).astype(F32)
        both = jnp.concatenate([coarse, raw - coarse], axis=0).astype(jnp.bfloat16)
        wide = jnp.broadcast_to(page[row : row + 1], (16, LANES)).astype(jnp.bfloat16)
        tiles = [jnp.where(wide == h, both, none) for h in range(PAGES)]
        tiles.append(jnp.concatenate([rest, jnp.zeros_like(rest)], axis=0).astype(jnp.bfloat16))
        left.append(jnp.concatenate(tiles, axis=0))
        wide = jnp.broadcast_to(lane[row : row + 1], (16, LANES)).astype(jnp.bfloat16)
        wide = jnp.concatenate([wide] * (LANES // 16), axis=0)
        right.append(jnp.where(wide == place, one, none))
    return left, right


def scatter_scratch(count):
    return [pltpu.VMEM((16 * count, LANES), F32), pltpu.VMEM((STACK, LANES), F32)]


def fold(total, out):
    for h in range(PAGES):
        out[pl.ds(h, JAC - 1, stride=PAGES), :] = (
            total[pl.ds(16 * h, 8), :] + total[pl.ds(16 * h + 8, 8), :]
        )
    out[pl.ds(ROWS - PAGES, PAGES), :] = total[64:68, :] + total[68:72, :]


def weave(cams, index):
    half = cams.shape[2]
    for s in range(2):
        for o in range(2):
            index[s, pl.ds(o, half, stride=2), :] = cams[s, o]


def pair_look(cam, point, index, table, seen_out, loose, sends, odd, with_h, squares, held, done):
    rows = cam.shape[2]
    half = rows // 2
    for turn in range(2):
        s = turn ^ odd
        share = part_of(s, held)

        def body(i, carry, s=s, turn=turn, share=share):
            at = pl.ds(pl.multiple_of(i * STEP, STEP), STEP)
            across = [cam[s, j, at, :].astype(F32) for j in range(2 * JAC)]
            along = [point[s, j, at, :].astype(F32) for j in range(6)]
            seen = predict(across, fetch(table, index[s, at, :]))
            for r in range(2):
                seen_out[turn, r, at, :] = seen[r]
            parts = project(along, seen)
            if with_h:
                parts = parts + normal(along)
            for n, part in enumerate(parts):
                loose[n, at, :] = part
            if squares is not None:
                squares[...] += share * (seen[0] * seen[0] + seen[1] * seen[1])
            return carry

        lax.fori_loop(0, rows // STEP, body, 0, unroll=True)
        for n in range(9 if with_h else 3):
            sends[turn][n] = (
                loose[n, pl.ds(0, half, stride=2), :] + loose[n, pl.ds(1, half, stride=2), :]
            )
        if done is not None:
            done(turn)


def part_of(side, held):
    if isinstance(side, int):
        return 1.0 if side == 0 else held.astype(F32)
    return jnp.where(side == 0, 1, held).astype(F32)


def pair_return(cam, point, index, seen_in, z, odd, held, stage, total, turns=(0, 1)):
    rows = cam.shape[2]
    for turn in turns:
        s = turn ^ odd
        share = part_of(s, held)

        def body(i, carry, s=s, turn=turn, share=share):
            at = pl.ds(pl.multiple_of(i * STEP, STEP), STEP)
            across = [cam[s, j, at, :].astype(F32) for j in range(2 * JAC)]
            along = [point[s, j, at, :].astype(F32) for j in range(6)]
            left = residue(
                along,
                [seen_in[turn, r, at, :] for r in range(2)],
                [z[turn, k, at, :] for k in range(3)],
            )
            left = [share * e for e in left]
            terms = [across[j] * left[0] + across[JAC + j] * left[1] for j in range(JAC)]
            spread(terms, index[s, at, :], stage, total)
            return carry

        lax.fori_loop(0, rows // STEP, body, 0, unroll=True)


def pair_solve(sent, met, inverse_out, z):
    half = sent[0].shape[1]
    for turn in range(2):
        for i in range(half // 8):
            at = pl.ds(8 * i, 8)
            joined = [sent[turn][k, at, :] + met[turn][k, at, :] for k in range(9)]
            inverse = invert(joined[3:])
            for k in range(6):
                inverse_out[turn, k, at, :] = inverse[k]
            put_z(z, turn, i, solve(inverse, joined[:3]))


def put_z(z, turn, i, solved):
    for k in range(3):
        for o in range(2):
            z[turn, k, pl.ds(16 * i + o, 8, stride=2), :] = solved[k]


def own_solve(own, met, inverse, z, products, odd):
    for i in range(own.shape[1] // 8):
        at = pl.ds(8 * i, 8)
        b = [own[k, at, :] + met[k, at, :] for k in range(3)]
        solved = solve([inverse[odd, k, at, :] for k in range(6)], b)
        products[...] += sum(b[k] * solved[k] for k in range(3))
        for k in range(3):
            z[k, at, :] = solved[k]


def both_solve(sent, met, inverse, z, products, odd):
    for turn in range(2):
        own = part_of(turn ^ odd, jnp.int32(0))
        for i in range(sent[0].shape[1] // 8):
            at = pl.ds(8 * i, 8)
            b = [sent[turn][k, at, :] + met[turn][k, at, :] for k in range(3)]
            solved = solve([inverse[turn, k, at, :] for k in range(6)], b)
            products[...] += own * sum(b[k] * solved[k] for k in range(3))
            put_z(z, turn, i, solved)


def widened(values, z, turn):
    for i in range(values.shape[1] // 8):
        put_z(z, turn, i, [values[k, pl.ds(8 * i, 8), :] for k in range(3)])


def place_of():
    seg, strip = lax.axis_index("seg"), lax.axis_index("strip")
    return (seg & 1, jnp.minimum(seg, 1)), (strip & 1, jnp.minimum(strip, 1))


def in_rows(lines, table):
    for j in range(JAC):
        for k in range(PAGES):
            table[pl.ds(PAGES * j + k, 1), :] = lines[j, :, pl.ds(LANES * k, LANES)]


def look_kernel(
    gradient, fcam_at, fpoint_at, fcams_at, scam_at, spoint_at, scams_at,
    fseen_at, fsend0_at, fsend1_at, sseen_at, ssend0_at, ssend1_at,
    lines, fcam, fpoint, fcams, scam, spoint, scams,
    fseen, fsend0, fsend1, sseen, ssend0, ssend1,
    table, findex, sindex, floose, sloose, arrived, left,
):
    (fodd, _), (sodd, _) = place_of()
    moves = [
        pltpu.make_async_copy(source, target, arrived.at[n])
        for n, (source, target) in enumerate(
            (
                (gradient, lines), (scams_at, scams), (scam_at, scam), (spoint_at, spoint),
                (fcams_at, fcams), (fcam_at, fcam), (fpoint_at, fpoint),
            )
        )
    ]
    back = [
        pltpu.make_async_copy(source, target, left.at[n])
        for n, (source, target) in enumerate(
            (
                (ssend0, ssend0_at), (ssend1, ssend1_at), (sseen, sseen_at),
                (fsend0, fsend0_at), (fsend1, fsend1_at), (fseen, fseen_at),
            )
        )
    ]
    for move in moves:
        move.start()
    for move in moves[:2]:
        move.wait()
    in_rows(lines, table)
    weave(scams, sindex)
    for move in moves[2:4]:
        move.wait()

    def sent(first):
        def done(turn):
            back[first + turn].start()
            if turn == 1:
                back[first + 2].start()

        return done

    pair_look(
        scam, spoint, sindex, table, sseen, sloose, (ssend0, ssend1), sodd, True, None, 0, sent(0)
    )
    moves[4].wait()
    weave(fcams, findex)
    for move in moves[5:]:
        move.wait()
    pair_look(
        fcam, fpoint, findex, table, fseen, floose, (fsend0, fsend1), fodd, True, None, 0, sent(3)
    )
    for move in back:
        move.wait()


def local_kernel(live, values, cam, point, cams, out, product, stage, total, table):
    total[...] = jnp.zeros_like(total)
    product[...] = jnp.zeros_like(product)
    if values.shape[0] == JAC:
        in_rows(values, table)
    else:
        table = values
    watched = cams.shape[0] // 16

    def block(i, stage):
        at = pl.ds(pl.multiple_of(i * LANES, LANES), LANES)
        index = cams[pl.ds(i, watched, stride=16), :]
        across = [cam[j, :, at].astype(F32) for j in range(2 * JAC)]
        along = [point[j, :, at].astype(F32) for j in range(6)]
        seen = predict(across, fetch(table, index))
        summed = [jnp.sum(x, axis=0, keepdims=True) for x in project(along, seen) + normal(along)]
        z = solve(invert(summed[3:]), summed[:3])
        share = (i < live[0]).astype(F32)
        left = [share * e for e in residue(along, seen, z)]
        terms = [across[j] * left[0] + across[JAC + j] * left[1] for j in range(JAC)]
        seen = jnp.sum(seen[0] * left[0] + seen[1] * left[1], axis=0, keepdims=True)
        return seen, stacked(terms, index, stage)

    def body(i, carry):
        done = [
            block(LOCAL_GROUP * i + n, stage.at[pl.ds(16 * watched * n, 16 * watched)])
            for n in range(LOCAL_GROUP)
        ]
        product[0:1, :] += sum(seen for seen, _ in done)
        add_in([parts for _, parts in done], total)
        return carry

    lax.fori_loop(0, (live[0] + LOCAL_GROUP - 1) // LOCAL_GROUP, body, 0)
    fold(total, out)


def middle_kernel(
    lines, extra, fcam, fpoint, fcams, scam, spoint, scams,
    fseen, fsent0, fsent1, fmet0, fmet1, sseen, ssent0, ssent1, smet0, smet1,
    result, finverse, sinverse, fseen2, fsend0, fsend1, sseen2, sown, sguest, dots,
    table, findex, sindex, floose, sloose, fz, sz, stage, total, squares,
):
    (fodd, fheld), (sodd, sheld) = place_of()
    in_rows(lines, table)
    weave(fcams, findex)
    weave(scams, sindex)
    total[...] = jnp.zeros_like(total)
    pair_solve((fsent0, fsent1), (fmet0, fmet1), finverse, fz)
    pair_return(fcam, fpoint, findex, fseen, fz, fodd, fheld, stage, total)
    pair_solve((ssent0, ssent1), (smet0, smet1), sinverse, sz)
    pair_return(scam, spoint, sindex, sseen, sz, sodd, sheld, stage, total)
    fold(total, result)
    step = result[...] + extra[...]
    result[...] = step
    squares[...] = jnp.zeros_like(squares)
    sends = (fsend0, fsend1)
    pair_look(
        fcam, fpoint, findex, result, fseen2, floose, sends, fodd, False, squares, fheld, None
    )
    sides = (sown, sguest)
    pair_look(scam, spoint, sindex, result, sseen2, sloose, sides, 0, False, squares, sheld, None)
    base = table[...]
    dots[...] = jnp.zeros_like(dots)
    for row, value in enumerate((base * base, base * step, step * step, squares[...])):
        dots[row : row + 1, :] = jnp.sum(value, axis=0, keepdims=True)


def dots_kernel(
    dots, product, fsent0, fsent1, fmet0, fmet1, finverse, sown, smet, sinverse,
    fz, sz, out, products,
):
    (fodd, _), (sodd, _) = place_of()
    products[...] = jnp.zeros_like(products)
    both_solve((fsent0, fsent1), (fmet0, fmet1), finverse, fz, products, fodd)
    own_solve(sown, smet, sinverse, sz, products, sodd)
    curve = dots[3:4, :] + product[0:1, :] - jnp.sum(products[...], axis=0, keepdims=True)
    rows = jnp.concatenate([dots[0:3, :], curve], axis=0)
    sums = jnp.sum(rows, axis=1, keepdims=True)
    place = lax.broadcasted_iota(jnp.int32, (1, LANES), 1)
    line = jnp.zeros((1, LANES), F32)
    for n in range(4):
        line = line + jnp.where(place == n, sums[n : n + 1, :], 0.0)
    out[...] = jnp.broadcast_to(line, out.shape)


def last_kernel(
    extra, fcam, fpoint, fcams, scam, spoint, scams, fseen, fz, sseen, svalues,
    result, findex, sindex, sz, stage, total,
):
    (fodd, fheld), (_, sheld) = place_of()
    weave(fcams, findex)
    weave(scams, sindex)
    total[...] = jnp.zeros_like(total)
    pair_return(fcam, fpoint, findex, fseen, fz, fodd, fheld, stage, total)
    widened(svalues, sz, 0)
    pair_return(scam, spoint, sindex, sseen, sz, 0, sheld, stage, total, (0,))
    fold(total, result)
    result[...] += extra[...]


def guest_kernel(extra, scam, spoint, scams, sseen, svalues, result, sindex, sz, stage, total):
    _, (_, sheld) = place_of()
    weave(scams, sindex)
    total[...] = jnp.zeros_like(total)
    widened(svalues, sz, 1)
    pair_return(scam, spoint, sindex, sseen, sz, 0, sheld, stage, total, (1,))
    fold(total, result)
    result[...] += extra[...]


def close_kernel(sums, lines, first, second, step_out, residual_out, base):
    in_rows(lines, base)
    line = jnp.sum(sums[...], axis=0, keepdims=True)
    place = lax.broadcasted_iota(jnp.int32, line.shape, 1)
    rr, bp, pp, curve = [
        jnp.sum(jnp.where(place == n, line, 0.0), axis=1, keepdims=True) for n in range(4)
    ]
    whole = rr + bp
    alpha = rr / whole
    rest = bp / whole
    new = alpha * (alpha * pp - rest * bp)
    gamma = rest + new / rr
    bend = gamma * gamma * rr - 2.0 * gamma * alpha * bp + alpha * alpha * pp
    bend = bend + gamma * gamma * bp - 2.0 * gamma * alpha * pp + alpha * alpha * curve
    again = new / bend
    d0, p, t = base[...], first[...], second[...]
    direction = gamma * d0 - alpha * p
    image = gamma * d0 + (gamma - alpha) * p - alpha * t
    step = -(alpha * d0 + again * direction)
    residual = -(rest * d0 - alpha * p - again * image)
    for j in range(JAC):
        for k in range(PAGES):
            row = PAGES * j + k
            step_out[j, :, pl.ds(LANES * k, LANES)] = step[row : row + 1, :]
            residual_out[j, :, pl.ds(LANES * k, LANES)] = residual[row : row + 1, :]


def call(kernel, ins, outs, scratch, flops, name, place=VMEM, to=VMEM, room=12):
    outs = [jax.ShapeDtypeStruct(shape, F32) for shape in outs]
    specs = [SMEM if i == 0 and x.ndim == 1 else place for i, x in enumerate(ins)]
    return pl.pallas_call(
        kernel,
        out_shape=outs,
        in_specs=specs,
        out_specs=[to] * len(outs),
        scratch_shapes=scratch,
        compiler_params=pltpu.CompilerParams(vmem_limit_bytes=room << 20),
        cost_estimate=pl.CostEstimate(flops=flops, bytes_accessed=2 << 20, transcendentals=0),
        name=name,
    )(*ins)


def rows_of(array):
    kinds, parts, two, _, points = array.shape
    array = array.reshape(kinds, parts, two, points // LANES, LANES)
    return array.transpose(0, 1, 3, 2, 4).reshape(kinds, parts, two * points // LANES, LANES)


def per_device(
    gradient, live_blocks, loc_cam_jac, loc_point_jac, loc_cams,
    fwd_cam_jac, fwd_point_jac, fwd_cams, side_cam_jac, side_point_jac, side_cams,
):
    strips, segs = lax.axis_size("strip"), lax.axis_size("seg")
    cells = [(s, g) for s in range(strips) for g in range(segs)]

    def pairs(move):
        found = []
        for s, g in cells:
            t, h = move(s, g)
            if 0 <= t < strips and 0 <= h < segs:
                found.append((s * segs + g, t * segs + h))
        return found

    fwd_rounds = pairs(lambda s, g: (s, g ^ 1)), pairs(lambda s, g: (s, (g + 1 ^ 1) - 1))
    side_down = pairs(lambda s, g: (s - 1, segs - 1 - g))
    side_up = pairs(lambda s, g: (s + 1, segs - 1 - g))
    side_rounds = (
        pairs(lambda s, g: (s ^ 1, segs - 1 - g)),
        pairs(lambda s, g: ((s + 1 ^ 1) - 1, segs - 1 - g)),
    )
    live = live_blocks.reshape(1)
    lcam, lpoint = loc_cam_jac[:, :, 0], loc_point_jac[:, :, 0]
    lcams = loc_cams.reshape(-1, LANES)
    fcam, fpoint = rows_of(fwd_cam_jac), rows_of(fwd_point_jac)
    scam, spoint = rows_of(side_cam_jac), rows_of(side_point_jac)
    fcams = fwd_cams.reshape(2, 2, -1, LANES)
    scams = side_cams.reshape(2, 2, -1, LANES)
    fr, sr = fcam.shape[2], scam.shape[2]
    watched = lcam.shape[1]

    def meet(sends, rounds):
        return [lax.ppermute(send, AXES, pairs) for send, pairs in zip(sends, rounds)]

    index_scratch = [pltpu.VMEM((2, fr, LANES), jnp.int32), pltpu.VMEM((2, sr, LANES), jnp.int32)]
    z_scratch = [pltpu.VMEM((2, 3, fr, LANES), F32), pltpu.VMEM((2, 3, sr, LANES), F32)]
    total_scratch = scatter_scratch(STEP)

    def sends_of(parts):
        return [(parts, fr // 2, LANES)] * 2, [(parts, sr // 2, LANES)] * 2

    far = [gradient, fcam, fpoint, fcams, scam, spoint, scams]
    table = [pltpu.VMEM((ROWS, LANES), F32)]
    fshapes, sshapes = sends_of(9)
    shapes = [(2, 2, fr, LANES)] + fshapes + [(2, 2, sr, LANES)] + sshapes
    fseen, *fsent, sseen, ssent0, ssent1 = call(
        look_kernel,
        far,
        shapes,
        [pltpu.VMEM(x.shape, x.dtype) for x in far]
        + [pltpu.VMEM(shape, F32) for shape in shapes]
        + table
        + index_scratch
        + [pltpu.VMEM((9, fr, LANES), F32), pltpu.VMEM((9, sr, LANES), F32)]
        + [pltpu.SemaphoreType.DMA((len(far),)), pltpu.SemaphoreType.DMA((len(shapes),))],
        10**9,
        "look",
        FAR,
        FAR,
        63,
    )
    ssent = [ssent0, ssent1]
    smet = meet(ssent, side_rounds)
    fmet = meet(fsent, fwd_rounds)

    def local(values):
        return call(
            local_kernel,
            [live, values, lcam, lpoint, lcams],
            [(ROWS, LANES), (8, LANES)],
            scatter_scratch(watched * LOCAL_GROUP) + table,
            5 * 10**9,
            "local",
        )

    extra, _ = local(gradient)
    fshapes, sshapes = sends_of(3)
    p, finverse, sinverse, fseen, fsend0, fsend1, sseen, sown, sguest, dots = call(
        middle_kernel,
        [gradient, extra, fcam, fpoint, fcams, scam, spoint, scams,
         fseen, *fsent, *fmet, sseen, *ssent, *smet],
        [(ROWS, LANES), (2, 6, fr // 2, LANES), (2, 6, sr // 2, LANES), (2, 2, fr, LANES)]
        + fshapes + [(2, 2, sr, LANES)] + sshapes + [(8, LANES)],
        table + index_scratch
        + [pltpu.VMEM((3, fr, LANES), F32), pltpu.VMEM((3, sr, LANES), F32)]
        + z_scratch + total_scratch + [pltpu.VMEM((STEP, LANES), F32)],
        10**10,
        "middle",
    )
    smet = lax.ppermute(sguest, AXES, side_down)
    fmet = meet((fsend0, fsend1), fwd_rounds)
    extra, product = local(p)
    fz, sz, line = call(
        dots_kernel,
        [dots, product, fsend0, fsend1, *fmet, finverse, sown, smet, sinverse],
        [(2, 3, fr, LANES), (3, sr // 2, LANES), (strips * segs, LANES)],
        [pltpu.VMEM((8, LANES), F32)],
        10**8,
        "dots",
    )
    line = lax.all_to_all(line, AXES, 0, 0, tiled=True)
    ssent = lax.ppermute(sz, AXES, side_up)
    (t,) = call(
        last_kernel,
        [extra, fcam, fpoint, fcams, scam, spoint, scams, fseen, fz, sseen, sz],
        [(ROWS, LANES)],
        index_scratch + z_scratch[1:] + total_scratch,
        5 * 10**9,
        "last",
    )
    (t,) = call(
        guest_kernel,
        [t, scam, spoint, scams, sseen, ssent],
        [(ROWS, LANES)],
        index_scratch[1:] + z_scratch[1:] + total_scratch,
        2 * 10**9,
        "guest",
    )
    step, residual = call(
        close_kernel, [line, gradient, p, t], [gradient.shape] * 2, table, 10**6, "close"
    )
    return step, residual


def solution(mesh):
    placed = (
        P(None, "strip", "seg"),
        P("strip", "seg"),
        P(None, None, "strip", "seg"),
        P(None, None, "strip", "seg"),
        P(None, "strip", "seg"),
        P(None, None, None, "strip", "seg"),
        P(None, None, None, "strip", "seg"),
        P(None, None, "strip", "seg"),
        P(None, None, None, "strip", "seg"),
        P(None, None, None, "strip", "seg"),
        P(None, None, "strip", "seg"),
    )
    return jax.shard_map(
        per_device,
        mesh=mesh,
        in_specs=placed,
        out_specs=(P(None, "strip", "seg"), P(None, "strip", "seg")),
        check_vma=False,
    )
```

```python
import jax
import jax.numpy as jnp
from jax import lax
from jax.experimental import pallas as pl
from jax.experimental.pallas import tpu as pltpu
from jax.sharding import PartitionSpec as P

AXES = ("strip", "seg")
LANES = 128
JAC = 9
PAGES = 4
ROWS = JAC * PAGES
STACK = 80
STEP = 16
LOCAL_GROUP = 8
SYM = ((0, 0), (0, 1), (0, 2), (1, 1), (1, 2), (2, 2))
DAMP = 1.0
VMEM = pl.BlockSpec(memory_space=pltpu.VMEM)
SMEM = pl.BlockSpec(memory_space=pltpu.SMEM)
FAR = pl.BlockSpec(memory_space=pltpu.HBM)
F32 = jnp.float32


def fetch(table, index):
    lane = index & (LANES - 1)
    odd = (index & LANES) != 0
    upper = index >= 2 * LANES
    found = []
    for j in range(JAC):
        page = [
            jnp.take_along_axis(
                jnp.broadcast_to(table[pl.ds(PAGES * j + k, 1), :], index.shape), lane, axis=1
            )
            for k in range(PAGES)
        ]
        low = jnp.where(odd, page[1], page[0])
        high = jnp.where(odd, page[3], page[2])
        found.append(jnp.where(upper, high, low))
    return found


def predict(across, values):
    return [sum(across[JAC * r + j] * values[j] for j in range(JAC)) for r in range(2)]


def project(along, seen):
    return [along[k] * seen[0] + along[3 + k] * seen[1] for k in range(3)]


def normal(along):
    return [along[i] * along[j] + along[3 + i] * along[3 + j] for i, j in SYM]


def invert(h):
    a, b, c, d, e, f = h[0] + DAMP, h[1], h[2], h[3] + DAMP, h[4], h[5] + DAMP
    first = d * f - e * e
    second = c * e - b * f
    third = b * e - c * d
    scale = 1.0 / (a * first + b * second + c * third)
    return [
        m * scale for m in (first, second, third, a * f - c * c, b * c - a * e, a * d - b * b)
    ]


def solve(m, b):
    return [
        m[0] * b[0] + m[1] * b[1] + m[2] * b[2],
        m[1] * b[0] + m[3] * b[1] + m[4] * b[2],
        m[2] * b[0] + m[4] * b[1] + m[5] * b[2],
    ]


def residue(along, seen, z):
    return [seen[r] - sum(along[3 * r + k] * z[k] for k in range(3)) for r in range(2)]


def spread(terms, index, stage, total):
    add_in([stacked(terms, index, stage)], total)


def add_in(parts, total):
    total[...] += lax.dot_general(
        jnp.concatenate([x for left, _ in parts for x in left], axis=1),
        jnp.concatenate([x for _, right in parts for x in right], axis=1),
        (((1,), (1,)), ((), ())),
        preferred_element_type=F32,
    )


def stacked(terms, index, stage):
    count = index.shape[0]
    page = index >> 7
    coarse = terms[JAC - 1].astype(jnp.bfloat16).astype(F32)
    fine = terms[JAC - 1] - coarse
    for j in range(JAC - 1):
        stage[pl.ds(j, count, stride=16), :] = terms[j]
    for h in range(PAGES):
        stage[pl.ds(8 + h, count, stride=16), :] = jnp.where(page == h, coarse, 0.0)
        stage[pl.ds(12 + h, count, stride=16), :] = jnp.where(page == h, fine, 0.0)
    page = page.astype(F32)
    lane = (index & (LANES - 1)).astype(F32)
    place = lax.broadcasted_iota(jnp.int32, (LANES, LANES), 0).astype(F32).astype(jnp.bfloat16)
    one, none = jnp.ones((), jnp.bfloat16), jnp.zeros((), jnp.bfloat16)
    left, right = [], []
    for row in range(count):
        raw = stage[pl.ds(16 * row, 8), :]
        rest = stage[pl.ds(16 * row + 8, 8), :]
        coarse = raw.astype(jnp.bfloat16).astype(F32)
        both = jnp.concatenate([coarse, raw - coarse], axis=0).astype(jnp.bfloat16)
        wide = jnp.broadcast_to(page[row : row + 1], (16, LANES)).astype(jnp.bfloat16)
        tiles = [jnp.where(wide == h, both, none) for h in range(PAGES)]
        tiles.append(jnp.concatenate([rest, jnp.zeros_like(rest)], axis=0).astype(jnp.bfloat16))
        left.append(jnp.concatenate(tiles, axis=0))
        wide = jnp.broadcast_to(lane[row : row + 1], (16, LANES)).astype(jnp.bfloat16)
        wide = jnp.concatenate([wide] * (LANES // 16), axis=0)
        right.append(jnp.where(wide == place, one, none))
    return left, right


def scatter_scratch(count):
    return [pltpu.VMEM((16 * count, LANES), F32), pltpu.VMEM((STACK, LANES), F32)]


def fold(total, out):
    for h in range(PAGES):
        out[pl.ds(h, JAC - 1, stride=PAGES), :] = (
            total[pl.ds(16 * h, 8), :] + total[pl.ds(16 * h + 8, 8), :]
        )
    out[pl.ds(ROWS - PAGES, PAGES), :] = total[64:68, :] + total[68:72, :]


def weave(cams, index):
    half = cams.shape[2]
    for s in range(2):
        for o in range(2):
            index[s, pl.ds(o, half, stride=2), :] = cams[s, o]


def pair_look(cam, point, index, table, seen_out, loose, sends, odd, with_h, squares, held, done):
    rows = cam.shape[2]
    half = rows // 2
    for turn in range(2):
        s = turn ^ odd
        share = part_of(s, held)

        def body(i, carry, s=s, turn=turn, share=share):
            at = pl.ds(pl.multiple_of(i * STEP, STEP), STEP)
            across = [cam[s, j, at, :].astype(F32) for j in range(2 * JAC)]
            along = [point[s, j, at, :].astype(F32) for j in range(6)]
            seen = predict(across, fetch(table, index[s, at, :]))
            for r in range(2):
                seen_out[turn, r, at, :] = seen[r]
            parts = project(along, seen)
            if with_h:
                parts = parts + normal(along)
            for n, part in enumerate(parts):
                loose[n, at, :] = part
            if squares is not None:
                squares[...] += share * (seen[0] * seen[0] + seen[1] * seen[1])
            return carry

        lax.fori_loop(0, rows // STEP, body, 0, unroll=True)
        for n in range(9 if with_h else 3):
            sends[turn][n] = (
                loose[n, pl.ds(0, half, stride=2), :] + loose[n, pl.ds(1, half, stride=2), :]
            )
        if done is not None:
            done(turn)


def part_of(side, held):
    if isinstance(side, int):
        return 1.0 if side == 0 else held.astype(F32)
    return jnp.where(side == 0, 1, held).astype(F32)


def pair_return(cam, point, index, seen_in, z, odd, held, stage, total, turns=(0, 1)):
    rows = cam.shape[2]
    for turn in turns:
        s = turn ^ odd
        share = part_of(s, held)

        def body(i, carry, s=s, turn=turn, share=share):
            at = pl.ds(pl.multiple_of(i * STEP, STEP), STEP)
            across = [cam[s, j, at, :].astype(F32) for j in range(2 * JAC)]
            along = [point[s, j, at, :].astype(F32) for j in range(6)]
            left = residue(
                along,
                [seen_in[turn, r, at, :] for r in range(2)],
                [z[turn, k, at, :] for k in range(3)],
            )
            left = [share * e for e in left]
            terms = [across[j] * left[0] + across[JAC + j] * left[1] for j in range(JAC)]
            spread(terms, index[s, at, :], stage, total)
            return carry

        lax.fori_loop(0, rows // STEP, body, 0, unroll=True)


def pair_solve(sent, met, inverse_out, z):
    half = sent[0].shape[1]
    for turn in range(2):
        for i in range(half // 8):
            at = pl.ds(8 * i, 8)
            joined = [sent[turn][k, at, :] + met[turn][k, at, :] for k in range(9)]
            inverse = invert(joined[3:])
            for k in range(6):
                inverse_out[turn, k, at, :] = inverse[k]
            put_z(z, turn, i, solve(inverse, joined[:3]))


def put_z(z, turn, i, solved):
    for k in range(3):
        for o in range(2):
            z[turn, k, pl.ds(16 * i + o, 8, stride=2), :] = solved[k]


def own_solve(own, met, inverse, z, products, odd):
    for i in range(own.shape[1] // 8):
        at = pl.ds(8 * i, 8)
        b = [own[k, at, :] + met[k, at, :] for k in range(3)]
        solved = solve([inverse[odd, k, at, :] for k in range(6)], b)
        products[...] += sum(b[k] * solved[k] for k in range(3))
        for k in range(3):
            z[k, at, :] = solved[k]


def both_solve(sent, met, inverse, z, products, odd):
    for turn in range(2):
        own = part_of(turn ^ odd, jnp.int32(0))
        for i in range(sent[0].shape[1] // 8):
            at = pl.ds(8 * i, 8)
            b = [sent[turn][k, at, :] + met[turn][k, at, :] for k in range(3)]
            solved = solve([inverse[turn, k, at, :] for k in range(6)], b)
            products[...] += own * sum(b[k] * solved[k] for k in range(3))
            put_z(z, turn, i, solved)


def widened(values, z, turn):
    for i in range(values.shape[1] // 8):
        put_z(z, turn, i, [values[k, pl.ds(8 * i, 8), :] for k in range(3)])


def place_of():
    seg, strip = lax.axis_index("seg"), lax.axis_index("strip")
    return (seg & 1, jnp.minimum(seg, 1)), (strip & 1, jnp.minimum(strip, 1))


def in_rows(lines, table):
    for j in range(JAC):
        for k in range(PAGES):
            table[pl.ds(PAGES * j + k, 1), :] = lines[j, :, pl.ds(LANES * k, LANES)]


def look_kernel(
    gradient, fcam_at, fpoint_at, fcams_at, scam_at, spoint_at, scams_at,
    fseen_at, fsend0_at, fsend1_at, sseen_at, ssend0_at, ssend1_at,
    lines, fcam, fpoint, fcams, scam, spoint, scams,
    fseen, fsend0, fsend1, sseen, ssend0, ssend1,
    table, findex, sindex, floose, sloose, arrived, left,
):
    (fodd, _), (sodd, _) = place_of()
    moves = [
        pltpu.make_async_copy(source, target, arrived.at[n])
        for n, (source, target) in enumerate(
            (
                (gradient, lines), (scams_at, scams), (scam_at, scam), (spoint_at, spoint),
                (fcams_at, fcams), (fcam_at, fcam), (fpoint_at, fpoint),
            )
        )
    ]
    back = [
        pltpu.make_async_copy(source, target, left.at[n])
        for n, (source, target) in enumerate(
            (
                (ssend0, ssend0_at), (ssend1, ssend1_at), (sseen, sseen_at),
                (fsend0, fsend0_at), (fsend1, fsend1_at), (fseen, fseen_at),
            )
        )
    ]
    for move in moves:
        move.start()
    for move in moves[:2]:
        move.wait()
    in_rows(lines, table)
    weave(scams, sindex)
    for move in moves[2:4]:
        move.wait()

    def sent(first):
        def done(turn):
            back[first + turn].start()
            if turn == 1:
                back[first + 2].start()

        return done

    pair_look(
        scam, spoint, sindex, table, sseen, sloose, (ssend0, ssend1), sodd, True, None, 0, sent(0)
    )
    moves[4].wait()
    weave(fcams, findex)
    for move in moves[5:]:
        move.wait()
    pair_look(
        fcam, fpoint, findex, table, fseen, floose, (fsend0, fsend1), fodd, True, None, 0, sent(3)
    )
    for move in back:
        move.wait()


def local_kernel(live, values, cam, point, cams, out, product, stage, total, table):
    total[...] = jnp.zeros_like(total)
    product[...] = jnp.zeros_like(product)
    if values.shape[0] == JAC:
        in_rows(values, table)
    else:
        table = values
    watched = cams.shape[0] // 16

    def block(i, stage):
        at = pl.ds(pl.multiple_of(i * LANES, LANES), LANES)
        index = cams[pl.ds(i, watched, stride=16), :]
        across = [cam[j, :, at].astype(F32) for j in range(2 * JAC)]
        along = [point[j, :, at].astype(F32) for j in range(6)]
        seen = predict(across, fetch(table, index))
        summed = [jnp.sum(x, axis=0, keepdims=True) for x in project(along, seen) + normal(along)]
        z = solve(invert(summed[3:]), summed[:3])
        share = (i < live[0, 0]).astype(F32)
        left = [share * e for e in residue(along, seen, z)]
        terms = [across[j] * left[0] + across[JAC + j] * left[1] for j in range(JAC)]
        seen = jnp.sum(seen[0] * left[0] + seen[1] * left[1], axis=0, keepdims=True)
        return seen, stacked(terms, index, stage)

    def body(i, carry):
        done = [
            block(LOCAL_GROUP * i + n, stage.at[pl.ds(16 * watched * n, 16 * watched)])
            for n in range(LOCAL_GROUP)
        ]
        product[0:1, :] += sum(seen for seen, _ in done)
        add_in([parts for _, parts in done], total)
        return carry

    lax.fori_loop(0, (live[0, 0] + LOCAL_GROUP - 1) // LOCAL_GROUP, body, 0)
    fold(total, out)


def middle_kernel(
    lines, extra, fcam, fpoint, fcams, scam, spoint, scams,
    fseen, fsent0, fsent1, fmet0, fmet1, sseen, ssent0, ssent1, smet0, smet1,
    result, finverse, sinverse, fseen2, fsend0, fsend1, sseen2, sown, sguest, dots,
    table, findex, sindex, floose, sloose, fz, sz, stage, total, squares,
):
    (fodd, fheld), (sodd, sheld) = place_of()
    in_rows(lines, table)
    weave(fcams, findex)
    weave(scams, sindex)
    total[...] = jnp.zeros_like(total)
    pair_solve((fsent0, fsent1), (fmet0, fmet1), finverse, fz)
    pair_return(fcam, fpoint, findex, fseen, fz, fodd, fheld, stage, total)
    pair_solve((ssent0, ssent1), (smet0, smet1), sinverse, sz)
    pair_return(scam, spoint, sindex, sseen, sz, sodd, sheld, stage, total)
    fold(total, result)
    step = result[...] + extra[...]
    result[...] = step
    squares[...] = jnp.zeros_like(squares)
    sends = (fsend0, fsend1)
    pair_look(
        fcam, fpoint, findex, result, fseen2, floose, sends, fodd, False, squares, fheld, None
    )
    sides = (sown, sguest)
    pair_look(scam, spoint, sindex, result, sseen2, sloose, sides, 0, False, squares, sheld, None)
    base = table[...]
    dots[...] = jnp.zeros_like(dots)
    for row, value in enumerate((base * base, base * step, step * step, squares[...])):
        dots[row : row + 1, :] = jnp.sum(value, axis=0, keepdims=True)


def dots_kernel(
    dots, product, fsent0, fsent1, fmet0, fmet1, finverse, sown, smet, sinverse,
    fz, sz, out, products,
):
    (fodd, _), (sodd, _) = place_of()
    products[...] = jnp.zeros_like(products)
    both_solve((fsent0, fsent1), (fmet0, fmet1), finverse, fz, products, fodd)
    own_solve(sown, smet, sinverse, sz, products, sodd)
    curve = dots[3:4, :] + product[0:1, :] - jnp.sum(products[...], axis=0, keepdims=True)
    rows = jnp.concatenate([dots[0:3, :], curve], axis=0)
    sums = jnp.sum(rows, axis=1, keepdims=True)
    place = lax.broadcasted_iota(jnp.int32, (1, LANES), 1)
    line = jnp.zeros((1, LANES), F32)
    for n in range(4):
        line = line + jnp.where(place == n, sums[n : n + 1, :], 0.0)
    out[...] = jnp.broadcast_to(line, out.shape)


def last_kernel(
    extra, fcam, fpoint, fcams, scam, spoint, scams, fseen, fz, sseen, svalues,
    result, findex, sindex, sz, stage, total,
):
    (fodd, fheld), (_, sheld) = place_of()
    weave(fcams, findex)
    weave(scams, sindex)
    total[...] = jnp.zeros_like(total)
    pair_return(fcam, fpoint, findex, fseen, fz, fodd, fheld, stage, total)
    widened(svalues, sz, 0)
    pair_return(scam, spoint, sindex, sseen, sz, 0, sheld, stage, total, (0,))
    fold(total, result)
    result[...] += extra[...]


def close_kernel(
    extra, scam, spoint, scams, sseen, svalues, sums, lines, first,
    step_out, residual_out, base, second, sindex, sz, stage, total,
):
    _, (_, sheld) = place_of()
    weave(scams, sindex)
    total[...] = jnp.zeros_like(total)
    widened(svalues, sz, 1)
    pair_return(scam, spoint, sindex, sseen, sz, 0, sheld, stage, total, (1,))
    fold(total, second)
    second[...] += extra[...]
    in_rows(lines, base)
    line = jnp.sum(sums[...], axis=0, keepdims=True)
    place = lax.broadcasted_iota(jnp.int32, line.shape, 1)
    rr, bp, pp, curve = [
        jnp.sum(jnp.where(place == n, line, 0.0), axis=1, keepdims=True) for n in range(4)
    ]
    whole = rr + bp
    alpha = rr / whole
    rest = bp / whole
    new = alpha * (alpha * pp - rest * bp)
    gamma = rest + new / rr
    bend = gamma * gamma * rr - 2.0 * gamma * alpha * bp + alpha * alpha * pp
    bend = bend + gamma * gamma * bp - 2.0 * gamma * alpha * pp + alpha * alpha * curve
    again = new / bend
    d0, p, t = base[...], first[...], second[...]
    direction = gamma * d0 - alpha * p
    image = gamma * d0 + (gamma - alpha) * p - alpha * t
    step = -(alpha * d0 + again * direction)
    residual = -(rest * d0 - alpha * p - again * image)
    for j in range(JAC):
        for k in range(PAGES):
            row = PAGES * j + k
            step_out[j, :, pl.ds(LANES * k, LANES)] = step[row : row + 1, :]
            residual_out[j, :, pl.ds(LANES * k, LANES)] = residual[row : row + 1, :]


def call(kernel, ins, outs, scratch, flops, name, place=VMEM, to=VMEM, room=12):
    outs = [jax.ShapeDtypeStruct(shape, F32) for shape in outs]
    specs = [SMEM if x.shape == (1, 1) else place for x in ins]
    return pl.pallas_call(
        kernel,
        out_shape=outs,
        in_specs=specs,
        out_specs=[to] * len(outs),
        scratch_shapes=scratch,
        compiler_params=pltpu.CompilerParams(vmem_limit_bytes=room << 20),
        cost_estimate=pl.CostEstimate(flops=flops, bytes_accessed=2 << 20, transcendentals=0),
        name=name,
    )(*ins)


def rows_of(array):
    kinds, parts, two, _, points = array.shape
    array = array.reshape(kinds, parts, two, points // LANES, LANES)
    return array.transpose(0, 1, 3, 2, 4).reshape(kinds, parts, two * points // LANES, LANES)


def per_device(
    gradient, live_blocks, loc_cam_jac, loc_point_jac, loc_cams,
    fwd_cam_jac, fwd_point_jac, fwd_cams, side_cam_jac, side_point_jac, side_cams,
):
    strips, segs = lax.axis_size("strip"), lax.axis_size("seg")
    cells = [(s, g) for s in range(strips) for g in range(segs)]

    def pairs(move):
        found = []
        for s, g in cells:
            t, h = move(s, g)
            if 0 <= t < strips and 0 <= h < segs:
                found.append((s * segs + g, t * segs + h))
        return found

    fwd_rounds = pairs(lambda s, g: (s, g ^ 1)), pairs(lambda s, g: (s, (g + 1 ^ 1) - 1))
    side_down = pairs(lambda s, g: (s - 1, segs - 1 - g))
    side_up = pairs(lambda s, g: (s + 1, segs - 1 - g))
    side_rounds = (
        pairs(lambda s, g: (s ^ 1, segs - 1 - g)),
        pairs(lambda s, g: ((s + 1 ^ 1) - 1, segs - 1 - g)),
    )
    lcam, lpoint = loc_cam_jac[:, :, 0], loc_point_jac[:, :, 0]
    lcams = loc_cams.reshape(-1, LANES)
    fcam, fpoint = rows_of(fwd_cam_jac), rows_of(fwd_point_jac)
    scam, spoint = rows_of(side_cam_jac), rows_of(side_point_jac)
    fcams = fwd_cams.reshape(2, 2, -1, LANES)
    scams = side_cams.reshape(2, 2, -1, LANES)
    fr, sr = fcam.shape[2], scam.shape[2]
    watched = lcam.shape[1]

    def meet(sends, rounds):
        return [lax.ppermute(send, AXES, pairs) for send, pairs in zip(sends, rounds)]

    index_scratch = [pltpu.VMEM((2, fr, LANES), jnp.int32), pltpu.VMEM((2, sr, LANES), jnp.int32)]
    z_scratch = [pltpu.VMEM((2, 3, fr, LANES), F32), pltpu.VMEM((2, 3, sr, LANES), F32)]
    total_scratch = scatter_scratch(STEP)

    def sends_of(parts):
        return [(parts, fr // 2, LANES)] * 2, [(parts, sr // 2, LANES)] * 2

    far = [gradient, fcam, fpoint, fcams, scam, spoint, scams]
    table = [pltpu.VMEM((ROWS, LANES), F32)]
    fshapes, sshapes = sends_of(9)
    shapes = [(2, 2, fr, LANES)] + fshapes + [(2, 2, sr, LANES)] + sshapes
    fseen, *fsent, sseen, ssent0, ssent1 = call(
        look_kernel,
        far,
        shapes,
        [pltpu.VMEM(x.shape, x.dtype) for x in far]
        + [pltpu.VMEM(shape, F32) for shape in shapes]
        + table
        + index_scratch
        + [pltpu.VMEM((9, fr, LANES), F32), pltpu.VMEM((9, sr, LANES), F32)]
        + [pltpu.SemaphoreType.DMA((len(far),)), pltpu.SemaphoreType.DMA((len(shapes),))],
        10**9,
        "look",
        FAR,
        FAR,
        63,
    )
    ssent = [ssent0, ssent1]
    smet = meet(ssent, side_rounds)
    fmet = meet(fsent, fwd_rounds)

    def local(values):
        return call(
            local_kernel,
            [live_blocks, values, lcam, lpoint, lcams],
            [(ROWS, LANES), (8, LANES)],
            scatter_scratch(watched * LOCAL_GROUP) + table,
            5 * 10**9,
            "local",
        )

    extra, _ = local(gradient)
    fshapes, sshapes = sends_of(3)
    p, finverse, sinverse, fseen, fsend0, fsend1, sseen, sown, sguest, dots = call(
        middle_kernel,
        [gradient, extra, fcam, fpoint, fcams, scam, spoint, scams,
         fseen, *fsent, *fmet, sseen, *ssent, *smet],
        [(ROWS, LANES), (2, 6, fr // 2, LANES), (2, 6, sr // 2, LANES), (2, 2, fr, LANES)]
        + fshapes + [(2, 2, sr, LANES)] + sshapes + [(8, LANES)],
        table + index_scratch
        + [pltpu.VMEM((3, fr, LANES), F32), pltpu.VMEM((3, sr, LANES), F32)]
        + z_scratch + total_scratch + [pltpu.VMEM((STEP, LANES), F32)],
        10**10,
        "middle",
    )
    smet = lax.ppermute(sguest, AXES, side_down)
    fmet = meet((fsend0, fsend1), fwd_rounds)
    extra, product = local(p)
    fz, sz, line = call(
        dots_kernel,
        [dots, product, fsend0, fsend1, *fmet, finverse, sown, smet, sinverse],
        [(2, 3, fr, LANES), (3, sr // 2, LANES), (strips * segs, LANES)],
        [pltpu.VMEM((8, LANES), F32)],
        10**8,
        "dots",
    )
    line = lax.all_to_all(line, AXES, 0, 0, tiled=True)
    ssent = lax.ppermute(sz, AXES, side_up)
    (t,) = call(
        last_kernel,
        [extra, fcam, fpoint, fcams, scam, spoint, scams, fseen, fz, sseen, sz],
        [(ROWS, LANES)],
        index_scratch + z_scratch[1:] + total_scratch,
        5 * 10**9,
        "last",
    )
    step, residual = call(
        close_kernel,
        [t, scam, spoint, scams, sseen, ssent, line, gradient, p],
        [gradient.shape] * 2,
        table * 2 + index_scratch[1:] + z_scratch[1:] + total_scratch,
        2 * 10**9,
        "close",
    )
    return step, residual


def solution(mesh):
    placed = (
        P(None, "strip", "seg"),
        P("strip", "seg"),
        P(None, None, "strip", "seg"),
        P(None, None, "strip", "seg"),
        P(None, "strip", "seg"),
        P(None, None, None, "strip", "seg"),
        P(None, None, None, "strip", "seg"),
        P(None, None, "strip", "seg"),
        P(None, None, None, "strip", "seg"),
        P(None, None, None, "strip", "seg"),
        P(None, None, "strip", "seg"),
    )
    return jax.shard_map(
        per_device,
        mesh=mesh,
        in_specs=placed,
        out_specs=(P(None, "strip", "seg"), P(None, "strip", "seg")),
        check_vma=False,
    )
```

```python
import jax
import jax.numpy as jnp
from jax import lax
from jax.experimental import pallas as pl
from jax.experimental.pallas import tpu as pltpu
from jax.sharding import PartitionSpec as P

AXES = ("strip", "seg")
LANES = 128
JAC = 9
PAGES = 4
ROWS = JAC * PAGES
STACK = 80
STEP = 16
LOCAL_GROUP = 8
SYM = ((0, 0), (0, 1), (0, 2), (1, 1), (1, 2), (2, 2))
DAMP = 1.0
VMEM = pl.BlockSpec(memory_space=pltpu.VMEM)
FAR = pl.BlockSpec(memory_space=pltpu.HBM)
F32 = jnp.float32


def fetch(table, index):
    lane = index & (LANES - 1)
    odd = (index & LANES) != 0
    upper = index >= 2 * LANES
    found = []
    for j in range(JAC):
        page = [
            jnp.take_along_axis(
                jnp.broadcast_to(table[pl.ds(PAGES * j + k, 1), :], index.shape), lane, axis=1
            )
            for k in range(PAGES)
        ]
        low = jnp.where(odd, page[1], page[0])
        high = jnp.where(odd, page[3], page[2])
        found.append(jnp.where(upper, high, low))
    return found


def predict(across, values):
    return [sum(across[JAC * r + j] * values[j] for j in range(JAC)) for r in range(2)]


def project(along, seen):
    return [along[k] * seen[0] + along[3 + k] * seen[1] for k in range(3)]


def normal(along):
    return [along[i] * along[j] + along[3 + i] * along[3 + j] for i, j in SYM]


def invert(h):
    a, b, c, d, e, f = h[0] + DAMP, h[1], h[2], h[3] + DAMP, h[4], h[5] + DAMP
    first = d * f - e * e
    second = c * e - b * f
    third = b * e - c * d
    scale = 1.0 / (a * first + b * second + c * third)
    return [
        m * scale for m in (first, second, third, a * f - c * c, b * c - a * e, a * d - b * b)
    ]


def solve(m, b):
    return [
        m[0] * b[0] + m[1] * b[1] + m[2] * b[2],
        m[1] * b[0] + m[3] * b[1] + m[4] * b[2],
        m[2] * b[0] + m[4] * b[1] + m[5] * b[2],
    ]


def residue(along, seen, z):
    return [seen[r] - sum(along[3 * r + k] * z[k] for k in range(3)) for r in range(2)]


def spread(terms, index, stage, total):
    add_in([stacked(terms, index, stage)], total)


def add_in(parts, total):
    total[...] += lax.dot_general(
        jnp.concatenate([x for left, _ in parts for x in left], axis=1),
        jnp.concatenate([x for _, right in parts for x in right], axis=1),
        (((1,), (1,)), ((), ())),
        preferred_element_type=F32,
    )


def stacked(terms, index, stage):
    count = index.shape[0]
    page = index >> 7
    coarse = terms[JAC - 1].astype(jnp.bfloat16).astype(F32)
    fine = terms[JAC - 1] - coarse
    for j in range(JAC - 1):
        stage[pl.ds(j, count, stride=16), :] = terms[j]
    for h in range(PAGES):
        stage[pl.ds(8 + h, count, stride=16), :] = jnp.where(page == h, coarse, 0.0)
        stage[pl.ds(12 + h, count, stride=16), :] = jnp.where(page == h, fine, 0.0)
    page = page.astype(F32)
    lane = (index & (LANES - 1)).astype(F32)
    place = lax.broadcasted_iota(jnp.int32, (LANES, LANES), 0).astype(F32).astype(jnp.bfloat16)
    one, none = jnp.ones((), jnp.bfloat16), jnp.zeros((), jnp.bfloat16)
    left, right = [], []
    for row in range(count):
        raw = stage[pl.ds(16 * row, 8), :]
        rest = stage[pl.ds(16 * row + 8, 8), :]
        coarse = raw.astype(jnp.bfloat16).astype(F32)
        both = jnp.concatenate([coarse, raw - coarse], axis=0).astype(jnp.bfloat16)
        wide = jnp.broadcast_to(page[row : row + 1], (16, LANES)).astype(jnp.bfloat16)
        tiles = [jnp.where(wide == h, both, none) for h in range(PAGES)]
        tiles.append(jnp.concatenate([rest, jnp.zeros_like(rest)], axis=0).astype(jnp.bfloat16))
        left.append(jnp.concatenate(tiles, axis=0))
        wide = jnp.broadcast_to(lane[row : row + 1], (16, LANES)).astype(jnp.bfloat16)
        wide = jnp.concatenate([wide] * (LANES // 16), axis=0)
        right.append(jnp.where(wide == place, one, none))
    return left, right


def scatter_scratch(count):
    return [pltpu.VMEM((16 * count, LANES), F32), pltpu.VMEM((STACK, LANES), F32)]


def fold(total, out):
    for h in range(PAGES):
        out[pl.ds(h, JAC - 1, stride=PAGES), :] = (
            total[pl.ds(16 * h, 8), :] + total[pl.ds(16 * h + 8, 8), :]
        )
    out[pl.ds(ROWS - PAGES, PAGES), :] = total[64:68, :] + total[68:72, :]


def weave(cams, index):
    half = cams.shape[2]
    for s in range(2):
        for o in range(2):
            index[s, pl.ds(o, half, stride=2), :] = cams[s, o]


def pair_look(cam, point, index, table, seen_out, loose, sends, odd, with_h, squares, held, done):
    rows = cam.shape[2]
    half = rows // 2
    for turn in range(2):
        s = turn ^ odd
        share = part_of(s, held)

        def body(i, carry, s=s, turn=turn, share=share):
            at = pl.ds(pl.multiple_of(i * STEP, STEP), STEP)
            across = [cam[s, j, at, :].astype(F32) for j in range(2 * JAC)]
            along = [point[s, j, at, :].astype(F32) for j in range(6)]
            seen = predict(across, fetch(table, index[s, at, :]))
            for r in range(2):
                seen_out[turn, r, at, :] = seen[r]
            parts = project(along, seen)
            if with_h:
                parts = parts + normal(along)
            for n, part in enumerate(parts):
                loose[n, at, :] = part
            if squares is not None:
                squares[...] += share * (seen[0] * seen[0] + seen[1] * seen[1])
            return carry

        lax.fori_loop(0, rows // STEP, body, 0, unroll=True)
        for n in range(9 if with_h else 3):
            sends[turn][n] = (
                loose[n, pl.ds(0, half, stride=2), :] + loose[n, pl.ds(1, half, stride=2), :]
            )
        if done is not None:
            done(turn)


def part_of(side, held):
    if isinstance(side, int):
        return 1.0 if side == 0 else held.astype(F32)
    return jnp.where(side == 0, 1, held).astype(F32)


def pair_return(cam, point, index, seen_in, z, odd, held, stage, total, turns=(0, 1)):
    rows = cam.shape[2]
    for turn in turns:
        s = turn ^ odd
        share = part_of(s, held)

        def body(i, carry, s=s, turn=turn, share=share):
            at = pl.ds(pl.multiple_of(i * STEP, STEP), STEP)
            across = [cam[s, j, at, :].astype(F32) for j in range(2 * JAC)]
            along = [point[s, j, at, :].astype(F32) for j in range(6)]
            left = residue(
                along,
                [seen_in[turn, r, at, :] for r in range(2)],
                [z[turn, k, at, :] for k in range(3)],
            )
            left = [share * e for e in left]
            terms = [across[j] * left[0] + across[JAC + j] * left[1] for j in range(JAC)]
            spread(terms, index[s, at, :], stage, total)
            return carry

        lax.fori_loop(0, rows // STEP, body, 0, unroll=True)


def pair_solve(sent, met, inverse_out, z):
    half = sent[0].shape[1]
    for turn in range(2):
        for i in range(half // 8):
            at = pl.ds(8 * i, 8)
            joined = [sent[turn][k, at, :] + met[turn][k, at, :] for k in range(9)]
            inverse = invert(joined[3:])
            for k in range(6):
                inverse_out[turn, k, at, :] = inverse[k]
            put_z(z, turn, i, solve(inverse, joined[:3]))


def put_z(z, turn, i, solved):
    for k in range(3):
        for o in range(2):
            z[turn, k, pl.ds(16 * i + o, 8, stride=2), :] = solved[k]


def own_solve(own, met, inverse, z, products, odd):
    for i in range(own.shape[1] // 8):
        at = pl.ds(8 * i, 8)
        b = [own[k, at, :] + met[k, at, :] for k in range(3)]
        solved = solve([inverse[odd, k, at, :] for k in range(6)], b)
        products[...] += sum(b[k] * solved[k] for k in range(3))
        for k in range(3):
            z[k, at, :] = solved[k]


def both_solve(sent, met, inverse, z, products, odd):
    for turn in range(2):
        own = part_of(turn ^ odd, jnp.int32(0))
        for i in range(sent[0].shape[1] // 8):
            at = pl.ds(8 * i, 8)
            b = [sent[turn][k, at, :] + met[turn][k, at, :] for k in range(3)]
            solved = solve([inverse[turn, k, at, :] for k in range(6)], b)
            products[...] += own * sum(b[k] * solved[k] for k in range(3))
            put_z(z, turn, i, solved)


def widened(values, z, turn):
    for i in range(values.shape[1] // 8):
        put_z(z, turn, i, [values[k, pl.ds(8 * i, 8), :] for k in range(3)])


def place_of():
    seg, strip = lax.axis_index("seg"), lax.axis_index("strip")
    return (1 - (seg & 1), jnp.minimum(seg, 1)), (1 - (strip & 1), jnp.minimum(strip, 1))


def in_rows(lines, table):
    for j in range(JAC):
        for k in range(PAGES):
            table[pl.ds(PAGES * j + k, 1), :] = lines[j, :, pl.ds(LANES * k, LANES)]


def look_kernel(
    gradient, fcam_at, fpoint_at, fcams_at, scam_at, spoint_at, scams_at,
    fseen_at, fsend0_at, fsend1_at, sseen_at, ssend0_at, ssend1_at,
    lines, fcam, fpoint, fcams, scam, spoint, scams,
    fseen, fsend0, fsend1, sseen, ssend0, ssend1,
    table, findex, sindex, floose, sloose, arrived, left,
):
    (fodd, _), (sodd, _) = place_of()
    moves = [
        pltpu.make_async_copy(source, target, arrived.at[n])
        for n, (source, target) in enumerate(
            (
                (gradient, lines), (scams_at, scams), (scam_at, scam), (spoint_at, spoint),
                (fcams_at, fcams), (fcam_at, fcam), (fpoint_at, fpoint),
            )
        )
    ]
    back = [
        pltpu.make_async_copy(source, target, left.at[n])
        for n, (source, target) in enumerate(
            (
                (ssend0, ssend0_at), (ssend1, ssend1_at), (sseen, sseen_at),
                (fsend0, fsend0_at), (fsend1, fsend1_at), (fseen, fseen_at),
            )
        )
    ]
    for move in moves:
        move.start()
    for move in moves[:2]:
        move.wait()
    in_rows(lines, table)
    weave(scams, sindex)
    for move in moves[2:4]:
        move.wait()

    def sent(first):
        def done(turn):
            back[first + turn].start()
            if turn == 1:
                back[first + 2].start()

        return done

    pair_look(
        scam, spoint, sindex, table, sseen, sloose, (ssend0, ssend1), sodd, True, None, 0, sent(0)
    )
    moves[4].wait()
    weave(fcams, findex)
    for move in moves[5:]:
        move.wait()
    pair_look(
        fcam, fpoint, findex, table, fseen, floose, (fsend0, fsend1), fodd, True, None, 0, sent(3)
    )
    for move in back:
        move.wait()


def local_kernel(live, values, cam, point, cams, out, product, stage, total, table):
    total[...] = jnp.zeros_like(total)
    product[...] = jnp.zeros_like(product)
    if values.shape[0] == JAC:
        in_rows(values, table)
    else:
        table = values
    watched, blocks = cams.shape[0] // 16, cam.shape[2] // LANES
    lives = jnp.broadcast_to(live[...], (1, LANES))

    def block(i, stage):
        at = pl.ds(pl.multiple_of(i * LANES, LANES), LANES)
        index = cams[pl.ds(i, watched, stride=16), :]
        across = [cam[j, :, at].astype(F32) for j in range(2 * JAC)]
        along = [point[j, :, at].astype(F32) for j in range(6)]
        seen = predict(across, fetch(table, index))
        summed = [jnp.sum(x, axis=0, keepdims=True) for x in project(along, seen) + normal(along)]
        z = solve(invert(summed[3:]), summed[:3])
        share = jnp.where(lives > i, 1.0, 0.0)
        left = [share * e for e in residue(along, seen, z)]
        terms = [across[j] * left[0] + across[JAC + j] * left[1] for j in range(JAC)]
        seen = jnp.sum(seen[0] * left[0] + seen[1] * left[1], axis=0, keepdims=True)
        return seen, stacked(terms, index, stage)

    def body(i, carry):
        done = [
            block(LOCAL_GROUP * i + n, stage.at[pl.ds(16 * watched * n, 16 * watched)])
            for n in range(LOCAL_GROUP)
        ]
        product[0:1, :] += sum(seen for seen, _ in done)
        add_in([parts for _, parts in done], total)
        return carry

    lax.fori_loop(0, blocks // LOCAL_GROUP, body, 0)
    fold(total, out)


def middle_kernel(
    lines, extra, fcam, fpoint, fcams, scam, spoint, scams,
    fseen, fsent0, fsent1, fmet0, fmet1, sseen, ssent0, ssent1, smet0, smet1,
    result, finverse, sinverse, fseen2, fsend0, fsend1, sseen2, sown, sguest, dots,
    table, findex, sindex, floose, sloose, fz, sz, stage, total, squares,
):
    (fodd, fheld), (sodd, sheld) = place_of()
    in_rows(lines, table)
    weave(fcams, findex)
    weave(scams, sindex)
    total[...] = jnp.zeros_like(total)
    pair_solve((fsent0, fsent1), (fmet0, fmet1), finverse, fz)
    pair_return(fcam, fpoint, findex, fseen, fz, fodd, fheld, stage, total)
    pair_solve((ssent0, ssent1), (smet0, smet1), sinverse, sz)
    pair_return(scam, spoint, sindex, sseen, sz, sodd, sheld, stage, total)
    fold(total, result)
    step = result[...] + extra[...]
    result[...] = step
    squares[...] = jnp.zeros_like(squares)
    sends = (fsend0, fsend1)
    pair_look(
        fcam, fpoint, findex, result, fseen2, floose, sends, fodd, False, squares, fheld, None
    )
    sides = (sown, sguest)
    pair_look(scam, spoint, sindex, result, sseen2, sloose, sides, 0, False, squares, sheld, None)
    base = table[...]
    dots[...] = jnp.zeros_like(dots)
    for row, value in enumerate((base * base, base * step, step * step, squares[...])):
        dots[row : row + 1, :] = jnp.sum(value, axis=0, keepdims=True)


def dots_kernel(
    dots, product, fsent0, fsent1, fmet0, fmet1, finverse, sown, smet, sinverse,
    fz, sz, out, products,
):
    (fodd, _), (sodd, _) = place_of()
    products[...] = jnp.zeros_like(products)
    both_solve((fsent0, fsent1), (fmet0, fmet1), finverse, fz, products, fodd)
    own_solve(sown, smet, sinverse, sz, products, sodd)
    curve = dots[3:4, :] + product[0:1, :] - jnp.sum(products[...], axis=0, keepdims=True)
    rows = jnp.concatenate([dots[0:3, :], curve], axis=0)
    sums = jnp.sum(rows, axis=1, keepdims=True)
    place = lax.broadcasted_iota(jnp.int32, (1, LANES), 1)
    line = jnp.zeros((1, LANES), F32)
    for n in range(4):
        line = line + jnp.where(place == n, sums[n : n + 1, :], 0.0)
    out[...] = jnp.broadcast_to(line, out.shape)


def last_kernel(
    extra, fcam, fpoint, fcams, scam, spoint, scams, fseen, fz, sseen, svalues,
    result, findex, sindex, sz, stage, total,
):
    (fodd, fheld), (_, sheld) = place_of()
    weave(fcams, findex)
    weave(scams, sindex)
    total[...] = jnp.zeros_like(total)
    pair_return(fcam, fpoint, findex, fseen, fz, fodd, fheld, stage, total)
    widened(svalues, sz, 0)
    pair_return(scam, spoint, sindex, sseen, sz, 0, sheld, stage, total, (0,))
    fold(total, result)
    result[...] += extra[...]


def close_kernel(
    extra, scam, spoint, scams, sseen, svalues, sums, lines, first,
    step_out, residual_out, base, second, sindex, sz, stage, total,
):
    _, (_, sheld) = place_of()
    weave(scams, sindex)
    total[...] = jnp.zeros_like(total)
    widened(svalues, sz, 1)
    pair_return(scam, spoint, sindex, sseen, sz, 0, sheld, stage, total, (1,))
    fold(total, second)
    second[...] += extra[...]
    in_rows(lines, base)
    line = jnp.sum(sums[...], axis=0, keepdims=True)
    place = lax.broadcasted_iota(jnp.int32, line.shape, 1)
    rr, bp, pp, curve = [
        jnp.sum(jnp.where(place == n, line, 0.0), axis=1, keepdims=True) for n in range(4)
    ]
    whole = rr + bp
    alpha = rr / whole
    rest = bp / whole
    new = alpha * (alpha * pp - rest * bp)
    gamma = rest + new / rr
    bend = gamma * gamma * rr - 2.0 * gamma * alpha * bp + alpha * alpha * pp
    bend = bend + gamma * gamma * bp - 2.0 * gamma * alpha * pp + alpha * alpha * curve
    again = new / bend
    d0, p, t = base[...], first[...], second[...]
    direction = gamma * d0 - alpha * p
    image = gamma * d0 + (gamma - alpha) * p - alpha * t
    step = -(alpha * d0 + again * direction)
    residual = -(rest * d0 - alpha * p - again * image)
    for j in range(JAC):
        for k in range(PAGES):
            row = PAGES * j + k
            step_out[j, :, pl.ds(LANES * k, LANES)] = step[row : row + 1, :]
            residual_out[j, :, pl.ds(LANES * k, LANES)] = residual[row : row + 1, :]


def call(kernel, ins, outs, scratch, flops, name, place=VMEM, to=VMEM, room=12):
    outs = [jax.ShapeDtypeStruct(shape, F32) for shape in outs]
    specs = [place] * len(ins)
    return pl.pallas_call(
        kernel,
        out_shape=outs,
        in_specs=specs,
        out_specs=[to] * len(outs),
        scratch_shapes=scratch,
        compiler_params=pltpu.CompilerParams(vmem_limit_bytes=room << 20),
        cost_estimate=pl.CostEstimate(flops=flops, bytes_accessed=2 << 20, transcendentals=0),
        name=name,
    )(*ins)


def rows_of(array):
    kinds, parts, two, _, points = array.shape
    array = array.reshape(kinds, parts, two, points // LANES, LANES)
    return array.transpose(0, 1, 3, 2, 4).reshape(kinds, parts, two * points // LANES, LANES)


def per_device(
    gradient, live_blocks, loc_cam_jac, loc_point_jac, loc_cams,
    fwd_cam_jac, fwd_point_jac, fwd_cams, side_cam_jac, side_point_jac, side_cams,
):
    strips, segs = lax.axis_size("strip"), lax.axis_size("seg")
    cells = [(s, g) for s in range(strips) for g in range(segs)]

    def pairs(move):
        found = []
        for s, g in cells:
            t, h = move(s, g)
            if 0 <= t < strips and 0 <= h < segs:
                found.append((s * segs + g, t * segs + h))
        return found

    fwd_rounds = pairs(lambda s, g: (s, (g + 1 ^ 1) - 1)), pairs(lambda s, g: (s, g ^ 1))
    side_down = pairs(lambda s, g: (s - 1, segs - 1 - g))
    side_up = pairs(lambda s, g: (s + 1, segs - 1 - g))
    side_rounds = (
        pairs(lambda s, g: ((s + 1 ^ 1) - 1, segs - 1 - g)),
        pairs(lambda s, g: (s ^ 1, segs - 1 - g)),
    )
    lcam, lpoint = loc_cam_jac[:, :, 0], loc_point_jac[:, :, 0]
    lcams = loc_cams.reshape(-1, LANES)
    fcam, fpoint = rows_of(fwd_cam_jac), rows_of(fwd_point_jac)
    scam, spoint = rows_of(side_cam_jac), rows_of(side_point_jac)
    fcams = fwd_cams.reshape(2, 2, -1, LANES)
    scams = side_cams.reshape(2, 2, -1, LANES)
    fr, sr = fcam.shape[2], scam.shape[2]
    watched = lcam.shape[1]

    def meet(sends, rounds):
        return [lax.ppermute(send, AXES, pairs) for send, pairs in zip(sends, rounds)]

    index_scratch = [pltpu.VMEM((2, fr, LANES), jnp.int32), pltpu.VMEM((2, sr, LANES), jnp.int32)]
    z_scratch = [pltpu.VMEM((2, 3, fr, LANES), F32), pltpu.VMEM((2, 3, sr, LANES), F32)]
    total_scratch = scatter_scratch(STEP)

    def sends_of(parts):
        return [(parts, fr // 2, LANES)] * 2, [(parts, sr // 2, LANES)] * 2

    far = [gradient, fcam, fpoint, fcams, scam, spoint, scams]
    table = [pltpu.VMEM((ROWS, LANES), F32)]
    fshapes, sshapes = sends_of(9)
    shapes = [(2, 2, fr, LANES)] + fshapes + [(2, 2, sr, LANES)] + sshapes
    fseen, *fsent, sseen, ssent0, ssent1 = call(
        look_kernel,
        far,
        shapes,
        [pltpu.VMEM(x.shape, x.dtype) for x in far]
        + [pltpu.VMEM(shape, F32) for shape in shapes]
        + table
        + index_scratch
        + [pltpu.VMEM((9, fr, LANES), F32), pltpu.VMEM((9, sr, LANES), F32)]
        + [pltpu.SemaphoreType.DMA((len(far),)), pltpu.SemaphoreType.DMA((len(shapes),))],
        10**9,
        "look",
        FAR,
        FAR,
        63,
    )
    ssent = [ssent0, ssent1]
    smet = meet(ssent, side_rounds)
    fmet = meet(fsent, fwd_rounds)

    def local(values):
        return call(
            local_kernel,
            [live_blocks, values, lcam, lpoint, lcams],
            [(ROWS, LANES), (8, LANES)],
            scatter_scratch(watched * LOCAL_GROUP) + table,
            5 * 10**9,
            "local",
        )

    extra, _ = local(gradient)
    fshapes, sshapes = sends_of(3)
    p, finverse, sinverse, fseen, fsend0, fsend1, sseen, sown, sguest, dots = call(
        middle_kernel,
        [gradient, extra, fcam, fpoint, fcams, scam, spoint, scams,
         fseen, *fsent, *fmet, sseen, *ssent, *smet],
        [(ROWS, LANES), (2, 6, fr // 2, LANES), (2, 6, sr // 2, LANES), (2, 2, fr, LANES)]
        + fshapes + [(2, 2, sr, LANES)] + sshapes + [(8, LANES)],
        table + index_scratch
        + [pltpu.VMEM((3, fr, LANES), F32), pltpu.VMEM((3, sr, LANES), F32)]
        + z_scratch + total_scratch + [pltpu.VMEM((STEP, LANES), F32)],
        10**10,
        "middle",
    )
    smet = lax.ppermute(sguest, AXES, side_down)
    fmet = meet((fsend0, fsend1), fwd_rounds)
    extra, product = local(p)
    fz, sz, line = call(
        dots_kernel,
        [dots, product, fsend0, fsend1, *fmet, finverse, sown, smet, sinverse],
        [(2, 3, fr, LANES), (3, sr // 2, LANES), (strips * segs, LANES)],
        [pltpu.VMEM((8, LANES), F32)],
        10**8,
        "dots",
    )
    line = lax.all_to_all(line, AXES, 0, 0, tiled=True)
    ssent = lax.ppermute(sz, AXES, side_up)
    (t,) = call(
        last_kernel,
        [extra, fcam, fpoint, fcams, scam, spoint, scams, fseen, fz, sseen, sz],
        [(ROWS, LANES)],
        index_scratch + z_scratch[1:] + total_scratch,
        5 * 10**9,
        "last",
    )
    step, residual = call(
        close_kernel,
        [t, scam, spoint, scams, sseen, ssent, line, gradient, p],
        [gradient.shape] * 2,
        table * 2 + index_scratch[1:] + z_scratch[1:] + total_scratch,
        2 * 10**9,
        "close",
    )
    return step, residual


def solution(mesh):
    placed = (
        P(None, "strip", "seg"),
        P("strip", "seg"),
        P(None, None, "strip", "seg"),
        P(None, None, "strip", "seg"),
        P(None, "strip", "seg"),
        P(None, None, None, "strip", "seg"),
        P(None, None, None, "strip", "seg"),
        P(None, None, "strip", "seg"),
        P(None, None, None, "strip", "seg"),
        P(None, None, None, "strip", "seg"),
        P(None, None, "strip", "seg"),
    )
    return jax.shard_map(
        per_device,
        mesh=mesh,
        in_specs=placed,
        out_specs=(P(None, "strip", "seg"), P(None, "strip", "seg")),
        check_vma=False,
    )
```

```python
import jax
import jax.numpy as jnp
from jax import lax
from jax.experimental import pallas as pl
from jax.experimental.pallas import tpu as pltpu
from jax.sharding import PartitionSpec as P

AXES = ("strip", "seg")
LANES = 128
JAC = 9
PAGES = 4
ROWS = JAC * PAGES
STACK = 80
STEP = 16
LOCAL_GROUP = 8
SYM = ((0, 0), (0, 1), (0, 2), (1, 1), (1, 2), (2, 2))
DAMP = 1.0
VMEM = pl.BlockSpec(memory_space=pltpu.VMEM)
FAR = pl.BlockSpec(memory_space=pltpu.HBM)
F32 = jnp.float32


def fetch(table, index):
    lane = index & (LANES - 1)
    odd = (index & LANES) != 0
    upper = index >= 2 * LANES
    found = []
    for j in range(JAC):
        page = [
            jnp.take_along_axis(
                jnp.broadcast_to(table[pl.ds(PAGES * j + k, 1), :], index.shape), lane, axis=1
            )
            for k in range(PAGES)
        ]
        low = jnp.where(odd, page[1], page[0])
        high = jnp.where(odd, page[3], page[2])
        found.append(jnp.where(upper, high, low))
    return found


def predict(across, values):
    return [sum(across[JAC * r + j] * values[j] for j in range(JAC)) for r in range(2)]


def project(along, seen):
    return [along[k] * seen[0] + along[3 + k] * seen[1] for k in range(3)]


def normal(along):
    return [along[i] * along[j] + along[3 + i] * along[3 + j] for i, j in SYM]


def invert(h):
    a, b, c, d, e, f = h[0] + DAMP, h[1], h[2], h[3] + DAMP, h[4], h[5] + DAMP
    first = d * f - e * e
    second = c * e - b * f
    third = b * e - c * d
    scale = 1.0 / (a * first + b * second + c * third)
    return [
        m * scale for m in (first, second, third, a * f - c * c, b * c - a * e, a * d - b * b)
    ]


def solve(m, b):
    return [
        m[0] * b[0] + m[1] * b[1] + m[2] * b[2],
        m[1] * b[0] + m[3] * b[1] + m[4] * b[2],
        m[2] * b[0] + m[4] * b[1] + m[5] * b[2],
    ]


def residue(along, seen, z):
    return [seen[r] - sum(along[3 * r + k] * z[k] for k in range(3)) for r in range(2)]


def mark(row):
    wide = jnp.broadcast_to((row & (LANES - 1)).astype(F32), (16, LANES)).astype(jnp.bfloat16)
    wide = jnp.concatenate([wide] * (LANES // 16), axis=0)
    place = lax.broadcasted_iota(jnp.int32, (LANES, LANES), 0).astype(F32).astype(jnp.bfloat16)
    return jnp.where(wide == place, jnp.ones((), jnp.bfloat16), jnp.zeros((), jnp.bfloat16))


def marks_kernel(fcams, scams, fmarks, smarks):
    for cams, marks in ((fcams, fmarks), (scams, smarks)):
        for s in range(2):
            for o in range(2):

                def body(r, carry, cams=cams, marks=marks, s=s, o=o):
                    marks[s, 2 * r + o] = mark(cams[s, o, pl.ds(r, 1), :])
                    return carry

                lax.fori_loop(0, cams.shape[2], body, 0, unroll=8)


def add_in(parts, total):
    total[...] += lax.dot_general(
        jnp.concatenate([x for left, _ in parts for x in left], axis=1),
        jnp.concatenate([x for _, right in parts for x in right], axis=1),
        (((1,), (1,)), ((), ())),
        preferred_element_type=F32,
    )


def stacked(terms, index, stage, marked=None):
    count = index.shape[0]
    page = index >> 7
    coarse = terms[JAC - 1].astype(jnp.bfloat16).astype(F32)
    fine = terms[JAC - 1] - coarse
    for j in range(JAC - 1):
        stage[pl.ds(j, count, stride=16), :] = terms[j]
    for h in range(PAGES):
        stage[pl.ds(8 + h, count, stride=16), :] = jnp.where(page == h, coarse, 0.0)
        stage[pl.ds(12 + h, count, stride=16), :] = jnp.where(page == h, fine, 0.0)
    page = page.astype(F32)
    none = jnp.zeros((), jnp.bfloat16)
    left, right = [], []
    for row in range(count):
        raw = stage[pl.ds(16 * row, 8), :]
        rest = stage[pl.ds(16 * row + 8, 8), :]
        coarse = raw.astype(jnp.bfloat16).astype(F32)
        both = jnp.concatenate([coarse, raw - coarse], axis=0).astype(jnp.bfloat16)
        wide = jnp.broadcast_to(page[row : row + 1], (16, LANES)).astype(jnp.bfloat16)
        tiles = [jnp.where(wide == h, both, none) for h in range(PAGES)]
        tiles.append(jnp.concatenate([rest, jnp.zeros_like(rest)], axis=0).astype(jnp.bfloat16))
        left.append(jnp.concatenate(tiles, axis=0))
        right.append(mark(index[row : row + 1]) if marked is None else marked(row))
    return left, right


def scatter_scratch(count):
    return [pltpu.VMEM((16 * count, LANES), F32), pltpu.VMEM((STACK, LANES), F32)]


def fold(total, out):
    for h in range(PAGES):
        out[pl.ds(h, JAC - 1, stride=PAGES), :] = (
            total[pl.ds(16 * h, 8), :] + total[pl.ds(16 * h + 8, 8), :]
        )
    out[pl.ds(ROWS - PAGES, PAGES), :] = total[64:68, :] + total[68:72, :]


def weave(cams, index):
    half = cams.shape[2]
    for s in range(2):
        for o in range(2):
            index[s, pl.ds(o, half, stride=2), :] = cams[s, o]


def pair_look(cam, point, index, table, seen_out, loose, sends, odd, with_h, squares, held, done):
    rows = cam.shape[2]
    half = rows // 2
    for turn in range(2):
        s = turn ^ odd
        share = part_of(s, held)

        def body(i, carry, s=s, turn=turn, share=share):
            at = pl.ds(pl.multiple_of(i * STEP, STEP), STEP)
            across = [cam[s, j, at, :].astype(F32) for j in range(2 * JAC)]
            along = [point[s, j, at, :].astype(F32) for j in range(6)]
            seen = predict(across, fetch(table, index[s, at, :]))
            for r in range(2):
                seen_out[turn, r, at, :] = seen[r]
            parts = project(along, seen)
            if with_h:
                parts = parts + normal(along)
            for n, part in enumerate(parts):
                loose[n, at, :] = part
            if squares is not None:
                squares[...] += share * (seen[0] * seen[0] + seen[1] * seen[1])
            return carry

        lax.fori_loop(0, rows // STEP, body, 0, unroll=True)
        for n in range(9 if with_h else 3):
            sends[turn][n] = (
                loose[n, pl.ds(0, half, stride=2), :] + loose[n, pl.ds(1, half, stride=2), :]
            )
        if done is not None:
            done(turn)


def part_of(side, held):
    if isinstance(side, int):
        return 1.0 if side == 0 else held.astype(F32)
    return jnp.where(side == 0, 1, held).astype(F32)


def pair_return(
    cam, point, index, marks, seen_in, z, odd, held, stage, total, turns=(0, 1)
):
    rows = cam.shape[2]
    for turn in turns:
        s = turn ^ odd
        share = part_of(s, held)

        def body(i, carry, s=s, turn=turn, share=share):
            at = pl.ds(pl.multiple_of(i * STEP, STEP), STEP)
            across = [cam[s, j, at, :].astype(F32) for j in range(2 * JAC)]
            along = [point[s, j, at, :].astype(F32) for j in range(6)]
            left = residue(
                along,
                [seen_in[turn, r, at, :] for r in range(2)],
                [z[turn, k, at, :] for k in range(3)],
            )
            left = [share * e for e in left]
            terms = [across[j] * left[0] + across[JAC + j] * left[1] for j in range(JAC)]

            def marked(row):
                return marks[s, i * STEP + row]

            add_in([stacked(terms, index[s, at, :], stage, marked)], total)
            return carry

        lax.fori_loop(0, rows // STEP, body, 0, unroll=True)


def pair_solve(sent, met, inverse_out, z):
    half = sent[0].shape[1]
    for turn in range(2):
        for i in range(half // 8):
            at = pl.ds(8 * i, 8)
            joined = [sent[turn][k, at, :] + met[turn][k, at, :] for k in range(9)]
            inverse = invert(joined[3:])
            for k in range(6):
                inverse_out[turn, k, at, :] = inverse[k]
            put_z(z, turn, i, solve(inverse, joined[:3]))


def put_z(z, turn, i, solved):
    for k in range(3):
        for o in range(2):
            z[turn, k, pl.ds(16 * i + o, 8, stride=2), :] = solved[k]


def own_solve(own, met, inverse, z, products, odd):
    for i in range(own.shape[1] // 8):
        at = pl.ds(8 * i, 8)
        b = [own[k, at, :] + met[k, at, :] for k in range(3)]
        solved = solve([inverse[odd, k, at, :] for k in range(6)], b)
        products[...] += sum(b[k] * solved[k] for k in range(3))
        for k in range(3):
            z[k, at, :] = solved[k]


def both_solve(sent, met, inverse, z, products, odd):
    for turn in range(2):
        own = part_of(turn ^ odd, jnp.int32(0))
        for i in range(sent[0].shape[1] // 8):
            at = pl.ds(8 * i, 8)
            b = [sent[turn][k, at, :] + met[turn][k, at, :] for k in range(3)]
            solved = solve([inverse[turn, k, at, :] for k in range(6)], b)
            products[...] += own * sum(b[k] * solved[k] for k in range(3))
            put_z(z, turn, i, solved)


def widened(values, z, turn):
    for i in range(values.shape[1] // 8):
        put_z(z, turn, i, [values[k, pl.ds(8 * i, 8), :] for k in range(3)])


def place_of():
    seg, strip = lax.axis_index("seg"), lax.axis_index("strip")
    return (1 - (seg & 1), jnp.minimum(seg, 1)), (1 - (strip & 1), jnp.minimum(strip, 1))


def in_rows(lines, table):
    for j in range(JAC):
        for k in range(PAGES):
            table[pl.ds(PAGES * j + k, 1), :] = lines[j, :, pl.ds(LANES * k, LANES)]


def look_kernel(
    gradient, fcam_at, fpoint_at, fcams_at, scam_at, spoint_at, scams_at,
    fseen_at, fsend0_at, fsend1_at, sseen_at, ssend0_at, ssend1_at,
    lines, fcam, fpoint, fcams, scam, spoint, scams,
    fseen, fsend0, fsend1, sseen, ssend0, ssend1,
    table, findex, sindex, floose, sloose, arrived, left,
):
    (fodd, _), (sodd, _) = place_of()
    moves = [
        pltpu.make_async_copy(source, target, arrived.at[n])
        for n, (source, target) in enumerate(
            (
                (gradient, lines), (scams_at, scams), (scam_at, scam), (spoint_at, spoint),
                (fcams_at, fcams), (fcam_at, fcam), (fpoint_at, fpoint),
            )
        )
    ]
    back = [
        pltpu.make_async_copy(source, target, left.at[n])
        for n, (source, target) in enumerate(
            (
                (ssend0, ssend0_at), (ssend1, ssend1_at), (sseen, sseen_at),
                (fsend0, fsend0_at), (fsend1, fsend1_at), (fseen, fseen_at),
            )
        )
    ]
    for move in moves:
        move.start()
    for move in moves[:2]:
        move.wait()
    in_rows(lines, table)
    weave(scams, sindex)
    for move in moves[2:4]:
        move.wait()

    def sent(first):
        def done(turn):
            back[first + turn].start()
            if turn == 1:
                back[first + 2].start()

        return done

    pair_look(
        scam, spoint, sindex, table, sseen, sloose, (ssend0, ssend1), sodd, True, None, 0, sent(0)
    )
    moves[4].wait()
    weave(fcams, findex)
    for move in moves[5:]:
        move.wait()
    pair_look(
        fcam, fpoint, findex, table, fseen, floose, (fsend0, fsend1), fodd, True, None, 0, sent(3)
    )
    for move in back:
        move.wait()


def local_kernel(live, values, cam, point, cams, out, product, stage, total, table):
    total[...] = jnp.zeros_like(total)
    product[...] = jnp.zeros_like(product)
    if values.shape[0] == JAC:
        in_rows(values, table)
    else:
        table = values
    watched, blocks = cams.shape[0] // 16, cam.shape[2] // LANES
    lives = jnp.broadcast_to(live[...], (1, LANES))

    def block(i, stage):
        at = pl.ds(pl.multiple_of(i * LANES, LANES), LANES)
        index = cams[pl.ds(i, watched, stride=16), :]
        across = [cam[j, :, at].astype(F32) for j in range(2 * JAC)]
        along = [point[j, :, at].astype(F32) for j in range(6)]
        seen = predict(across, fetch(table, index))
        summed = [jnp.sum(x, axis=0, keepdims=True) for x in project(along, seen) + normal(along)]
        z = solve(invert(summed[3:]), summed[:3])
        share = jnp.where(lives > i, 1.0, 0.0)
        left = [share * e for e in residue(along, seen, z)]
        terms = [across[j] * left[0] + across[JAC + j] * left[1] for j in range(JAC)]
        seen = jnp.sum(seen[0] * left[0] + seen[1] * left[1], axis=0, keepdims=True)
        return seen, stacked(terms, index, stage)

    def body(i, carry):
        done = [
            block(LOCAL_GROUP * i + n, stage.at[pl.ds(16 * watched * n, 16 * watched)])
            for n in range(LOCAL_GROUP)
        ]
        product[0:1, :] += sum(seen for seen, _ in done)
        add_in([parts for _, parts in done], total)
        return carry

    lax.fori_loop(0, blocks // LOCAL_GROUP, body, 0)
    fold(total, out)


def middle_kernel(
    lines, extra, fcam, fpoint, fcams, scam, spoint, scams, fmarks, smarks,
    fseen, fsent0, fsent1, fmet0, fmet1, sseen, ssent0, ssent1, smet0, smet1,
    result, finverse, sinverse, fseen2, fsend0, fsend1, sseen2, sown, sguest, dots,
    table, findex, sindex, floose, sloose, fz, sz, stage, total, squares,
):
    (fodd, fheld), (sodd, sheld) = place_of()
    in_rows(lines, table)
    weave(fcams, findex)
    weave(scams, sindex)
    total[...] = jnp.zeros_like(total)
    pair_solve((fsent0, fsent1), (fmet0, fmet1), finverse, fz)
    pair_return(fcam, fpoint, findex, fmarks, fseen, fz, fodd, fheld, stage, total)
    pair_solve((ssent0, ssent1), (smet0, smet1), sinverse, sz)
    pair_return(scam, spoint, sindex, smarks, sseen, sz, sodd, sheld, stage, total)
    fold(total, result)
    step = result[...] + extra[...]
    result[...] = step
    squares[...] = jnp.zeros_like(squares)
    sends = (fsend0, fsend1)
    pair_look(
        fcam, fpoint, findex, result, fseen2, floose, sends, fodd, False, squares, fheld, None
    )
    sides = (sown, sguest)
    pair_look(scam, spoint, sindex, result, sseen2, sloose, sides, 0, False, squares, sheld, None)
    base = table[...]
    dots[...] = jnp.zeros_like(dots)
    for row, value in enumerate((base * base, base * step, step * step, squares[...])):
        dots[row : row + 1, :] = jnp.sum(value, axis=0, keepdims=True)


def dots_kernel(
    dots, product, fsent0, fsent1, fmet0, fmet1, finverse, sown, smet, sinverse,
    fz, sz, out, products,
):
    (fodd, _), (sodd, _) = place_of()
    products[...] = jnp.zeros_like(products)
    both_solve((fsent0, fsent1), (fmet0, fmet1), finverse, fz, products, fodd)
    own_solve(sown, smet, sinverse, sz, products, sodd)
    curve = dots[3:4, :] + product[0:1, :] - jnp.sum(products[...], axis=0, keepdims=True)
    rows = jnp.concatenate([dots[0:3, :], curve], axis=0)
    sums = jnp.sum(rows, axis=1, keepdims=True)
    place = lax.broadcasted_iota(jnp.int32, (1, LANES), 1)
    line = jnp.zeros((1, LANES), F32)
    for n in range(4):
        line = line + jnp.where(place == n, sums[n : n + 1, :], 0.0)
    out[...] = jnp.broadcast_to(line, out.shape)


def last_kernel(
    extra, fcam, fpoint, fcams, scam, spoint, scams, fmarks, smarks, fseen, fz, sseen, svalues,
    result, findex, sindex, sz, stage, total,
):
    (fodd, fheld), (_, sheld) = place_of()
    weave(fcams, findex)
    weave(scams, sindex)
    total[...] = jnp.zeros_like(total)
    pair_return(fcam, fpoint, findex, fmarks, fseen, fz, fodd, fheld, stage, total)
    widened(svalues, sz, 0)
    pair_return(scam, spoint, sindex, smarks, sseen, sz, 0, sheld, stage, total, (0,))
    fold(total, result)
    result[...] += extra[...]


def close_kernel(
    extra, scam, spoint, scams, smarks, sseen, svalues, sums, lines, first,
    step_out, residual_out, base, second, sindex, sz, stage, total,
):
    _, (_, sheld) = place_of()
    weave(scams, sindex)
    total[...] = jnp.zeros_like(total)
    widened(svalues, sz, 1)
    pair_return(scam, spoint, sindex, smarks, sseen, sz, 0, sheld, stage, total, (1,))
    fold(total, second)
    second[...] += extra[...]
    in_rows(lines, base)
    line = jnp.sum(sums[...], axis=0, keepdims=True)
    place = lax.broadcasted_iota(jnp.int32, line.shape, 1)
    rr, bp, pp, curve = [
        jnp.sum(jnp.where(place == n, line, 0.0), axis=1, keepdims=True) for n in range(4)
    ]
    whole = rr + bp
    alpha = rr / whole
    rest = bp / whole
    new = alpha * (alpha * pp - rest * bp)
    gamma = rest + new / rr
    bend = gamma * gamma * rr - 2.0 * gamma * alpha * bp + alpha * alpha * pp
    bend = bend + gamma * gamma * bp - 2.0 * gamma * alpha * pp + alpha * alpha * curve
    again = new / bend
    d0, p, t = base[...], first[...], second[...]
    direction = gamma * d0 - alpha * p
    image = gamma * d0 + (gamma - alpha) * p - alpha * t
    step = -(alpha * d0 + again * direction)
    residual = -(rest * d0 - alpha * p - again * image)
    for j in range(JAC):
        for k in range(PAGES):
            row = PAGES * j + k
            step_out[j, :, pl.ds(LANES * k, LANES)] = step[row : row + 1, :]
            residual_out[j, :, pl.ds(LANES * k, LANES)] = residual[row : row + 1, :]


def call(kernel, ins, outs, scratch, flops, name, place=VMEM, to=VMEM, room=12, kind=F32):
    outs = [jax.ShapeDtypeStruct(shape, kind) for shape in outs]
    specs = [place] * len(ins)
    return pl.pallas_call(
        kernel,
        out_shape=outs,
        in_specs=specs,
        out_specs=[to] * len(outs),
        scratch_shapes=scratch,
        compiler_params=pltpu.CompilerParams(vmem_limit_bytes=room << 20),
        cost_estimate=pl.CostEstimate(flops=flops, bytes_accessed=2 << 20, transcendentals=0),
        name=name,
    )(*ins)


def rows_of(array):
    kinds, parts, two, _, points = array.shape
    array = array.reshape(kinds, parts, two, points // LANES, LANES)
    return array.transpose(0, 1, 3, 2, 4).reshape(kinds, parts, two * points // LANES, LANES)


def per_device(
    gradient, live_blocks, loc_cam_jac, loc_point_jac, loc_cams,
    fwd_cam_jac, fwd_point_jac, fwd_cams, side_cam_jac, side_point_jac, side_cams,
):
    strips, segs = lax.axis_size("strip"), lax.axis_size("seg")
    cells = [(s, g) for s in range(strips) for g in range(segs)]

    def pairs(move):
        found = []
        for s, g in cells:
            t, h = move(s, g)
            if 0 <= t < strips and 0 <= h < segs:
                found.append((s * segs + g, t * segs + h))
        return found

    fwd_rounds = pairs(lambda s, g: (s, (g + 1 ^ 1) - 1)), pairs(lambda s, g: (s, g ^ 1))
    side_down = pairs(lambda s, g: (s - 1, segs - 1 - g))
    side_up = pairs(lambda s, g: (s + 1, segs - 1 - g))
    side_rounds = (
        pairs(lambda s, g: ((s + 1 ^ 1) - 1, segs - 1 - g)),
        pairs(lambda s, g: (s ^ 1, segs - 1 - g)),
    )
    lcam, lpoint = loc_cam_jac[:, :, 0], loc_point_jac[:, :, 0]
    lcams = loc_cams.reshape(-1, LANES)
    fcam, fpoint = rows_of(fwd_cam_jac), rows_of(fwd_point_jac)
    scam, spoint = rows_of(side_cam_jac), rows_of(side_point_jac)
    fcams = fwd_cams.reshape(2, 2, -1, LANES)
    scams = side_cams.reshape(2, 2, -1, LANES)
    fr, sr = fcam.shape[2], scam.shape[2]
    watched = lcam.shape[1]

    def meet(sends, rounds):
        return [lax.ppermute(send, AXES, pairs) for send, pairs in zip(sends, rounds)]

    index_scratch = [pltpu.VMEM((2, fr, LANES), jnp.int32), pltpu.VMEM((2, sr, LANES), jnp.int32)]
    z_scratch = [pltpu.VMEM((2, 3, fr, LANES), F32), pltpu.VMEM((2, 3, sr, LANES), F32)]
    total_scratch = scatter_scratch(STEP)

    def sends_of(parts):
        return [(parts, fr // 2, LANES)] * 2, [(parts, sr // 2, LANES)] * 2

    far = [gradient, fcam, fpoint, fcams, scam, spoint, scams]
    table = [pltpu.VMEM((ROWS, LANES), F32)]
    fshapes, sshapes = sends_of(9)
    shapes = [(2, 2, fr, LANES)] + fshapes + [(2, 2, sr, LANES)] + sshapes
    fseen, *fsent, sseen, ssent0, ssent1 = call(
        look_kernel,
        far,
        shapes,
        [pltpu.VMEM(x.shape, x.dtype) for x in far]
        + [pltpu.VMEM(shape, F32) for shape in shapes]
        + table
        + index_scratch
        + [pltpu.VMEM((9, fr, LANES), F32), pltpu.VMEM((9, sr, LANES), F32)]
        + [pltpu.SemaphoreType.DMA((len(far),)), pltpu.SemaphoreType.DMA((len(shapes),))],
        10**9,
        "look",
        FAR,
        FAR,
        63,
    )
    ssent = [ssent0, ssent1]
    smet = meet(ssent, side_rounds)
    fmet = meet(fsent, fwd_rounds)

    def local(values):
        return call(
            local_kernel,
            [live_blocks, values, lcam, lpoint, lcams],
            [(ROWS, LANES), (8, LANES)],
            scatter_scratch(watched * LOCAL_GROUP) + table,
            5 * 10**9,
            "local",
        )

    extra, _ = local(gradient)
    fmarks, smarks = call(
        marks_kernel,
        [fcams, scams],
        [(2, fr, LANES, LANES), (2, sr, LANES, LANES)],
        [],
        10**9,
        "marks",
        kind=jnp.bfloat16,
    )
    fshapes, sshapes = sends_of(3)
    p, finverse, sinverse, fseen, fsend0, fsend1, sseen, sown, sguest, dots = call(
        middle_kernel,
        [gradient, extra, fcam, fpoint, fcams, scam, spoint, scams, fmarks, smarks,
         fseen, *fsent, *fmet, sseen, *ssent, *smet],
        [(ROWS, LANES), (2, 6, fr // 2, LANES), (2, 6, sr // 2, LANES), (2, 2, fr, LANES)]
        + fshapes + [(2, 2, sr, LANES)] + sshapes + [(8, LANES)],
        table + index_scratch
        + [pltpu.VMEM((3, fr, LANES), F32), pltpu.VMEM((3, sr, LANES), F32)]
        + z_scratch + total_scratch + [pltpu.VMEM((STEP, LANES), F32)],
        10**10,
        "middle",
    )
    smet = lax.ppermute(sguest, AXES, side_down)
    fmet = meet((fsend0, fsend1), fwd_rounds)
    extra, product = local(p)
    fz, sz, line = call(
        dots_kernel,
        [dots, product, fsend0, fsend1, *fmet, finverse, sown, smet, sinverse],
        [(2, 3, fr, LANES), (3, sr // 2, LANES), (strips * segs, LANES)],
        [pltpu.VMEM((8, LANES), F32)],
        10**8,
        "dots",
    )
    line = lax.all_to_all(line, AXES, 0, 0, tiled=True)
    ssent = lax.ppermute(sz, AXES, side_up)
    (t,) = call(
        last_kernel,
        [extra, fcam, fpoint, fcams, scam, spoint, scams, fmarks, smarks, fseen, fz, sseen, sz],
        [(ROWS, LANES)],
        index_scratch + z_scratch[1:] + total_scratch,
        5 * 10**9,
        "last",
    )
    step, residual = call(
        close_kernel,
        [t, scam, spoint, scams, smarks, sseen, ssent, line, gradient, p],
        [gradient.shape] * 2,
        table * 2 + index_scratch[1:] + z_scratch[1:] + total_scratch,
        2 * 10**9,
        "close",
    )
    return step, residual


def solution(mesh):
    placed = (
        P(None, "strip", "seg"),
        P("strip", "seg"),
        P(None, None, "strip", "seg"),
        P(None, None, "strip", "seg"),
        P(None, "strip", "seg"),
        P(None, None, None, "strip", "seg"),
        P(None, None, None, "strip", "seg"),
        P(None, None, "strip", "seg"),
        P(None, None, None, "strip", "seg"),
        P(None, None, None, "strip", "seg"),
        P(None, None, "strip", "seg"),
    )
    return jax.shard_map(
        per_device,
        mesh=mesh,
        in_specs=placed,
        out_specs=(P(None, "strip", "seg"), P(None, "strip", "seg")),
        check_vma=False,
    )
```

```python
import jax
import jax.numpy as jnp
from jax import lax
from jax.experimental import pallas as pl
from jax.experimental.pallas import tpu as pltpu
from jax.sharding import PartitionSpec as P

AXES = ("strip", "seg")
LANES = 128
JAC = 9
PAGES = 4
ROWS = JAC * PAGES
STACK = 80
STEP = 16
LOCAL_GROUP = 8
SYM = ((0, 0), (0, 1), (0, 2), (1, 1), (1, 2), (2, 2))
DAMP = 1.0
VMEM = pl.BlockSpec(memory_space=pltpu.VMEM)
FAR = pl.BlockSpec(memory_space=pltpu.HBM)
F32 = jnp.float32


def fetch(table, index):
    lane = index & (LANES - 1)
    odd = (index & LANES) != 0
    upper = index >= 2 * LANES
    found = []
    for j in range(JAC):
        page = [
            jnp.take_along_axis(
                jnp.broadcast_to(table[pl.ds(PAGES * j + k, 1), :], index.shape), lane, axis=1
            )
            for k in range(PAGES)
        ]
        low = jnp.where(odd, page[1], page[0])
        high = jnp.where(odd, page[3], page[2])
        found.append(jnp.where(upper, high, low))
    return found


def predict(across, values):
    return [sum(across[JAC * r + j] * values[j] for j in range(JAC)) for r in range(2)]


def project(along, seen):
    return [along[k] * seen[0] + along[3 + k] * seen[1] for k in range(3)]


def normal(along):
    return [along[i] * along[j] + along[3 + i] * along[3 + j] for i, j in SYM]


def invert(h):
    a, b, c, d, e, f = h[0] + DAMP, h[1], h[2], h[3] + DAMP, h[4], h[5] + DAMP
    first = d * f - e * e
    second = c * e - b * f
    third = b * e - c * d
    scale = 1.0 / (a * first + b * second + c * third)
    return [
        m * scale for m in (first, second, third, a * f - c * c, b * c - a * e, a * d - b * b)
    ]


def solve(m, b):
    return [
        m[0] * b[0] + m[1] * b[1] + m[2] * b[2],
        m[1] * b[0] + m[3] * b[1] + m[4] * b[2],
        m[2] * b[0] + m[4] * b[1] + m[5] * b[2],
    ]


def residue(along, seen, z):
    return [seen[r] - sum(along[3 * r + k] * z[k] for k in range(3)) for r in range(2)]


def spread(terms, index, stage, total):
    add_in([stacked(terms, index, stage)], total)


def add_in(parts, total):
    total[...] += lax.dot_general(
        jnp.concatenate([x for left, _ in parts for x in left], axis=1),
        jnp.concatenate([x for _, right in parts for x in right], axis=1),
        (((1,), (1,)), ((), ())),
        preferred_element_type=F32,
    )


def stacked(terms, index, stage):
    count = index.shape[0]
    page = index >> 7
    coarse = terms[JAC - 1].astype(jnp.bfloat16).astype(F32)
    fine = terms[JAC - 1] - coarse
    for j in range(JAC - 1):
        stage[pl.ds(j, count, stride=16), :] = terms[j]
    for h in range(PAGES):
        stage[pl.ds(8 + h, count, stride=16), :] = jnp.where(page == h, coarse, 0.0)
        stage[pl.ds(12 + h, count, stride=16), :] = jnp.where(page == h, fine, 0.0)
    page = page.astype(F32)
    lane = (index & (LANES - 1)).astype(F32)
    place = lax.broadcasted_iota(jnp.int32, (LANES, LANES), 0).astype(F32).astype(jnp.bfloat16)
    one, none = jnp.ones((), jnp.bfloat16), jnp.zeros((), jnp.bfloat16)
    left, right = [], []
    for row in range(count):
        raw = stage[pl.ds(16 * row, 8), :]
        rest = stage[pl.ds(16 * row + 8, 8), :]
        coarse = raw.astype(jnp.bfloat16).astype(F32)
        both = jnp.concatenate([coarse, raw - coarse], axis=0).astype(jnp.bfloat16)
        wide = jnp.broadcast_to(page[row : row + 1], (16, LANES)).astype(jnp.bfloat16)
        tiles = [jnp.where(wide == h, both, none) for h in range(PAGES)]
        tiles.append(jnp.concatenate([rest, jnp.zeros_like(rest)], axis=0).astype(jnp.bfloat16))
        left.append(jnp.concatenate(tiles, axis=0))
        wide = jnp.broadcast_to(lane[row : row + 1], (16, LANES)).astype(jnp.bfloat16)
        wide = jnp.concatenate([wide] * (LANES // 16), axis=0)
        right.append(jnp.where(wide == place, one, none))
    return left, right


def scatter_scratch(count):
    return [pltpu.VMEM((16 * count, LANES), F32), pltpu.VMEM((STACK, LANES), F32)]


def fold(total, out):
    for h in range(PAGES):
        out[pl.ds(h, JAC - 1, stride=PAGES), :] = (
            total[pl.ds(16 * h, 8), :] + total[pl.ds(16 * h + 8, 8), :]
        )
    out[pl.ds(ROWS - PAGES, PAGES), :] = total[64:68, :] + total[68:72, :]


def weave(cams, index):
    half = cams.shape[2]
    for s in range(2):
        for o in range(2):
            index[s, pl.ds(o, half, stride=2), :] = cams[s, o]


def pair_look(cam, point, index, table, seen_out, loose, sends, odd, with_h, squares, held, done):
    rows = cam.shape[2]
    half = rows // 2
    for turn in range(2):
        s = turn ^ odd
        share = part_of(s, held)

        def body(i, carry, s=s, turn=turn, share=share):
            at = pl.ds(pl.multiple_of(i * STEP, STEP), STEP)
            across = [cam[s, j, at, :].astype(F32) for j in range(2 * JAC)]
            along = [point[s, j, at, :].astype(F32) for j in range(6)]
            seen = predict(across, fetch(table, index[s, at, :]))
            for r in range(2):
                seen_out[turn, r, at, :] = seen[r]
            parts = project(along, seen)
            if with_h:
                parts = parts + normal(along)
            for n, part in enumerate(parts):
                loose[n, at, :] = part
            if squares is not None:
                squares[...] += share * (seen[0] * seen[0] + seen[1] * seen[1])
            return carry

        lax.fori_loop(0, rows // STEP, body, 0, unroll=True)
        for n in range(9 if with_h else 3):
            sends[turn][n] = (
                loose[n, pl.ds(0, half, stride=2), :] + loose[n, pl.ds(1, half, stride=2), :]
            )
        if done is not None:
            done(turn)


def part_of(side, held):
    if isinstance(side, int):
        return 1.0 if side == 0 else held.astype(F32)
    return jnp.where(side == 0, 1, held).astype(F32)


def pair_return(cam, point, index, seen_in, z, odd, held, stage, total, turns=(0, 1)):
    rows = cam.shape[2]
    for turn in turns:
        s = turn ^ odd
        share = part_of(s, held)

        def body(i, carry, s=s, turn=turn, share=share):
            at = pl.ds(pl.multiple_of(i * STEP, STEP), STEP)
            across = [cam[s, j, at, :].astype(F32) for j in range(2 * JAC)]
            along = [point[s, j, at, :].astype(F32) for j in range(6)]
            left = residue(
                along,
                [seen_in[turn, r, at, :] for r in range(2)],
                [z[turn, k, at, :] for k in range(3)],
            )
            left = [share * e for e in left]
            terms = [across[j] * left[0] + across[JAC + j] * left[1] for j in range(JAC)]
            spread(terms, index[s, at, :], stage, total)
            return carry

        lax.fori_loop(0, rows // STEP, body, 0, unroll=True)


def pair_solve(sent, met, inverse_out, z):
    half = sent[0].shape[1]
    for turn in range(2):
        for i in range(half // 8):
            at = pl.ds(8 * i, 8)
            joined = [sent[turn][k, at, :] + met[turn][k, at, :] for k in range(9)]
            inverse = invert(joined[3:])
            for k in range(6):
                inverse_out[turn, k, at, :] = inverse[k]
            put_z(z, turn, i, solve(inverse, joined[:3]))


def put_z(z, turn, i, solved):
    for k in range(3):
        for o in range(2):
            z[turn, k, pl.ds(16 * i + o, 8, stride=2), :] = solved[k]


def own_solve(own, met, inverse, z, products, odd):
    for i in range(own.shape[1] // 8):
        at = pl.ds(8 * i, 8)
        b = [own[k, at, :] + met[k, at, :] for k in range(3)]
        solved = solve([inverse[odd, k, at, :] for k in range(6)], b)
        products[...] += sum(b[k] * solved[k] for k in range(3))
        for k in range(3):
            z[k, at, :] = solved[k]


def both_solve(sent, met, inverse, z, products, odd):
    for turn in range(2):
        own = part_of(turn ^ odd, jnp.int32(0))
        for i in range(sent[0].shape[1] // 8):
            at = pl.ds(8 * i, 8)
            b = [sent[turn][k, at, :] + met[turn][k, at, :] for k in range(3)]
            solved = solve([inverse[turn, k, at, :] for k in range(6)], b)
            products[...] += own * sum(b[k] * solved[k] for k in range(3))
            put_z(z, turn, i, solved)


def widened(values, z, turn):
    for i in range(values.shape[1] // 8):
        put_z(z, turn, i, [values[k, pl.ds(8 * i, 8), :] for k in range(3)])


def place_of():
    seg, strip = lax.axis_index("seg"), lax.axis_index("strip")
    return (1 - (seg & 1), jnp.minimum(seg, 1)), (1 - (strip & 1), jnp.minimum(strip, 1))


def in_rows(lines, table):
    for j in range(JAC):
        for k in range(PAGES):
            table[pl.ds(PAGES * j + k, 1), :] = lines[j, :, pl.ds(LANES * k, LANES)]


def side_look_kernel(
    gradient, scam_at, spoint_at, scams_at, sseen_at, ssend0_at, ssend1_at,
    lines, scam, spoint, scams, sseen, ssend0, ssend1, table, sindex, sloose, arrived, left,
):
    _, (sodd, _) = place_of()
    moves = [
        pltpu.make_async_copy(source, target, arrived.at[n])
        for n, (source, target) in enumerate(
            ((gradient, lines), (scams_at, scams), (scam_at, scam), (spoint_at, spoint))
        )
    ]
    back = [
        pltpu.make_async_copy(source, target, left.at[n])
        for n, (source, target) in enumerate(
            ((ssend0, ssend0_at), (ssend1, ssend1_at), (sseen, sseen_at))
        )
    ]
    for move in moves:
        move.start()
    for move in moves[:2]:
        move.wait()
    in_rows(lines, table)
    weave(scams, sindex)
    for move in moves[2:]:
        move.wait()

    def done(turn):
        back[turn].start()
        if turn == 1:
            back[2].start()

    pair_look(
        scam, spoint, sindex, table, sseen, sloose, (ssend0, ssend1), sodd, True, None, 0, done
    )
    for move in back:
        move.wait()


def forward_look_kernel(
    lines, fcam, fpoint, fcams, fseen, fsend0, fsend1, table, findex, floose
):
    (fodd, _), _ = place_of()
    in_rows(lines, table)
    weave(fcams, findex)
    pair_look(
        fcam, fpoint, findex, table, fseen, floose, (fsend0, fsend1), fodd, True, None, 0, None
    )


def local_kernel(live, values, cam, point, cams, out, product, stage, total, table):
    total[...] = jnp.zeros_like(total)
    product[...] = jnp.zeros_like(product)
    if values.shape[0] == JAC:
        in_rows(values, table)
    else:
        table = values
    watched, blocks = cams.shape[0] // 16, cam.shape[2] // LANES
    lives = jnp.broadcast_to(live[...], (1, LANES))

    def block(i, stage):
        at = pl.ds(pl.multiple_of(i * LANES, LANES), LANES)
        index = cams[pl.ds(i, watched, stride=16), :]
        across = [cam[j, :, at].astype(F32) for j in range(2 * JAC)]
        along = [point[j, :, at].astype(F32) for j in range(6)]
        seen = predict(across, fetch(table, index))
        summed = [jnp.sum(x, axis=0, keepdims=True) for x in project(along, seen) + normal(along)]
        z = solve(invert(summed[3:]), summed[:3])
        share = jnp.where(lives > i, 1.0, 0.0)
        left = [share * e for e in residue(along, seen, z)]
        terms = [across[j] * left[0] + across[JAC + j] * left[1] for j in range(JAC)]
        seen = jnp.sum(seen[0] * left[0] + seen[1] * left[1], axis=0, keepdims=True)
        return seen, stacked(terms, index, stage)

    def body(i, carry):
        done = [
            block(LOCAL_GROUP * i + n, stage.at[pl.ds(16 * watched * n, 16 * watched)])
            for n in range(LOCAL_GROUP)
        ]
        product[0:1, :] += sum(seen for seen, _ in done)
        add_in([parts for _, parts in done], total)
        return carry

    lax.fori_loop(0, blocks // LOCAL_GROUP, body, 0)
    fold(total, out)


def middle_kernel(
    lines, extra, fcam, fpoint, fcams, scam, spoint, scams,
    fseen, fsent0, fsent1, fmet0, fmet1, sseen, ssent0, ssent1, smet0, smet1,
    result, finverse, sinverse, fseen2, fsend0, fsend1, sseen2, sown, sguest, dots,
    table, findex, sindex, floose, sloose, fz, sz, stage, total, squares,
):
    (fodd, fheld), (sodd, sheld) = place_of()
    in_rows(lines, table)
    weave(fcams, findex)
    weave(scams, sindex)
    total[...] = jnp.zeros_like(total)
    pair_solve((fsent0, fsent1), (fmet0, fmet1), finverse, fz)
    pair_return(fcam, fpoint, findex, fseen, fz, fodd, fheld, stage, total)
    pair_solve((ssent0, ssent1), (smet0, smet1), sinverse, sz)
    pair_return(scam, spoint, sindex, sseen, sz, sodd, sheld, stage, total)
    fold(total, result)
    step = result[...] + extra[...]
    result[...] = step
    squares[...] = jnp.zeros_like(squares)
    sends = (fsend0, fsend1)
    pair_look(
        fcam, fpoint, findex, result, fseen2, floose, sends, fodd, False, squares, fheld, None
    )
    sides = (sown, sguest)
    pair_look(scam, spoint, sindex, result, sseen2, sloose, sides, 0, False, squares, sheld, None)
    base = table[...]
    dots[...] = jnp.zeros_like(dots)
    for row, value in enumerate((base * base, base * step, step * step, squares[...])):
        dots[row : row + 1, :] = jnp.sum(value, axis=0, keepdims=True)


def dots_kernel(
    dots, product, fsent0, fsent1, fmet0, fmet1, finverse, sown, smet, sinverse,
    fz, sz, out, products,
):
    (fodd, _), (sodd, _) = place_of()
    products[...] = jnp.zeros_like(products)
    both_solve((fsent0, fsent1), (fmet0, fmet1), finverse, fz, products, fodd)
    own_solve(sown, smet, sinverse, sz, products, sodd)
    curve = dots[3:4, :] + product[0:1, :] - jnp.sum(products[...], axis=0, keepdims=True)
    rows = jnp.concatenate([dots[0:3, :], curve], axis=0)
    sums = jnp.sum(rows, axis=1, keepdims=True)
    place = lax.broadcasted_iota(jnp.int32, (1, LANES), 1)
    line = jnp.zeros((1, LANES), F32)
    for n in range(4):
        line = line + jnp.where(place == n, sums[n : n + 1, :], 0.0)
    out[...] = jnp.broadcast_to(line, out.shape)


def last_kernel(
    extra, fcam, fpoint, fcams, scam, spoint, scams, fseen, fz, sseen, svalues,
    result, findex, sindex, sz, stage, total,
):
    (fodd, fheld), (_, sheld) = place_of()
    weave(fcams, findex)
    weave(scams, sindex)
    total[...] = jnp.zeros_like(total)
    pair_return(fcam, fpoint, findex, fseen, fz, fodd, fheld, stage, total)
    widened(svalues, sz, 0)
    pair_return(scam, spoint, sindex, sseen, sz, 0, sheld, stage, total, (0,))
    fold(total, result)
    result[...] += extra[...]


def close_kernel(
    extra, scam, spoint, scams, sseen, svalues, sums, lines, first,
    step_out, residual_out, base, second, sindex, sz, stage, total,
):
    _, (_, sheld) = place_of()
    weave(scams, sindex)
    total[...] = jnp.zeros_like(total)
    widened(svalues, sz, 1)
    pair_return(scam, spoint, sindex, sseen, sz, 0, sheld, stage, total, (1,))
    fold(total, second)
    second[...] += extra[...]
    in_rows(lines, base)
    line = jnp.sum(sums[...], axis=0, keepdims=True)
    place = lax.broadcasted_iota(jnp.int32, line.shape, 1)
    rr, bp, pp, curve = [
        jnp.sum(jnp.where(place == n, line, 0.0), axis=1, keepdims=True) for n in range(4)
    ]
    whole = rr + bp
    alpha = rr / whole
    rest = bp / whole
    new = alpha * (alpha * pp - rest * bp)
    gamma = rest + new / rr
    bend = gamma * gamma * rr - 2.0 * gamma * alpha * bp + alpha * alpha * pp
    bend = bend + gamma * gamma * bp - 2.0 * gamma * alpha * pp + alpha * alpha * curve
    again = new / bend
    d0, p, t = base[...], first[...], second[...]
    direction = gamma * d0 - alpha * p
    image = gamma * d0 + (gamma - alpha) * p - alpha * t
    step = -(alpha * d0 + again * direction)
    residual = -(rest * d0 - alpha * p - again * image)
    for j in range(JAC):
        for k in range(PAGES):
            row = PAGES * j + k
            step_out[j, :, pl.ds(LANES * k, LANES)] = step[row : row + 1, :]
            residual_out[j, :, pl.ds(LANES * k, LANES)] = residual[row : row + 1, :]


def call(kernel, ins, outs, scratch, flops, name, place=VMEM, to=VMEM, room=12):
    outs = [jax.ShapeDtypeStruct(shape, F32) for shape in outs]
    specs = [place] * len(ins)
    return pl.pallas_call(
        kernel,
        out_shape=outs,
        in_specs=specs,
        out_specs=[to] * len(outs),
        scratch_shapes=scratch,
        compiler_params=pltpu.CompilerParams(vmem_limit_bytes=room << 20),
        cost_estimate=pl.CostEstimate(flops=flops, bytes_accessed=2 << 20, transcendentals=0),
        name=name,
    )(*ins)


def rows_of(array):
    kinds, parts, two, _, points = array.shape
    array = array.reshape(kinds, parts, two, points // LANES, LANES)
    return array.transpose(0, 1, 3, 2, 4).reshape(kinds, parts, two * points // LANES, LANES)


def per_device(
    gradient, live_blocks, loc_cam_jac, loc_point_jac, loc_cams,
    fwd_cam_jac, fwd_point_jac, fwd_cams, side_cam_jac, side_point_jac, side_cams,
):
    strips, segs = lax.axis_size("strip"), lax.axis_size("seg")
    cells = [(s, g) for s in range(strips) for g in range(segs)]

    def pairs(move):
        found = []
        for s, g in cells:
            t, h = move(s, g)
            if 0 <= t < strips and 0 <= h < segs:
                found.append((s * segs + g, t * segs + h))
        return found

    fwd_rounds = pairs(lambda s, g: (s, (g + 1 ^ 1) - 1)), pairs(lambda s, g: (s, g ^ 1))
    side_down = pairs(lambda s, g: (s - 1, segs - 1 - g))
    side_up = pairs(lambda s, g: (s + 1, segs - 1 - g))
    side_rounds = (
        pairs(lambda s, g: ((s + 1 ^ 1) - 1, segs - 1 - g)),
        pairs(lambda s, g: (s ^ 1, segs - 1 - g)),
    )
    lcam, lpoint = loc_cam_jac[:, :, 0], loc_point_jac[:, :, 0]
    lcams = loc_cams.reshape(-1, LANES)
    fcam, fpoint = rows_of(fwd_cam_jac), rows_of(fwd_point_jac)
    scam, spoint = rows_of(side_cam_jac), rows_of(side_point_jac)
    fcams = fwd_cams.reshape(2, 2, -1, LANES)
    scams = side_cams.reshape(2, 2, -1, LANES)
    fr, sr = fcam.shape[2], scam.shape[2]
    watched = lcam.shape[1]

    def meet(sends, rounds):
        return [lax.ppermute(send, AXES, pairs) for send, pairs in zip(sends, rounds)]

    index_scratch = [pltpu.VMEM((2, fr, LANES), jnp.int32), pltpu.VMEM((2, sr, LANES), jnp.int32)]
    z_scratch = [pltpu.VMEM((2, 3, fr, LANES), F32), pltpu.VMEM((2, 3, sr, LANES), F32)]
    total_scratch = scatter_scratch(STEP)

    def sends_of(parts):
        return [(parts, fr // 2, LANES)] * 2, [(parts, sr // 2, LANES)] * 2

    far = [gradient, scam, spoint, scams]
    table = [pltpu.VMEM((ROWS, LANES), F32)]
    fshapes, sshapes = sends_of(9)
    shapes = [(2, 2, sr, LANES)] + sshapes
    sseen, *ssent = call(
        side_look_kernel,
        far,
        shapes,
        [pltpu.VMEM(x.shape, x.dtype) for x in far]
        + [pltpu.VMEM(shape, F32) for shape in shapes]
        + table
        + index_scratch[1:]
        + [pltpu.VMEM((9, sr, LANES), F32)]
        + [pltpu.SemaphoreType.DMA((len(far),)), pltpu.SemaphoreType.DMA((len(shapes),))],
        10**9,
        "look",
        FAR,
        FAR,
        63,
    )
    fseen, *fsent = call(
        forward_look_kernel,
        [gradient, fcam, fpoint, fcams],
        [(2, 2, fr, LANES)] + fshapes,
        table + index_scratch[:1] + [pltpu.VMEM((9, fr, LANES), F32)],
        10**9,
        "forward_look",
    )
    smet = meet(ssent, side_rounds)
    fmet = meet(fsent, fwd_rounds)

    def local(values):
        return call(
            local_kernel,
            [live_blocks, values, lcam, lpoint, lcams],
            [(ROWS, LANES), (8, LANES)],
            scatter_scratch(watched * LOCAL_GROUP) + table,
            5 * 10**9,
            "local",
        )

    extra, _ = local(gradient)
    fshapes, sshapes = sends_of(3)
    p, finverse, sinverse, fseen, fsend0, fsend1, sseen, sown, sguest, dots = call(
        middle_kernel,
        [gradient, extra, fcam, fpoint, fcams, scam, spoint, scams,
         fseen, *fsent, *fmet, sseen, *ssent, *smet],
        [(ROWS, LANES), (2, 6, fr // 2, LANES), (2, 6, sr // 2, LANES), (2, 2, fr, LANES)]
        + fshapes + [(2, 2, sr, LANES)] + sshapes + [(8, LANES)],
        table + index_scratch
        + [pltpu.VMEM((3, fr, LANES), F32), pltpu.VMEM((3, sr, LANES), F32)]
        + z_scratch + total_scratch + [pltpu.VMEM((STEP, LANES), F32)],
        10**10,
        "middle",
    )
    smet = lax.ppermute(sguest, AXES, side_down)
    fmet = meet((fsend0, fsend1), fwd_rounds)
    extra, product = local(p)
    fz, sz, line = call(
        dots_kernel,
        [dots, product, fsend0, fsend1, *fmet, finverse, sown, smet, sinverse],
        [(2, 3, fr, LANES), (3, sr // 2, LANES), (strips * segs, LANES)],
        [pltpu.VMEM((8, LANES), F32)],
        10**8,
        "dots",
    )
    line = lax.all_to_all(line, AXES, 0, 0, tiled=True)
    ssent = lax.ppermute(sz, AXES, side_up)
    (t,) = call(
        last_kernel,
        [extra, fcam, fpoint, fcams, scam, spoint, scams, fseen, fz, sseen, sz],
        [(ROWS, LANES)],
        index_scratch + z_scratch[1:] + total_scratch,
        5 * 10**9,
        "last",
    )
    step, residual = call(
        close_kernel,
        [t, scam, spoint, scams, sseen, ssent, line, gradient, p],
        [gradient.shape] * 2,
        table * 2 + index_scratch[1:] + z_scratch[1:] + total_scratch,
        2 * 10**9,
        "close",
    )
    return step, residual


def solution(mesh):
    placed = (
        P(None, "strip", "seg"),
        P("strip", "seg"),
        P(None, None, "strip", "seg"),
        P(None, None, "strip", "seg"),
        P(None, "strip", "seg"),
        P(None, None, None, "strip", "seg"),
        P(None, None, None, "strip", "seg"),
        P(None, None, "strip", "seg"),
        P(None, None, None, "strip", "seg"),
        P(None, None, None, "strip", "seg"),
        P(None, None, "strip", "seg"),
    )
    return jax.shard_map(
        per_device,
        mesh=mesh,
        in_specs=placed,
        out_specs=(P(None, "strip", "seg"), P(None, "strip", "seg")),
        check_vma=False,
    )
```

```python
import jax
import jax.numpy as jnp
from jax import lax
from jax.experimental import pallas as pl
from jax.experimental.pallas import tpu as pltpu
from jax.sharding import PartitionSpec as P

AXES = ("strip", "seg")
LANES = 128
JAC = 9
PAGES = 4
ROWS = JAC * PAGES
STACK = 80
STEP = 16
LOCAL_GROUP = 8
SYM = ((0, 0), (0, 1), (0, 2), (1, 1), (1, 2), (2, 2))
DAMP = 1.0
VMEM = pl.BlockSpec(memory_space=pltpu.VMEM)
FAR = pl.BlockSpec(memory_space=pltpu.HBM)
F32 = jnp.float32


def fetch(table, index):
    lane = index & (LANES - 1)
    odd = (index & LANES) != 0
    upper = index >= 2 * LANES
    found = []
    for j in range(JAC):
        page = [
            jnp.take_along_axis(
                jnp.broadcast_to(table[pl.ds(PAGES * j + k, 1), :], index.shape), lane, axis=1
            )
            for k in range(PAGES)
        ]
        low = jnp.where(odd, page[1], page[0])
        high = jnp.where(odd, page[3], page[2])
        found.append(jnp.where(upper, high, low))
    return found


def predict(across, values):
    return [sum(across[JAC * r + j] * values[j] for j in range(JAC)) for r in range(2)]


def project(along, seen):
    return [along[k] * seen[0] + along[3 + k] * seen[1] for k in range(3)]


def normal(along):
    return [along[i] * along[j] + along[3 + i] * along[3 + j] for i, j in SYM]


def invert(h):
    a, b, c, d, e, f = h[0] + DAMP, h[1], h[2], h[3] + DAMP, h[4], h[5] + DAMP
    first = d * f - e * e
    second = c * e - b * f
    third = b * e - c * d
    scale = 1.0 / (a * first + b * second + c * third)
    return [
        m * scale for m in (first, second, third, a * f - c * c, b * c - a * e, a * d - b * b)
    ]


def solve(m, b):
    return [
        m[0] * b[0] + m[1] * b[1] + m[2] * b[2],
        m[1] * b[0] + m[3] * b[1] + m[4] * b[2],
        m[2] * b[0] + m[4] * b[1] + m[5] * b[2],
    ]


def residue(along, seen, z):
    return [seen[r] - sum(along[3 * r + k] * z[k] for k in range(3)) for r in range(2)]


def spread(terms, index, stage, total):
    add_in([stacked(terms, index, stage)], total)


def add_in(parts, total):
    total[...] += lax.dot_general(
        jnp.concatenate([x for left, _ in parts for x in left], axis=1),
        jnp.concatenate([x for _, right in parts for x in right], axis=1),
        (((1,), (1,)), ((), ())),
        preferred_element_type=F32,
    )


def stacked(terms, index, stage):
    count = index.shape[0]
    page = index >> 7
    coarse = terms[JAC - 1].astype(jnp.bfloat16).astype(F32)
    fine = terms[JAC - 1] - coarse
    for j in range(JAC - 1):
        stage[pl.ds(j, count, stride=16), :] = terms[j]
    for h in range(PAGES):
        stage[pl.ds(8 + h, count, stride=16), :] = jnp.where(page == h, coarse, 0.0)
        stage[pl.ds(12 + h, count, stride=16), :] = jnp.where(page == h, fine, 0.0)
    page = page.astype(F32)
    lane = (index & (LANES - 1)).astype(F32)
    place = lax.broadcasted_iota(jnp.int32, (LANES, LANES), 0).astype(F32).astype(jnp.bfloat16)
    one, none = jnp.ones((), jnp.bfloat16), jnp.zeros((), jnp.bfloat16)
    left, right = [], []
    for row in range(count):
        raw = stage[pl.ds(16 * row, 8), :]
        rest = stage[pl.ds(16 * row + 8, 8), :]
        coarse = raw.astype(jnp.bfloat16).astype(F32)
        both = jnp.concatenate([coarse, raw - coarse], axis=0).astype(jnp.bfloat16)
        wide = jnp.broadcast_to(page[row : row + 1], (16, LANES)).astype(jnp.bfloat16)
        tiles = [jnp.where(wide == h, both, none) for h in range(PAGES)]
        tiles.append(jnp.concatenate([rest, jnp.zeros_like(rest)], axis=0).astype(jnp.bfloat16))
        left.append(jnp.concatenate(tiles, axis=0))
        wide = jnp.broadcast_to(lane[row : row + 1], (16, LANES)).astype(jnp.bfloat16)
        wide = jnp.concatenate([wide] * (LANES // 16), axis=0)
        right.append(jnp.where(wide == place, one, none))
    return left, right


def scatter_scratch(count):
    return [pltpu.VMEM((16 * count, LANES), F32), pltpu.VMEM((STACK, LANES), F32)]


def fold(total, out):
    for h in range(PAGES):
        out[pl.ds(h, JAC - 1, stride=PAGES), :] = (
            total[pl.ds(16 * h, 8), :] + total[pl.ds(16 * h + 8, 8), :]
        )
    out[pl.ds(ROWS - PAGES, PAGES), :] = total[64:68, :] + total[68:72, :]


def weave(cams, index):
    half = cams.shape[2]
    for s in range(2):
        for o in range(2):
            index[s, pl.ds(o, half, stride=2), :] = cams[s, o]


def pair_look(
    cam, point, index, table, seen_out, loose, sends, odd, with_h, squares, held, done,
    kept=None, ready=None,
):
    rows = cam.shape[2]
    half = rows // 2
    if kept is not None:
        for s in range(2):
            for i in range(rows // STEP):
                at = pl.ds(i * STEP, STEP)
                for j, found in enumerate(fetch(table, index[s, at, :])):
                    kept[s, j, at, :] = found
        ready()
    for turn in range(2):
        s = turn ^ odd
        share = part_of(s, held)

        def body(i, carry, s=s, turn=turn, share=share):
            at = pl.ds(pl.multiple_of(i * STEP, STEP), STEP)
            across = [cam[s, j, at, :].astype(F32) for j in range(2 * JAC)]
            along = [point[s, j, at, :].astype(F32) for j in range(6)]
            if kept is None:
                values = fetch(table, index[s, at, :])
            else:
                values = [kept[s, j, at, :] for j in range(JAC)]
            seen = predict(across, values)
            for r in range(2):
                seen_out[turn, r, at, :] = seen[r]
            parts = project(along, seen)
            if with_h:
                parts = parts + normal(along)
            for n, part in enumerate(parts):
                loose[n, at, :] = part
            if squares is not None:
                squares[...] += share * (seen[0] * seen[0] + seen[1] * seen[1])
            return carry

        lax.fori_loop(0, rows // STEP, body, 0, unroll=True)
        for n in range(9 if with_h else 3):
            sends[turn][n] = (
                loose[n, pl.ds(0, half, stride=2), :] + loose[n, pl.ds(1, half, stride=2), :]
            )
        if done is not None:
            done(turn)


def part_of(side, held):
    if isinstance(side, int):
        return 1.0 if side == 0 else held.astype(F32)
    return jnp.where(side == 0, 1, held).astype(F32)


def pair_return(cam, point, index, seen_in, z, odd, held, stage, total, turns=(0, 1)):
    rows = cam.shape[2]
    for turn in turns:
        s = turn ^ odd
        share = part_of(s, held)

        def body(i, carry, s=s, turn=turn, share=share):
            at = pl.ds(pl.multiple_of(i * STEP, STEP), STEP)
            across = [cam[s, j, at, :].astype(F32) for j in range(2 * JAC)]
            along = [point[s, j, at, :].astype(F32) for j in range(6)]
            left = residue(
                along,
                [seen_in[turn, r, at, :] for r in range(2)],
                [z[turn, k, at, :] for k in range(3)],
            )
            left = [share * e for e in left]
            terms = [across[j] * left[0] + across[JAC + j] * left[1] for j in range(JAC)]
            spread(terms, index[s, at, :], stage, total)
            return carry

        lax.fori_loop(0, rows // STEP, body, 0, unroll=True)


def pair_solve(sent, met, inverse_out, z):
    half = sent[0].shape[1]
    for turn in range(2):
        for i in range(half // 8):
            at = pl.ds(8 * i, 8)
            joined = [sent[turn][k, at, :] + met[turn][k, at, :] for k in range(9)]
            inverse = invert(joined[3:])
            for k in range(6):
                inverse_out[turn, k, at, :] = inverse[k]
            put_z(z, turn, i, solve(inverse, joined[:3]))


def put_z(z, turn, i, solved):
    for k in range(3):
        for o in range(2):
            z[turn, k, pl.ds(16 * i + o, 8, stride=2), :] = solved[k]


def own_solve(own, met, inverse, z, products, odd):
    for i in range(own.shape[1] // 8):
        at = pl.ds(8 * i, 8)
        b = [own[k, at, :] + met[k, at, :] for k in range(3)]
        solved = solve([inverse[odd, k, at, :] for k in range(6)], b)
        products[...] += sum(b[k] * solved[k] for k in range(3))
        for k in range(3):
            z[k, at, :] = solved[k]


def both_solve(sent, met, inverse, z, products, odd):
    for turn in range(2):
        own = part_of(turn ^ odd, jnp.int32(0))
        for i in range(sent[0].shape[1] // 8):
            at = pl.ds(8 * i, 8)
            b = [sent[turn][k, at, :] + met[turn][k, at, :] for k in range(3)]
            solved = solve([inverse[turn, k, at, :] for k in range(6)], b)
            products[...] += own * sum(b[k] * solved[k] for k in range(3))
            put_z(z, turn, i, solved)


def widened(values, z, turn):
    for i in range(values.shape[1] // 8):
        put_z(z, turn, i, [values[k, pl.ds(8 * i, 8), :] for k in range(3)])


def place_of():
    seg, strip = lax.axis_index("seg"), lax.axis_index("strip")
    return (1 - (seg & 1), jnp.minimum(seg, 1)), (1 - (strip & 1), jnp.minimum(strip, 1))


def in_rows(lines, table):
    for j in range(JAC):
        for k in range(PAGES):
            table[pl.ds(PAGES * j + k, 1), :] = lines[j, :, pl.ds(LANES * k, LANES)]


def side_look_kernel(
    gradient, scam_at, spoint_at, scams_at, sseen_at, ssend0_at, ssend1_at,
    lines, scam, spoint, scams, sseen, ssend0, ssend1, table, sindex, sloose, kept,
    arrived, left,
):
    _, (sodd, _) = place_of()
    moves = [
        pltpu.make_async_copy(source, target, arrived.at[n])
        for n, (source, target) in enumerate(
            ((gradient, lines), (scams_at, scams), (scam_at, scam), (spoint_at, spoint))
        )
    ]
    back = [
        pltpu.make_async_copy(source, target, left.at[n])
        for n, (source, target) in enumerate(
            ((ssend0, ssend0_at), (ssend1, ssend1_at), (sseen, sseen_at))
        )
    ]
    for move in moves:
        move.start()
    for move in moves[:2]:
        move.wait()
    in_rows(lines, table)
    weave(scams, sindex)

    def ready():
        for move in moves[2:]:
            move.wait()

    def done(turn):
        back[turn].start()
        if turn == 1:
            back[2].start()

    pair_look(
        scam, spoint, sindex, table, sseen, sloose, (ssend0, ssend1), sodd, True, None, 0, done,
        kept, ready,
    )
    for move in back:
        move.wait()


def forward_look_kernel(
    lines, fcam, fpoint, fcams, fseen, fsend0, fsend1, table, findex, floose
):
    (fodd, _), _ = place_of()
    in_rows(lines, table)
    weave(fcams, findex)
    pair_look(
        fcam, fpoint, findex, table, fseen, floose, (fsend0, fsend1), fodd, True, None, 0, None
    )


def local_kernel(live, values, cam, point, cams, out, product, stage, total, table):
    total[...] = jnp.zeros_like(total)
    product[...] = jnp.zeros_like(product)
    if values.shape[0] == JAC:
        in_rows(values, table)
    else:
        table = values
    watched, blocks = cams.shape[0] // 16, cam.shape[2] // LANES
    lives = jnp.broadcast_to(live[...], (1, LANES))

    def block(i, stage):
        at = pl.ds(pl.multiple_of(i * LANES, LANES), LANES)
        index = cams[pl.ds(i, watched, stride=16), :]
        across = [cam[j, :, at].astype(F32) for j in range(2 * JAC)]
        along = [point[j, :, at].astype(F32) for j in range(6)]
        seen = predict(across, fetch(table, index))
        summed = [jnp.sum(x, axis=0, keepdims=True) for x in project(along, seen) + normal(along)]
        z = solve(invert(summed[3:]), summed[:3])
        share = jnp.where(lives > i, 1.0, 0.0)
        left = [share * e for e in residue(along, seen, z)]
        terms = [across[j] * left[0] + across[JAC + j] * left[1] for j in range(JAC)]
        seen = jnp.sum(seen[0] * left[0] + seen[1] * left[1], axis=0, keepdims=True)
        return seen, stacked(terms, index, stage)

    def body(i, carry):
        done = [
            block(LOCAL_GROUP * i + n, stage.at[pl.ds(16 * watched * n, 16 * watched)])
            for n in range(LOCAL_GROUP)
        ]
        product[0:1, :] += sum(seen for seen, _ in done)
        add_in([parts for _, parts in done], total)
        return carry

    lax.fori_loop(0, blocks // LOCAL_GROUP, body, 0)
    fold(total, out)


def middle_kernel(
    lines, extra, fcam, fpoint, fcams, scam, spoint, scams,
    fseen, fsent0, fsent1, fmet0, fmet1, sseen, ssent0, ssent1, smet0, smet1,
    result, finverse, sinverse, fseen2, fsend0, fsend1, sseen2, sown, sguest, dots,
    table, findex, sindex, floose, sloose, fz, sz, stage, total, squares,
):
    (fodd, fheld), (sodd, sheld) = place_of()
    in_rows(lines, table)
    weave(fcams, findex)
    weave(scams, sindex)
    total[...] = jnp.zeros_like(total)
    pair_solve((fsent0, fsent1), (fmet0, fmet1), finverse, fz)
    pair_return(fcam, fpoint, findex, fseen, fz, fodd, fheld, stage, total)
    pair_solve((ssent0, ssent1), (smet0, smet1), sinverse, sz)
    pair_return(scam, spoint, sindex, sseen, sz, sodd, sheld, stage, total)
    fold(total, result)
    step = result[...] + extra[...]
    result[...] = step
    squares[...] = jnp.zeros_like(squares)
    sends = (fsend0, fsend1)
    pair_look(
        fcam, fpoint, findex, result, fseen2, floose, sends, fodd, False, squares, fheld, None
    )
    sides = (sown, sguest)
    pair_look(scam, spoint, sindex, result, sseen2, sloose, sides, 0, False, squares, sheld, None)
    base = table[...]
    dots[...] = jnp.zeros_like(dots)
    for row, value in enumerate((base * base, base * step, step * step, squares[...])):
        dots[row : row + 1, :] = jnp.sum(value, axis=0, keepdims=True)


def dots_kernel(
    dots, product, fsent0, fsent1, fmet0, fmet1, finverse, sown, smet, sinverse,
    fz, sz, out, products,
):
    (fodd, _), (sodd, _) = place_of()
    products[...] = jnp.zeros_like(products)
    both_solve((fsent0, fsent1), (fmet0, fmet1), finverse, fz, products, fodd)
    own_solve(sown, smet, sinverse, sz, products, sodd)
    curve = dots[3:4, :] + product[0:1, :] - jnp.sum(products[...], axis=0, keepdims=True)
    rows = jnp.concatenate([dots[0:3, :], curve], axis=0)
    sums = jnp.sum(rows, axis=1, keepdims=True)
    place = lax.broadcasted_iota(jnp.int32, (1, LANES), 1)
    line = jnp.zeros((1, LANES), F32)
    for n in range(4):
        line = line + jnp.where(place == n, sums[n : n + 1, :], 0.0)
    out[...] = jnp.broadcast_to(line, out.shape)


def last_kernel(
    extra, fcam, fpoint, fcams, scam, spoint, scams, fseen, fz, sseen, svalues,
    result, findex, sindex, sz, stage, total,
):
    (fodd, fheld), (_, sheld) = place_of()
    weave(fcams, findex)
    weave(scams, sindex)
    total[...] = jnp.zeros_like(total)
    pair_return(fcam, fpoint, findex, fseen, fz, fodd, fheld, stage, total)
    widened(svalues, sz, 0)
    pair_return(scam, spoint, sindex, sseen, sz, 0, sheld, stage, total, (0,))
    fold(total, result)
    result[...] += extra[...]


def guest_kernel(extra, scam, spoint, scams, sseen, svalues, result, sindex, sz, stage, total):
    _, (_, sheld) = place_of()
    weave(scams, sindex)
    total[...] = jnp.zeros_like(total)
    widened(svalues, sz, 1)
    pair_return(scam, spoint, sindex, sseen, sz, 0, sheld, stage, total, (1,))
    fold(total, result)
    result[...] += extra[...]


def close_kernel(sums, lines, first, second, step_out, residual_out, base):
    in_rows(lines, base)
    line = jnp.sum(sums[...], axis=0, keepdims=True)
    place = lax.broadcasted_iota(jnp.int32, line.shape, 1)
    rr, bp, pp, curve = [
        jnp.sum(jnp.where(place == n, line, 0.0), axis=1, keepdims=True) for n in range(4)
    ]
    whole = rr + bp
    alpha = rr / whole
    rest = bp / whole
    new = alpha * (alpha * pp - rest * bp)
    gamma = rest + new / rr
    bend = gamma * gamma * rr - 2.0 * gamma * alpha * bp + alpha * alpha * pp
    bend = bend + gamma * gamma * bp - 2.0 * gamma * alpha * pp + alpha * alpha * curve
    again = new / bend
    d0, p, t = base[...], first[...], second[...]
    direction = gamma * d0 - alpha * p
    image = gamma * d0 + (gamma - alpha) * p - alpha * t
    step = -(alpha * d0 + again * direction)
    residual = -(rest * d0 - alpha * p - again * image)
    for j in range(JAC):
        for k in range(PAGES):
            row = PAGES * j + k
            step_out[j, :, pl.ds(LANES * k, LANES)] = step[row : row + 1, :]
            residual_out[j, :, pl.ds(LANES * k, LANES)] = residual[row : row + 1, :]


def call(kernel, ins, outs, scratch, flops, name, place=VMEM, to=VMEM, room=12):
    outs = [jax.ShapeDtypeStruct(shape, F32) for shape in outs]
    specs = [place] * len(ins)
    return pl.pallas_call(
        kernel,
        out_shape=outs,
        in_specs=specs,
        out_specs=[to] * len(outs),
        scratch_shapes=scratch,
        compiler_params=pltpu.CompilerParams(vmem_limit_bytes=room << 20),
        cost_estimate=pl.CostEstimate(flops=flops, bytes_accessed=2 << 20, transcendentals=0),
        name=name,
    )(*ins)


def rows_of(array):
    kinds, parts, two, _, points = array.shape
    array = array.reshape(kinds, parts, two, points // LANES, LANES)
    return array.transpose(0, 1, 3, 2, 4).reshape(kinds, parts, two * points // LANES, LANES)


def per_device(
    gradient, live_blocks, loc_cam_jac, loc_point_jac, loc_cams,
    fwd_cam_jac, fwd_point_jac, fwd_cams, side_cam_jac, side_point_jac, side_cams,
):
    strips, segs = lax.axis_size("strip"), lax.axis_size("seg")
    cells = [(s, g) for s in range(strips) for g in range(segs)]

    def pairs(move):
        found = []
        for s, g in cells:
            t, h = move(s, g)
            if 0 <= t < strips and 0 <= h < segs:
                found.append((s * segs + g, t * segs + h))
        return found

    fwd_rounds = pairs(lambda s, g: (s, (g + 1 ^ 1) - 1)), pairs(lambda s, g: (s, g ^ 1))
    side_down = pairs(lambda s, g: (s - 1, segs - 1 - g))
    side_up = pairs(lambda s, g: (s + 1, segs - 1 - g))
    side_rounds = (
        pairs(lambda s, g: ((s + 1 ^ 1) - 1, segs - 1 - g)),
        pairs(lambda s, g: (s ^ 1, segs - 1 - g)),
    )
    lcam, lpoint = loc_cam_jac[:, :, 0], loc_point_jac[:, :, 0]
    lcams = loc_cams.reshape(-1, LANES)
    fcam, fpoint = rows_of(fwd_cam_jac), rows_of(fwd_point_jac)
    scam, spoint = rows_of(side_cam_jac), rows_of(side_point_jac)
    fcams = fwd_cams.reshape(2, 2, -1, LANES)
    scams = side_cams.reshape(2, 2, -1, LANES)
    fr, sr = fcam.shape[2], scam.shape[2]
    watched = lcam.shape[1]

    def meet(sends, rounds):
        return [lax.ppermute(send, AXES, pairs) for send, pairs in zip(sends, rounds)]

    index_scratch = [pltpu.VMEM((2, fr, LANES), jnp.int32), pltpu.VMEM((2, sr, LANES), jnp.int32)]
    z_scratch = [pltpu.VMEM((2, 3, fr, LANES), F32), pltpu.VMEM((2, 3, sr, LANES), F32)]
    total_scratch = scatter_scratch(STEP)

    def sends_of(parts):
        return [(parts, fr // 2, LANES)] * 2, [(parts, sr // 2, LANES)] * 2

    far = [gradient, scam, spoint, scams]
    table = [pltpu.VMEM((ROWS, LANES), F32)]
    fshapes, sshapes = sends_of(9)
    shapes = [(2, 2, sr, LANES)] + sshapes
    sseen, *ssent = call(
        side_look_kernel,
        far,
        shapes,
        [pltpu.VMEM(x.shape, x.dtype) for x in far]
        + [pltpu.VMEM(shape, F32) for shape in shapes]
        + table
        + index_scratch[1:]
        + [pltpu.VMEM((9, sr, LANES), F32), pltpu.VMEM((2, JAC, sr, LANES), F32)]
        + [pltpu.SemaphoreType.DMA((len(far),)), pltpu.SemaphoreType.DMA((len(shapes),))],
        10**9,
        "look",
        FAR,
        FAR,
        63,
    )
    fseen, *fsent = call(
        forward_look_kernel,
        [gradient, fcam, fpoint, fcams],
        [(2, 2, fr, LANES)] + fshapes,
        table + index_scratch[:1] + [pltpu.VMEM((9, fr, LANES), F32)],
        10**9,
        "forward_look",
    )
    smet = meet(ssent, side_rounds)
    fmet = meet(fsent, fwd_rounds)

    def local(values):
        return call(
            local_kernel,
            [live_blocks, values, lcam, lpoint, lcams],
            [(ROWS, LANES), (8, LANES)],
            scatter_scratch(watched * LOCAL_GROUP) + table,
            5 * 10**9,
            "local",
        )

    extra, _ = local(gradient)
    fshapes, sshapes = sends_of(3)
    p, finverse, sinverse, fseen, fsend0, fsend1, sseen, sown, sguest, dots = call(
        middle_kernel,
        [gradient, extra, fcam, fpoint, fcams, scam, spoint, scams,
         fseen, *fsent, *fmet, sseen, *ssent, *smet],
        [(ROWS, LANES), (2, 6, fr // 2, LANES), (2, 6, sr // 2, LANES), (2, 2, fr, LANES)]
        + fshapes + [(2, 2, sr, LANES)] + sshapes + [(8, LANES)],
        table + index_scratch
        + [pltpu.VMEM((3, fr, LANES), F32), pltpu.VMEM((3, sr, LANES), F32)]
        + z_scratch + total_scratch + [pltpu.VMEM((STEP, LANES), F32)],
        10**10,
        "middle",
    )
    smet = lax.ppermute(sguest, AXES, side_down)
    fmet = meet((fsend0, fsend1), fwd_rounds)
    extra, product = local(p)
    fz, sz, line = call(
        dots_kernel,
        [dots, product, fsend0, fsend1, *fmet, finverse, sown, smet, sinverse],
        [(2, 3, fr, LANES), (3, sr // 2, LANES), (strips * segs, LANES)],
        [pltpu.VMEM((8, LANES), F32)],
        10**8,
        "dots",
    )
    line = lax.all_to_all(line, AXES, 0, 0, tiled=True)
    ssent = lax.ppermute(sz, AXES, side_up)
    (t,) = call(
        last_kernel,
        [extra, fcam, fpoint, fcams, scam, spoint, scams, fseen, fz, sseen, sz],
        [(ROWS, LANES)],
        index_scratch + z_scratch[1:] + total_scratch,
        5 * 10**9,
        "last",
    )
    (t,) = call(
        guest_kernel,
        [t, scam, spoint, scams, sseen, ssent],
        [(ROWS, LANES)],
        index_scratch[1:] + z_scratch[1:] + total_scratch,
        2 * 10**9,
        "guest",
    )
    step, residual = call(
        close_kernel, [line, gradient, p, t], [gradient.shape] * 2, table, 10**6, "close"
    )
    return step, residual


def solution(mesh):
    placed = (
        P(None, "strip", "seg"),
        P("strip", "seg"),
        P(None, None, "strip", "seg"),
        P(None, None, "strip", "seg"),
        P(None, "strip", "seg"),
        P(None, None, None, "strip", "seg"),
        P(None, None, None, "strip", "seg"),
        P(None, None, "strip", "seg"),
        P(None, None, None, "strip", "seg"),
        P(None, None, None, "strip", "seg"),
        P(None, None, "strip", "seg"),
    )
    return jax.shard_map(
        per_device,
        mesh=mesh,
        in_specs=placed,
        out_specs=(P(None, "strip", "seg"), P(None, "strip", "seg")),
        check_vma=False,
    )
```

```python
import jax
import jax.numpy as jnp
from jax import lax
from jax.experimental import pallas as pl
from jax.experimental.pallas import tpu as pltpu
from jax.sharding import PartitionSpec as P

AXES = ("strip", "seg")
LANES = 128
JAC = 9
PAGES = 4
ROWS = JAC * PAGES
STACK = 80
STEP = 16
LOCAL_GROUP = 16
SYM = ((0, 0), (0, 1), (0, 2), (1, 1), (1, 2), (2, 2))
DAMP = 1.0
VMEM = pl.BlockSpec(memory_space=pltpu.VMEM)
FAR = pl.BlockSpec(memory_space=pltpu.HBM)
F32 = jnp.float32


def fetch(table, index):
    lane = index & (LANES - 1)
    odd = (index & LANES) != 0
    upper = index >= 2 * LANES
    found = []
    for j in range(JAC):
        page = [
            jnp.take_along_axis(
                jnp.broadcast_to(table[pl.ds(PAGES * j + k, 1), :], index.shape), lane, axis=1
            )
            for k in range(PAGES)
        ]
        low = jnp.where(odd, page[1], page[0])
        high = jnp.where(odd, page[3], page[2])
        found.append(jnp.where(upper, high, low))
    return found


def predict(across, values):
    return [sum(across[JAC * r + j] * values[j] for j in range(JAC)) for r in range(2)]


def project(along, seen):
    return [along[k] * seen[0] + along[3 + k] * seen[1] for k in range(3)]


def normal(along):
    return [along[i] * along[j] + along[3 + i] * along[3 + j] for i, j in SYM]


def invert(h):
    a, b, c, d, e, f = h[0] + DAMP, h[1], h[2], h[3] + DAMP, h[4], h[5] + DAMP
    first = d * f - e * e
    second = c * e - b * f
    third = b * e - c * d
    scale = 1.0 / (a * first + b * second + c * third)
    return [
        m * scale for m in (first, second, third, a * f - c * c, b * c - a * e, a * d - b * b)
    ]


def solve(m, b):
    return [
        m[0] * b[0] + m[1] * b[1] + m[2] * b[2],
        m[1] * b[0] + m[3] * b[1] + m[4] * b[2],
        m[2] * b[0] + m[4] * b[1] + m[5] * b[2],
    ]


def residue(along, seen, z):
    return [seen[r] - sum(along[3 * r + k] * z[k] for k in range(3)) for r in range(2)]


def spread(terms, index, stage, total):
    add_in([stacked(terms, index, stage)], total)


def add_in(parts, total):
    total[...] += lax.dot_general(
        jnp.concatenate([x for left, _ in parts for x in left], axis=1),
        jnp.concatenate([x for _, right in parts for x in right], axis=1),
        (((1,), (1,)), ((), ())),
        preferred_element_type=F32,
    )


def stacked(terms, index, stage):
    count = index.shape[0]
    page = index >> 7
    coarse = terms[JAC - 1].astype(jnp.bfloat16).astype(F32)
    fine = terms[JAC - 1] - coarse
    for j in range(JAC - 1):
        stage[pl.ds(j, count, stride=16), :] = terms[j]
    for h in range(PAGES):
        stage[pl.ds(8 + h, count, stride=16), :] = jnp.where(page == h, coarse, 0.0)
        stage[pl.ds(12 + h, count, stride=16), :] = jnp.where(page == h, fine, 0.0)
    page = page.astype(F32)
    lane = (index & (LANES - 1)).astype(F32)
    place = lax.broadcasted_iota(jnp.int32, (LANES, LANES), 0).astype(F32).astype(jnp.bfloat16)
    one, none = jnp.ones((), jnp.bfloat16), jnp.zeros((), jnp.bfloat16)
    left, right = [], []
    for row in range(count):
        raw = stage[pl.ds(16 * row, 8), :]
        rest = stage[pl.ds(16 * row + 8, 8), :]
        coarse = raw.astype(jnp.bfloat16).astype(F32)
        both = jnp.concatenate([coarse, raw - coarse], axis=0).astype(jnp.bfloat16)
        wide = jnp.broadcast_to(page[row : row + 1], (16, LANES)).astype(jnp.bfloat16)
        tiles = [jnp.where(wide == h, both, none) for h in range(PAGES)]
        tiles.append(jnp.concatenate([rest, jnp.zeros_like(rest)], axis=0).astype(jnp.bfloat16))
        left.append(jnp.concatenate(tiles, axis=0))
        wide = jnp.broadcast_to(lane[row : row + 1], (16, LANES)).astype(jnp.bfloat16)
        wide = jnp.concatenate([wide] * (LANES // 16), axis=0)
        right.append(jnp.where(wide == place, one, none))
    return left, right


def scatter_scratch(count):
    return [pltpu.VMEM((16 * count, LANES), F32), pltpu.VMEM((STACK, LANES), F32)]


def fold(total, out):
    for h in range(PAGES):
        out[pl.ds(h, JAC - 1, stride=PAGES), :] = (
            total[pl.ds(16 * h, 8), :] + total[pl.ds(16 * h + 8, 8), :]
        )
    out[pl.ds(ROWS - PAGES, PAGES), :] = total[64:68, :] + total[68:72, :]


def weave(cams, index):
    half = cams.shape[2]
    for s in range(2):
        for o in range(2):
            index[s, pl.ds(o, half, stride=2), :] = cams[s, o]


def pair_look(
    cam, point, index, table, seen_out, loose, sends, odd, with_h, squares, held, done,
    kept=None, ready=None,
):
    rows = cam.shape[2]
    half = rows // 2
    if kept is not None:
        for s in range(2):
            for i in range(rows // STEP):
                at = pl.ds(i * STEP, STEP)
                for j, found in enumerate(fetch(table, index[s, at, :])):
                    kept[s, j, at, :] = found
        ready()
    for turn in range(2):
        s = turn ^ odd
        share = part_of(s, held)

        def body(i, carry, s=s, turn=turn, share=share):
            at = pl.ds(pl.multiple_of(i * STEP, STEP), STEP)
            across = [cam[s, j, at, :].astype(F32) for j in range(2 * JAC)]
            along = [point[s, j, at, :].astype(F32) for j in range(6)]
            if kept is None:
                values = fetch(table, index[s, at, :])
            else:
                values = [kept[s, j, at, :] for j in range(JAC)]
            seen = predict(across, values)
            for r in range(2):
                seen_out[turn, r, at, :] = seen[r]
            parts = project(along, seen)
            if with_h:
                parts = parts + normal(along)
            for n, part in enumerate(parts):
                loose[n, at, :] = part
            if squares is not None:
                squares[...] += share * (seen[0] * seen[0] + seen[1] * seen[1])
            return carry

        lax.fori_loop(0, rows // STEP, body, 0, unroll=True)
        for n in range(9 if with_h else 3):
            sends[turn][n] = (
                loose[n, pl.ds(0, half, stride=2), :] + loose[n, pl.ds(1, half, stride=2), :]
            )
        if done is not None:
            done(turn)


def part_of(side, held):
    if isinstance(side, int):
        return 1.0 if side == 0 else held.astype(F32)
    return jnp.where(side == 0, 1, held).astype(F32)


def pair_return(cam, point, index, seen_in, z, odd, held, stage, total, turns=(0, 1)):
    rows = cam.shape[2]
    for turn in turns:
        s = turn ^ odd
        share = part_of(s, held)

        def body(i, carry, s=s, turn=turn, share=share):
            at = pl.ds(pl.multiple_of(i * STEP, STEP), STEP)
            across = [cam[s, j, at, :].astype(F32) for j in range(2 * JAC)]
            along = [point[s, j, at, :].astype(F32) for j in range(6)]
            left = residue(
                along,
                [seen_in[turn, r, at, :] for r in range(2)],
                [z[turn, k, at, :] for k in range(3)],
            )
            left = [share * e for e in left]
            terms = [across[j] * left[0] + across[JAC + j] * left[1] for j in range(JAC)]
            spread(terms, index[s, at, :], stage, total)
            return carry

        lax.fori_loop(0, rows // STEP, body, 0, unroll=True)


def pair_solve(sent, met, inverse_out, z):
    half = sent[0].shape[1]
    for turn in range(2):
        for i in range(half // 8):
            at = pl.ds(8 * i, 8)
            joined = [sent[turn][k, at, :] + met[turn][k, at, :] for k in range(9)]
            inverse = invert(joined[3:])
            for k in range(6):
                inverse_out[turn, k, at, :] = inverse[k]
            put_z(z, turn, i, solve(inverse, joined[:3]))


def put_z(z, turn, i, solved):
    for k in range(3):
        for o in range(2):
            z[turn, k, pl.ds(16 * i + o, 8, stride=2), :] = solved[k]


def own_solve(own, met, inverse, z, products, odd):
    for i in range(own.shape[1] // 8):
        at = pl.ds(8 * i, 8)
        b = [own[k, at, :] + met[k, at, :] for k in range(3)]
        solved = solve([inverse[odd, k, at, :] for k in range(6)], b)
        products[...] += sum(b[k] * solved[k] for k in range(3))
        for k in range(3):
            z[k, at, :] = solved[k]


def both_solve(sent, met, inverse, z, products, odd):
    for turn in range(2):
        own = part_of(turn ^ odd, jnp.int32(0))
        for i in range(sent[0].shape[1] // 8):
            at = pl.ds(8 * i, 8)
            b = [sent[turn][k, at, :] + met[turn][k, at, :] for k in range(3)]
            solved = solve([inverse[turn, k, at, :] for k in range(6)], b)
            products[...] += own * sum(b[k] * solved[k] for k in range(3))
            put_z(z, turn, i, solved)


def widened(values, z, turn):
    for i in range(values.shape[1] // 8):
        put_z(z, turn, i, [values[k, pl.ds(8 * i, 8), :] for k in range(3)])


def place_of():
    seg, strip = lax.axis_index("seg"), lax.axis_index("strip")
    return (1 - (seg & 1), jnp.minimum(seg, 1)), (1 - (strip & 1), jnp.minimum(strip, 1))


def in_rows(lines, table):
    for j in range(JAC):
        for k in range(PAGES):
            table[pl.ds(PAGES * j + k, 1), :] = lines[j, :, pl.ds(LANES * k, LANES)]


def side_look_kernel(
    gradient, scam_at, spoint_at, scams_at, sseen_at, ssend0_at, ssend1_at,
    lines, scam, spoint, scams, sseen, ssend0, ssend1, table, sindex, sloose, kept,
    arrived, left,
):
    _, (sodd, _) = place_of()
    moves = [
        pltpu.make_async_copy(source, target, arrived.at[n])
        for n, (source, target) in enumerate(
            ((gradient, lines), (scams_at, scams), (scam_at, scam), (spoint_at, spoint))
        )
    ]
    back = [
        pltpu.make_async_copy(source, target, left.at[n])
        for n, (source, target) in enumerate(
            ((ssend0, ssend0_at), (ssend1, ssend1_at), (sseen, sseen_at))
        )
    ]
    for move in moves:
        move.start()
    for move in moves[:2]:
        move.wait()
    in_rows(lines, table)
    weave(scams, sindex)

    def ready():
        for move in moves[2:]:
            move.wait()

    def done(turn):
        back[turn].start()
        if turn == 1:
            back[2].start()

    pair_look(
        scam, spoint, sindex, table, sseen, sloose, (ssend0, ssend1), sodd, True, None, 0, done,
        kept, ready,
    )
    for move in back:
        move.wait()


def forward_look_kernel(
    lines, fcam, fpoint, fcams, fseen, fsend0, fsend1, table, findex, floose
):
    (fodd, _), _ = place_of()
    in_rows(lines, table)
    weave(fcams, findex)
    pair_look(
        fcam, fpoint, findex, table, fseen, floose, (fsend0, fsend1), fodd, True, None, 0, None
    )


def local_kernel(live, values, cam, point, cams, out, product, stage, total, table):
    total[...] = jnp.zeros_like(total)
    product[...] = jnp.zeros_like(product)
    if values.shape[0] == JAC:
        in_rows(values, table)
    else:
        table = values
    watched, blocks = cams.shape[0] // 16, cam.shape[2] // LANES
    lives = jnp.broadcast_to(live[...], (1, LANES))

    def block(i, stage):
        at = pl.ds(pl.multiple_of(i * LANES, LANES), LANES)
        index = cams[pl.ds(i, watched, stride=16), :]
        across = [cam[j, :, at].astype(F32) for j in range(2 * JAC)]
        along = [point[j, :, at].astype(F32) for j in range(6)]
        seen = predict(across, fetch(table, index))
        summed = [jnp.sum(x, axis=0, keepdims=True) for x in project(along, seen) + normal(along)]
        z = solve(invert(summed[3:]), summed[:3])
        share = jnp.where(lives > i, 1.0, 0.0)
        left = [share * e for e in residue(along, seen, z)]
        terms = [across[j] * left[0] + across[JAC + j] * left[1] for j in range(JAC)]
        seen = jnp.sum(seen[0] * left[0] + seen[1] * left[1], axis=0, keepdims=True)
        return seen, stacked(terms, index, stage)

    def body(i, carry):
        done = [
            block(LOCAL_GROUP * i + n, stage.at[pl.ds(16 * watched * n, 16 * watched)])
            for n in range(LOCAL_GROUP)
        ]
        product[0:1, :] += sum(seen for seen, _ in done)
        add_in([parts for _, parts in done], total)
        return carry

    lax.fori_loop(0, blocks // LOCAL_GROUP, body, 0)
    fold(total, out)


def middle_kernel(
    lines, extra, fcam, fpoint, fcams, scam, spoint, scams,
    fseen, fsent0, fsent1, fmet0, fmet1, sseen, ssent0, ssent1, smet0, smet1,
    result, finverse, sinverse, fseen2, fsend0, fsend1, sseen2, sown, sguest, dots,
    table, findex, sindex, floose, sloose, fz, sz, stage, total, squares,
):
    (fodd, fheld), (sodd, sheld) = place_of()
    in_rows(lines, table)
    weave(fcams, findex)
    weave(scams, sindex)
    total[...] = jnp.zeros_like(total)
    pair_solve((fsent0, fsent1), (fmet0, fmet1), finverse, fz)
    pair_return(fcam, fpoint, findex, fseen, fz, fodd, fheld, stage, total)
    pair_solve((ssent0, ssent1), (smet0, smet1), sinverse, sz)
    pair_return(scam, spoint, sindex, sseen, sz, sodd, sheld, stage, total)
    fold(total, result)
    step = result[...] + extra[...]
    result[...] = step
    squares[...] = jnp.zeros_like(squares)
    sends = (fsend0, fsend1)
    pair_look(
        fcam, fpoint, findex, result, fseen2, floose, sends, fodd, False, squares, fheld, None
    )
    sides = (sown, sguest)
    pair_look(scam, spoint, sindex, result, sseen2, sloose, sides, 0, False, squares, sheld, None)
    base = table[...]
    dots[...] = jnp.zeros_like(dots)
    for row, value in enumerate((base * base, base * step, step * step, squares[...])):
        dots[row : row + 1, :] = jnp.sum(value, axis=0, keepdims=True)


def dots_kernel(
    dots, product, fsent0, fsent1, fmet0, fmet1, finverse, sown, smet, sinverse,
    fz, sz, out, products,
):
    (fodd, _), (sodd, _) = place_of()
    products[...] = jnp.zeros_like(products)
    both_solve((fsent0, fsent1), (fmet0, fmet1), finverse, fz, products, fodd)
    own_solve(sown, smet, sinverse, sz, products, sodd)
    curve = dots[3:4, :] + product[0:1, :] - jnp.sum(products[...], axis=0, keepdims=True)
    rows = jnp.concatenate([dots[0:3, :], curve], axis=0)
    sums = jnp.sum(rows, axis=1, keepdims=True)
    place = lax.broadcasted_iota(jnp.int32, (1, LANES), 1)
    line = jnp.zeros((1, LANES), F32)
    for n in range(4):
        line = line + jnp.where(place == n, sums[n : n + 1, :], 0.0)
    out[...] = jnp.broadcast_to(line, out.shape)


def last_kernel(
    extra, fcam, fpoint, fcams, scam, spoint, scams, fseen, fz, sseen, svalues,
    result, findex, sindex, sz, stage, total,
):
    (fodd, fheld), (_, sheld) = place_of()
    weave(fcams, findex)
    weave(scams, sindex)
    total[...] = jnp.zeros_like(total)
    pair_return(fcam, fpoint, findex, fseen, fz, fodd, fheld, stage, total)
    widened(svalues, sz, 0)
    pair_return(scam, spoint, sindex, sseen, sz, 0, sheld, stage, total, (0,))
    fold(total, result)
    result[...] += extra[...]


def guest_kernel(extra, scam, spoint, scams, sseen, svalues, result, sindex, sz, stage, total):
    _, (_, sheld) = place_of()
    weave(scams, sindex)
    total[...] = jnp.zeros_like(total)
    widened(svalues, sz, 1)
    pair_return(scam, spoint, sindex, sseen, sz, 0, sheld, stage, total, (1,))
    fold(total, result)
    result[...] += extra[...]


def close_kernel(sums, lines, first, second, step_out, residual_out, base):
    in_rows(lines, base)
    line = jnp.sum(sums[...], axis=0, keepdims=True)
    place = lax.broadcasted_iota(jnp.int32, line.shape, 1)
    rr, bp, pp, curve = [
        jnp.sum(jnp.where(place == n, line, 0.0), axis=1, keepdims=True) for n in range(4)
    ]
    whole = rr + bp
    alpha = rr / whole
    rest = bp / whole
    new = alpha * (alpha * pp - rest * bp)
    gamma = rest + new / rr
    bend = gamma * gamma * rr - 2.0 * gamma * alpha * bp + alpha * alpha * pp
    bend = bend + gamma * gamma * bp - 2.0 * gamma * alpha * pp + alpha * alpha * curve
    again = new / bend
    d0, p, t = base[...], first[...], second[...]
    direction = gamma * d0 - alpha * p
    image = gamma * d0 + (gamma - alpha) * p - alpha * t
    step = -(alpha * d0 + again * direction)
    residual = -(rest * d0 - alpha * p - again * image)
    for j in range(JAC):
        for k in range(PAGES):
            row = PAGES * j + k
            step_out[j, :, pl.ds(LANES * k, LANES)] = step[row : row + 1, :]
            residual_out[j, :, pl.ds(LANES * k, LANES)] = residual[row : row + 1, :]


def call(kernel, ins, outs, scratch, flops, name, place=VMEM, to=VMEM, room=12):
    outs = [jax.ShapeDtypeStruct(shape, F32) for shape in outs]
    specs = [place] * len(ins)
    return pl.pallas_call(
        kernel,
        out_shape=outs,
        in_specs=specs,
        out_specs=[to] * len(outs),
        scratch_shapes=scratch,
        compiler_params=pltpu.CompilerParams(vmem_limit_bytes=room << 20),
        cost_estimate=pl.CostEstimate(flops=flops, bytes_accessed=2 << 20, transcendentals=0),
        name=name,
    )(*ins)


def rows_of(array):
    kinds, parts, two, _, points = array.shape
    array = array.reshape(kinds, parts, two, points // LANES, LANES)
    return array.transpose(0, 1, 3, 2, 4).reshape(kinds, parts, two * points // LANES, LANES)


def per_device(
    gradient, live_blocks, loc_cam_jac, loc_point_jac, loc_cams,
    fwd_cam_jac, fwd_point_jac, fwd_cams, side_cam_jac, side_point_jac, side_cams,
):
    strips, segs = lax.axis_size("strip"), lax.axis_size("seg")
    cells = [(s, g) for s in range(strips) for g in range(segs)]

    def pairs(move):
        found = []
        for s, g in cells:
            t, h = move(s, g)
            if 0 <= t < strips and 0 <= h < segs:
                found.append((s * segs + g, t * segs + h))
        return found

    fwd_rounds = pairs(lambda s, g: (s, (g + 1 ^ 1) - 1)), pairs(lambda s, g: (s, g ^ 1))
    side_down = pairs(lambda s, g: (s - 1, segs - 1 - g))
    side_up = pairs(lambda s, g: (s + 1, segs - 1 - g))
    side_rounds = (
        pairs(lambda s, g: ((s + 1 ^ 1) - 1, segs - 1 - g)),
        pairs(lambda s, g: (s ^ 1, segs - 1 - g)),
    )
    lcam, lpoint = loc_cam_jac[:, :, 0], loc_point_jac[:, :, 0]
    lcams = loc_cams.reshape(-1, LANES)
    fcam, fpoint = rows_of(fwd_cam_jac), rows_of(fwd_point_jac)
    scam, spoint = rows_of(side_cam_jac), rows_of(side_point_jac)
    fcams = fwd_cams.reshape(2, 2, -1, LANES)
    scams = side_cams.reshape(2, 2, -1, LANES)
    fr, sr = fcam.shape[2], scam.shape[2]
    watched = lcam.shape[1]

    def meet(sends, rounds):
        return [lax.ppermute(send, AXES, pairs) for send, pairs in zip(sends, rounds)]

    index_scratch = [pltpu.VMEM((2, fr, LANES), jnp.int32), pltpu.VMEM((2, sr, LANES), jnp.int32)]
    z_scratch = [pltpu.VMEM((2, 3, fr, LANES), F32), pltpu.VMEM((2, 3, sr, LANES), F32)]
    total_scratch = scatter_scratch(STEP)

    def sends_of(parts):
        return [(parts, fr // 2, LANES)] * 2, [(parts, sr // 2, LANES)] * 2

    far = [gradient, scam, spoint, scams]
    table = [pltpu.VMEM((ROWS, LANES), F32)]
    fshapes, sshapes = sends_of(9)
    shapes = [(2, 2, sr, LANES)] + sshapes
    sseen, *ssent = call(
        side_look_kernel,
        far,
        shapes,
        [pltpu.VMEM(x.shape, x.dtype) for x in far]
        + [pltpu.VMEM(shape, F32) for shape in shapes]
        + table
        + index_scratch[1:]
        + [pltpu.VMEM((9, sr, LANES), F32), pltpu.VMEM((2, JAC, sr, LANES), F32)]
        + [pltpu.SemaphoreType.DMA((len(far),)), pltpu.SemaphoreType.DMA((len(shapes),))],
        10**9,
        "look",
        FAR,
        FAR,
        63,
    )
    fseen, *fsent = call(
        forward_look_kernel,
        [gradient, fcam, fpoint, fcams],
        [(2, 2, fr, LANES)] + fshapes,
        table + index_scratch[:1] + [pltpu.VMEM((9, fr, LANES), F32)],
        10**9,
        "forward_look",
    )
    smet = meet(ssent, side_rounds)
    fmet = meet(fsent, fwd_rounds)

    def local(values):
        return call(
            local_kernel,
            [live_blocks, values, lcam, lpoint, lcams],
            [(ROWS, LANES), (8, LANES)],
            scatter_scratch(watched * LOCAL_GROUP) + table,
            5 * 10**9,
            "local",
        )

    extra, _ = local(gradient)
    fshapes, sshapes = sends_of(3)
    p, finverse, sinverse, fseen, fsend0, fsend1, sseen, sown, sguest, dots = call(
        middle_kernel,
        [gradient, extra, fcam, fpoint, fcams, scam, spoint, scams,
         fseen, *fsent, *fmet, sseen, *ssent, *smet],
        [(ROWS, LANES), (2, 6, fr // 2, LANES), (2, 6, sr // 2, LANES), (2, 2, fr, LANES)]
        + fshapes + [(2, 2, sr, LANES)] + sshapes + [(8, LANES)],
        table + index_scratch
        + [pltpu.VMEM((3, fr, LANES), F32), pltpu.VMEM((3, sr, LANES), F32)]
        + z_scratch + total_scratch + [pltpu.VMEM((STEP, LANES), F32)],
        10**10,
        "middle",
    )
    smet = lax.ppermute(sguest, AXES, side_down)
    fmet = meet((fsend0, fsend1), fwd_rounds)
    extra, product = local(p)
    fz, sz, line = call(
        dots_kernel,
        [dots, product, fsend0, fsend1, *fmet, finverse, sown, smet, sinverse],
        [(2, 3, fr, LANES), (3, sr // 2, LANES), (strips * segs, LANES)],
        [pltpu.VMEM((8, LANES), F32)],
        10**8,
        "dots",
    )
    line = lax.all_to_all(line, AXES, 0, 0, tiled=True)
    ssent = lax.ppermute(sz, AXES, side_up)
    (t,) = call(
        last_kernel,
        [extra, fcam, fpoint, fcams, scam, spoint, scams, fseen, fz, sseen, sz],
        [(ROWS, LANES)],
        index_scratch + z_scratch[1:] + total_scratch,
        5 * 10**9,
        "last",
    )
    (t,) = call(
        guest_kernel,
        [t, scam, spoint, scams, sseen, ssent],
        [(ROWS, LANES)],
        index_scratch[1:] + z_scratch[1:] + total_scratch,
        2 * 10**9,
        "guest",
    )
    step, residual = call(
        close_kernel, [line, gradient, p, t], [gradient.shape] * 2, table, 10**6, "close"
    )
    return step, residual


def solution(mesh):
    placed = (
        P(None, "strip", "seg"),
        P("strip", "seg"),
        P(None, None, "strip", "seg"),
        P(None, None, "strip", "seg"),
        P(None, "strip", "seg"),
        P(None, None, None, "strip", "seg"),
        P(None, None, None, "strip", "seg"),
        P(None, None, "strip", "seg"),
        P(None, None, None, "strip", "seg"),
        P(None, None, None, "strip", "seg"),
        P(None, None, "strip", "seg"),
    )
    return jax.shard_map(
        per_device,
        mesh=mesh,
        in_specs=placed,
        out_specs=(P(None, "strip", "seg"), P(None, "strip", "seg")),
        check_vma=False,
    )
```
